32 devices in a mesh: seq: 8 (over y, x, core), dp: 4 (over z).
Axes of the slice: x: 2, y: 2, z: 4, core: 2. Of those that a mesh axis runs over, the one named last changes fastest.
Arguments:
- attn_queries: bfloat16 [4, 8, 8, 2048], P('dp', 'seq'), may hold values from -190 to 190
- attn_keys: bfloat16 [4, 8, 8, 2048], P('dp', 'seq'), may hold values from -7 to 7
- attn_values: bfloat16 [4, 8, 8, 2048], P('dp', 'seq'), may hold values from -6 to 6
- out_grad: bfloat16 [4, 8, 8, 2048], P('dp', 'seq'), may hold values from -0.359375 to 0.359375
- fold_maps: bfloat16 [3, 6, 2048], replicated, may hold values from -0.078125 to 0.078125
- dec_grad: float32 [4, 6, 8, 8], P('dp', None, 'seq'), may hold values from -0.36 to 0.36
- conv_input: bfloat16 [4, 8, 8, 256], P('dp', 'seq'), may hold values from -6 to 6
- pre_act: bfloat16 [4, 8, 8, 256], P('dp', 'seq'), may hold values from -6 to 6
- proj_weight: bfloat16 [6, 256], replicated, may hold values from -0.375 to 0.375
Outputs:
- conv_grad: float32 [256, 9, 256], P('seq')
- proj_grad: float32 [256, 6], P('seq')
The draws below stay inside these ranges and needn't reach their ends.
All inputs are finite; a program needn't handle non-finite values.
Results may differ from the reference program's by a relative error of at most 0.0046.
Values may be sent and summed in bfloat16 or wider, within the bound.
No kernel may reach another device: no remote copies, remote signals or barrier semaphores. Data moves between devices by JAX's collectives and lax.ppermute only.
A program may use at most 64 MiB of HBM per device.

```python
import math
import jax
import jax.numpy as jnp
from jax import lax

HEAD_DIM = 128
CH = 256
LATENT = 6
HALF = 8
WIDTH = 2048
IMAGES = 4
GRID_H = 8
GRID_W = 8


def drawn_fields(key):
    base = jax.random.fold_in(key, 4242)
    key_draw, query_draw = jax.random.split(base, 2)
    full_shape = (IMAGES, GRID_H, GRID_W, WIDTH)
    keys_drawn = jnp.clip(jax.random.normal(key_draw, full_shape, jnp.float32), -6.0, 6.0)
    queries_drawn = jnp.clip(jax.random.normal(query_draw, full_shape, jnp.float32), -6.0, 6.0)
    return (queries_drawn, keys_drawn)


def draw_attn_queries(key, part):
    return drawn_fields(key)[0].astype(jnp.bfloat16)


def draw_attn_keys(key, part):
    return drawn_fields(key)[1].astype(jnp.bfloat16)


def strengthened(drawn, own_key, source, target, parts, factor):
    owner, partner = [(jnp.arange(drawn.shape[dim]) // (drawn.shape[dim] // parts)).reshape([-1 if axis == dim else 1 for axis in range(drawn.ndim)]) for dim in (source, target)]
    chosen = jax.random.permutation(own_key, parts)[partner]
    strong = (owner == chosen) | (owner == (partner + parts // 2) % parts)
    return jnp.where(strong, factor * drawn, drawn)


def steps_of(own_key, shape, cuts, least, high):
    level = 1.0
    for dim, blocks in cuts:
        steps = jax.random.uniform(jax.random.fold_in(jax.random.fold_in(own_key, 6), dim), (blocks,), jnp.float32, least / len(cuts), high / len(cuts))
        level = level * jnp.repeat(jnp.exp(steps), shape[dim] // blocks).reshape((-1,) + (1,) * (len(shape) - 1 - dim))
    return level


def bell_draw(own_key, dims, deviation, reach, shards=(), dtype=jnp.bfloat16):
    result = deviation * jax.random.normal(own_key, dims, jnp.float32)
    if shards:
        result = result * steps_of(own_key, dims, shards, -0.22, 0.18)
    return jnp.clip(result, -reach, reach).astype(dtype)


def noise_with(rng, shape, deviation, limit, shards, heavy, held_as=jnp.bfloat16):
    entries = deviation * jax.random.normal(rng, shape, jnp.float32)
    if shards:
        entries = entries * steps_of(rng, shape, shards, -0.22, 0.18)
    return jnp.clip(strengthened(entries, jax.random.fold_in(rng, 3), *heavy), -limit, limit).astype(held_as)


def setup_inputs(seed: int = 0) -> dict:
    seeds = jax.random.split(jax.random.key(seed), 10)
    return {
        "attn_queries": draw_attn_queries(jax.random.fold_in(seeds[9], 71), 0),
        "attn_keys": draw_attn_keys(jax.random.fold_in(seeds[9], 71), 0),
        "attn_values": bell_draw(seeds[2], (IMAGES, GRID_H, GRID_W, WIDTH), 1.0, 6.0, ((0, 4), (1, 8))),
        "out_grad": bell_draw(seeds[3], (IMAGES, GRID_H, GRID_W, WIDTH), 0.06, 0.359375, ((0, 4), (1, 8))),
        "fold_maps": bell_draw(seeds[4], (3, LATENT, WIDTH), (3 * WIDTH) ** -0.5, 0.078125),
        "dec_grad": bell_draw(seeds[5], (IMAGES, LATENT, GRID_H, GRID_W), 0.06, 0.36, ((0, 4), (2, 8)), jnp.float32),
        "conv_input": noise_with(seeds[6], (IMAGES, GRID_H, GRID_W, CH), 1.0, 6.0, ((0, 4), (1, 8)), (1, 3, 8, 2.0)),
        "pre_act": noise_with(seeds[7], (IMAGES, GRID_H, GRID_W, CH), 1.0, 6.0, ((0, 4), (1, 8)), (1, 3, 8, 2.0)),
        "proj_weight": bell_draw(seeds[8], (LATENT, CH), CH ** -0.5, 0.375),
    }


fsq_levels = (8.0, 8.0, 8.0, 5.0, 5.0, 5.0)
fsq_bins = (4.0, 4.0, 4.0, 2.0, 2.0, 2.0)

def bound_tables():
    halves = [(levels_one - 1.0) * 1.001 / 2.0 for levels_one in fsq_levels]
    shifts = []
    for levels_one, half_width in zip(fsq_levels, halves):
        offset_one = 0.5 if levels_one % 2.0 == 0.0 else 0.0
        ratio_one = offset_one / half_width
        shifts.append(0.5 * math.log((1.0 + ratio_one) / (1.0 - ratio_one)))
    return (jnp.array(halves, jnp.float32), jnp.array(shifts, jnp.float32), jnp.array(fsq_bins, jnp.float32))

def attend_back(queries, keys_in, values_in, grads_in):
    scaling = 1.0 / math.sqrt(queries.shape[-1])
    length = queries.shape[1]
    query_wide = queries.astype(jnp.float32)
    key_wide = keys_in.astype(jnp.float32)
    value_wide = values_in.astype(jnp.float32)
    grad_wide = grads_in.astype(jnp.float32)
    scores = jnp.einsum('blhd,bmhd->bhlm', query_wide, key_wide) * scaling
    causal = jnp.arange(length)[:, None] >= jnp.arange(length)[None, :]
    scores = jnp.where(causal, scores, -jnp.inf)
    exp_scores = jnp.exp(scores - lax.optimization_barrier(jnp.max(scores, axis=-1, keepdims=True)))
    attn_probs = exp_scores / lax.optimization_barrier(jnp.sum(exp_scores, axis=-1, keepdims=True))
    probs_low = lax.optimization_barrier(attn_probs.astype(jnp.bfloat16)).astype(jnp.float32)
    dprobs = jnp.einsum('blhd,bmhd->bhlm', grad_wide, value_wide)
    rowdot = lax.optimization_barrier(jnp.sum(attn_probs * dprobs, axis=-1, keepdims=True))
    dscore = lax.optimization_barrier((attn_probs * (dprobs - rowdot) * scaling).astype(jnp.bfloat16)).astype(jnp.float32)
    grad_query = jnp.einsum('bhlm,bmhd->blhd', dscore, key_wide).astype(jnp.bfloat16)
    grad_key = jnp.einsum('bhlm,blhd->bmhd', dscore, query_wide).astype(jnp.bfloat16)
    grad_value = jnp.einsum('bhlm,blhd->bmhd', probs_low, grad_wide).astype(jnp.bfloat16)
    return (grad_query, grad_key, grad_value)

def reference(attn_queries, attn_keys, attn_values, out_grad, fold_maps, dec_grad, conv_input, pre_act, proj_weight):
    fold_wide = fold_maps.astype(jnp.float32)
    proj_wide = proj_weight.astype(jnp.float32)
    halves, shifts, bins_arr = bound_tables()

    def one_image(packed):
        queries, keys_in, values_in, grads_in, decoder, inputs, preact = packed
        split_at = HALF * HEAD_DIM
        grid_rows = queries.shape[0]
        grid_cols = queries.shape[1]

        def row_heads(array_in):
            return array_in[:, :, :split_at].reshape(grid_rows, grid_cols, HALF, HEAD_DIM)

        def col_heads(array_in):
            return jnp.swapaxes(array_in[:, :, split_at:], 0, 1).reshape(grid_cols, grid_rows, HALF, HEAD_DIM)
        row_grads = attend_back(row_heads(queries), row_heads(keys_in), row_heads(values_in), row_heads(grads_in))
        col_grads = attend_back(col_heads(queries), col_heads(keys_in), col_heads(values_in), col_heads(grads_in))
        latent = jnp.zeros((LATENT, grid_rows, grid_cols), jnp.float32)
        for position in range(3):
            row_part = row_grads[position].reshape(grid_rows, grid_cols, split_at)
            col_part = jnp.swapaxes(col_grads[position].reshape(grid_cols, grid_rows, split_at), 0, 1)
            full_grad = jnp.concatenate([row_part, col_part], axis=-1).astype(jnp.float32)
            latent = latent + jnp.einsum('cw,yxw->cyx', fold_wide[position], full_grad)
        pre_wide = preact.astype(jnp.float32)
        sigmoid_v = jax.nn.sigmoid(pre_wide)
        act_low = lax.optimization_barrier((pre_wide * sigmoid_v).astype(jnp.bfloat16)).astype(jnp.float32)
        latent_pre = jnp.einsum('yxj,cj->cyx', act_low, proj_wide)
        tanh_val = jnp.tanh(latent_pre + shifts[:, None, None])
        slope_fsq = (halves / bins_arr)[:, None, None] * (1.0 - tanh_val * tanh_val)
        latent_grad = lax.optimization_barrier(((latent + decoder) * slope_fsq).astype(jnp.bfloat16)).astype(jnp.float32)
        proj_term = jnp.einsum('cyx,yxj->jc', latent_grad, act_low)
        act_grad = jnp.einsum('cyx,cj->yxj', latent_grad, proj_wide)
        pre_grad = lax.optimization_barrier((act_grad * sigmoid_v * (1.0 + pre_wide * (1.0 - sigmoid_v))).astype(jnp.bfloat16)).astype(jnp.float32)
        padded = jnp.pad(inputs.astype(jnp.float32), ((1, 1), (1, 1), (0, 0)))
        taps = []
        for row_off in range(3):
            for col_off in range(3):
                window = padded[row_off:row_off + grid_rows, col_off:col_off + grid_cols]
                taps.append(jnp.einsum('yxa,yxb->ab', window, pre_grad))
        conv_term = jnp.stack(taps, axis=1)
        return (conv_term, proj_term)
    conv_terms, proj_terms = lax.map(one_image, (attn_queries, attn_keys, attn_values, out_grad, dec_grad, conv_input, pre_act))
    return (lax.optimization_barrier(jnp.sum(conv_terms, axis=0)), lax.optimization_barrier(jnp.sum(proj_terms, axis=0)))
```

```python
import functools
import math

import jax
import jax.numpy as jnp
from jax import lax
from jax.experimental import pallas as pl
from jax.experimental.pallas import tpu as pltpu
from jax.sharding import PartitionSpec as P

HEAD_DIM = 128
HALF = 8


fsq_levels = (8.0, 8.0, 8.0, 5.0, 5.0, 5.0)
fsq_bins = (4.0, 4.0, 4.0, 2.0, 2.0, 2.0)


def padded_2(block, sides, width):
    for axis, dim in sides:
        count = lax.axis_size(axis)
        forward = [(i, i + 1) for i in range(count - 1)]
        backward = [(target, source) for source, target in forward]
        low = lax.ppermute(
            lax.slice_in_dim(block, block.shape[dim] - width, None, axis=dim), axis, forward
        )
        high = lax.ppermute(lax.slice_in_dim(block, 0, width, axis=dim), axis, backward)
        block = jnp.concatenate([low, block, high], axis=dim)
    return block


def bound_tables():
    halves = [(levels_one - 1.0) * 1.001 / 2.0 for levels_one in fsq_levels]
    shifts = []
    for levels_one, half_width in zip(fsq_levels, halves):
        offset_one = 0.5 if levels_one % 2.0 == 0.0 else 0.0
        ratio_one = offset_one / half_width
        shifts.append(0.5 * math.log((1.0 + ratio_one) / (1.0 - ratio_one)))
    return (
        jnp.array(halves, jnp.float32),
        jnp.array(shifts, jnp.float32),
        jnp.array(fsq_bins, jnp.float32),
    )


def attend_back(queries, keys_in, values_in, grads_in):
    scaling = 1.0 / math.sqrt(queries.shape[-1])
    length = queries.shape[1]
    scores = (
        jnp.einsum("blhd,bmhd->bhlm", queries, keys_in, preferred_element_type=jnp.float32)
        * scaling
    )
    causal = jnp.arange(length)[:, None] >= jnp.arange(length)[None, :]
    scores = jnp.where(causal, scores, -jnp.inf)
    exp_scores = jnp.exp(scores - jnp.max(scores, axis=-1, keepdims=True))
    attn_probs = exp_scores / jnp.sum(exp_scores, axis=-1, keepdims=True)
    probs_low = attn_probs.astype(jnp.bfloat16)
    dprobs = jnp.einsum("blhd,bmhd->bhlm", grads_in, values_in, preferred_element_type=jnp.float32)
    rowdot = jnp.sum(attn_probs * dprobs, axis=-1, keepdims=True)
    dscore = (attn_probs * (dprobs - rowdot) * scaling).astype(jnp.bfloat16)
    grad_query = jnp.einsum(
        "bhlm,bmhd->blhd", dscore, keys_in, preferred_element_type=jnp.float32
    ).astype(jnp.bfloat16)
    grad_key = jnp.einsum(
        "bhlm,blhd->bmhd", dscore, queries, preferred_element_type=jnp.float32
    ).astype(jnp.bfloat16)
    grad_value = jnp.einsum(
        "bhlm,blhd->bmhd", probs_low, grads_in, preferred_element_type=jnp.float32
    ).astype(jnp.bfloat16)
    return (grad_query, grad_key, grad_value)


def fold_sum(grads, maps):
    total = jnp.einsum("cw,iyxw->icyx", maps[0], grads[0], preferred_element_type=jnp.float32)
    total = total + jnp.einsum(
        "cw,iyxw->icyx", maps[1], grads[1], preferred_element_type=jnp.float32
    )
    return total + jnp.einsum(
        "cw,iyxw->icyx", maps[2], grads[2], preferred_element_type=jnp.float32
    )


def reduce_plan(
    attn_queries,
    attn_keys,
    attn_values,
    out_grad,
    fold_maps,
    dec_grad,
    conv_input,
    pre_act,
    proj_weight,
):
    split_at = HALF * HEAD_DIM
    width_cols = attn_queries.shape[2]
    rim_rows = padded_2(conv_input, (("seq", 1),), 1)
    column_parts = (
        lax.all_to_all(
            attn_queries[..., split_at:], "seq", split_axis=2, concat_axis=1, tiled=True
        ),
        lax.all_to_all(attn_keys[..., split_at:], "seq", split_axis=2, concat_axis=1, tiled=True),
        lax.all_to_all(attn_values[..., split_at:], "seq", split_axis=2, concat_axis=1, tiled=True),
        lax.all_to_all(out_grad[..., split_at:], "seq", split_axis=2, concat_axis=1, tiled=True),
    )

    def row_heads(array_in):
        return array_in[0, :, :, :split_at].reshape(array_in.shape[1], width_cols, HALF, HEAD_DIM)

    row_grads = attend_back(
        row_heads(attn_queries), row_heads(attn_keys), row_heads(attn_values), row_heads(out_grad)
    )
    row_grads = [grad_one.reshape(1, 1, width_cols, split_at) for grad_one in row_grads]
    grid_rows = column_parts[0].shape[1]
    col_count = column_parts[0].shape[2]

    def col_heads(array_in):
        return jnp.transpose(array_in[0], (1, 0, 2)).reshape(col_count, grid_rows, HALF, HEAD_DIM)

    col_grads = attend_back(
        col_heads(column_parts[0]),
        col_heads(column_parts[1]),
        col_heads(column_parts[2]),
        col_heads(column_parts[3]),
    )
    col_grads = [
        jnp.transpose(grad_one.reshape(col_count, grid_rows, split_at), (1, 0, 2))[None]
        for grad_one in col_grads
    ]
    latent_col = fold_sum(col_grads, fold_maps[:, :, split_at:])
    latent_rows = lax.all_to_all(latent_col, "seq", split_axis=2, concat_axis=3, tiled=True)
    latent = fold_sum(row_grads, fold_maps[:, :, :split_at]) + latent_rows
    halves, shifts, bins_arr = bound_tables()
    pre_wide = pre_act.astype(jnp.float32)
    sigmoid_v = jax.nn.sigmoid(pre_wide)
    act_low = (pre_wide * sigmoid_v).astype(jnp.bfloat16)
    latent_pre = jnp.einsum(
        "iyxj,cj->icyx", act_low, proj_weight, preferred_element_type=jnp.float32
    )
    tanh_val = jnp.tanh(latent_pre + shifts[None, :, None, None])
    slope_fsq = (halves / bins_arr)[None, :, None, None] * (1.0 - tanh_val * tanh_val)
    latent_grad = ((latent + dec_grad) * slope_fsq).astype(jnp.bfloat16)
    proj_term = jnp.einsum(
        "icyx,iyxj->jc", latent_grad, act_low, preferred_element_type=jnp.float32
    )
    act_grad = jnp.einsum(
        "icyx,cj->iyxj", latent_grad, proj_weight, preferred_element_type=jnp.float32
    )
    pre_grad = (act_grad * sigmoid_v * (1.0 + pre_wide * (1.0 - sigmoid_v))).astype(jnp.bfloat16)
    padded = jnp.pad(rim_rows, ((0, 0), (0, 0), (1, 1), (0, 0)))
    windows = jnp.stack(
        [
            padded[0, row_off, col_off : col_off + width_cols]
            for row_off in range(3)
            for col_off in range(3)
        ]
    )
    conv_term = jnp.einsum(
        "kpa,pb->akb", windows, pre_grad[0, 0], preferred_element_type=jnp.float32
    )
    shares = (
        lax.psum_scatter(conv_term, "seq", scatter_dimension=0, tiled=True),
        lax.psum_scatter(proj_term, "seq", scatter_dimension=0, tiled=True),
    )
    conv_out, proj_out = lax.psum((shares[0], shares[1]), "dp")
    return (conv_out, proj_out)


LANES = 128
FLOAT = jnp.float32
HALFWORD = jnp.bfloat16


def dot(lhs, rhs, lhs_dim=1, rhs_dim=0, precision=None):
    return lax.dot_general(
        lhs,
        rhs,
        (((lhs_dim,), (rhs_dim,)), ((), ())),
        precision=precision,
        preferred_element_type=FLOAT,
    )


def iota(shape, axis):
    return lax.broadcasted_iota(jnp.int32, shape, axis)


def attend_tile(queries, keys_in, values_in, grads_in, allowed):
    scaling = 1.0 / math.sqrt(queries.shape[-1])
    scores = jnp.where(allowed, dot(queries, keys_in, 1, 1) * scaling, -jnp.inf)
    exp_scores = jnp.exp(scores - jnp.max(scores, axis=-1, keepdims=True))
    attn_probs = exp_scores / jnp.sum(exp_scores, axis=-1, keepdims=True)
    dprobs = dot(grads_in, values_in, 1, 1)
    rowdot = jnp.sum(attn_probs * dprobs, axis=-1, keepdims=True)
    dscore = (attn_probs * (dprobs - rowdot) * scaling).astype(HALFWORD)
    return (
        dot(dscore, keys_in).astype(HALFWORD),
        dot(dscore, queries, 0, 0).astype(HALFWORD),
        dot(attn_probs.astype(HALFWORD), grads_in, 0, 0).astype(HALFWORD),
    )


def lane_places(rows, lanes, start, latents, width):
    lane = iota((rows, lanes), 1)
    inside = lane >= start
    offset = lax.rem(jnp.maximum(lane - start, 0), latents * width)
    return inside, lax.div(offset, width), lax.rem(offset, width)


def pack_kernel(query_ref, key_ref, value_ref, grad_ref, out_ref):
    heads = out_ref.shape[0]
    for part, ref in enumerate((query_ref, key_ref, value_ref, grad_ref)):
        for head in range(heads):
            out_ref[head, part] = ref[0, 0, :, head * HEAD_DIM : (head + 1) * HEAD_DIM]


def local_kernel(
    query_ref,
    key_ref,
    value_ref,
    grad_ref,
    fold_ref,
    dec_ref,
    conv_ref,
    proj_ref,
    row_ref,
    fold_own_ref,
    conv_out_ref,
    proj_rep_ref,
):
    width = query_ref.shape[2]
    latents = fold_ref.shape[1]
    devices, _, lanes = conv_out_ref.shape
    span = conv_ref.shape[3] // devices
    mine = lax.axis_index("seq")

    def stacked(ref):
        return jnp.concatenate(
            [
                ref[0, 0, :, head * HEAD_DIM : (head + 1) * HEAD_DIM].astype(FLOAT)
                for head in range(HALF)
            ],
            axis=0,
        ).astype(HALFWORD)

    count = HALF * width
    row, col = iota((count, count), 0), iota((count, count), 1)
    allowed = (lax.div(row, width) == lax.div(col, width)) & (col <= row)
    grads = attend_tile(
        stacked(query_ref), stacked(key_ref), stacked(value_ref), stacked(grad_ref), allowed
    )
    inside, channel, place = lane_places(width, lanes, span, latents, width)
    lane = iota((lanes, latents), 0)
    spread_at = lax.rem(jnp.maximum(lane - span, 0), latents * width)
    hit = (lane >= span) & (lax.div(spread_at, width) == iota((lanes, latents), 1))
    spread = jnp.where(hit, 1.0, 0.0).astype(HALFWORD)
    once = jnp.where(hit & (lane < span + latents * width), 1.0, 0.0).astype(HALFWORD)
    split_at = HALF * HEAD_DIM
    total = jnp.zeros((width, lanes), FLOAT)
    for part in range(3):
        maps = dot(spread, fold_ref[part, :, :split_at]).astype(HALFWORD)
        wide = grads[part].astype(FLOAT)
        wide = jnp.concatenate(
            [wide[head * width : (head + 1) * width] for head in range(HALF)], axis=1
        ).astype(HALFWORD)
        total = total + dot(wide, maps, 1, 1)
        own = fold_ref[part, :, pl.ds(pl.multiple_of(split_at + mine * HEAD_DIM, HEAD_DIM), HEAD_DIM)]
        fold_own_ref[part] = dot(spread, own).astype(HALFWORD)
    total = jnp.where(inside & (iota((width, lanes), 0) == place), total, 0.0)
    decoder = dec_ref[0, :, 0, :]
    column = jnp.where(
        iota((width, lanes), 0) == lax.rem(iota((width, lanes), 1), width), 1.0, 0.0
    )
    decoder = dot(decoder, column, precision=lax.Precision.HIGHEST)
    _, channel, _ = lane_places(latents, lanes, span, latents, width)
    keep = (iota((latents, lanes), 1) >= span) & (iota((latents, lanes), 0) == channel)
    vector = jnp.sum(total, axis=0, keepdims=True) + jnp.sum(
        jnp.where(keep, decoder, 0.0), axis=0, keepdims=True
    )
    row_ref[...] = jnp.where(iota((width, lanes), 0) == mine, vector, 0.0)
    proj_rep_ref[...] = dot(once, proj_ref[...]).astype(HALFWORD)
    for device in range(devices):
        first = device * span
        block = conv_ref[0, 0, :, first // lanes * lanes : first // lanes * lanes + lanes].astype(FLOAT)
        if first % lanes:
            block = pltpu.roll(block, lanes - first % lanes, 1)
        conv_out_ref[device] = block


def column_kernel(recv_ref, fold_ref, row_ref, conv_ref, pre_ref, out_ref):
    rows, _, width, _ = recv_ref.shape
    devices, _, lanes = conv_ref.shape
    channels = pre_ref.shape[3]
    images = out_ref.shape[0] // devices
    span = channels // devices
    half = (lanes - span) // 2
    count = rows * width

    def stacked(part):
        return recv_ref[:, part].astype(FLOAT).reshape(count, HEAD_DIM).astype(HALFWORD)

    row, col = iota((count, count), 0), iota((count, count), 1)
    allowed = (lax.rem(row, width) == lax.rem(col, width)) & (col <= row)
    grads = attend_tile(stacked(0), stacked(1), stacked(2), stacked(3), allowed)
    total = dot(grads[0], fold_ref[0], 1, 1)
    total = total + dot(grads[1], fold_ref[1], 1, 1)
    total = total + dot(grads[2], fold_ref[2], 1, 1)
    match = lax.rem(iota((count, lanes), 0), width) == lax.rem(iota((count, lanes), 1), width)
    total = jnp.where(match, total, 0.0).reshape(rows, width, lanes)
    share = jnp.sum(total, axis=1) + row_ref[...]
    high = share.astype(HALFWORD).astype(FLOAT)
    lane = iota((rows, lanes), 1)
    pair = jnp.where(lane < span + half, high, share - high)
    pre = pre_ref[0, 0]
    for device in range(devices):
        block = jnp.where(lane < span, conv_ref[device], pair).astype(HALFWORD)
        for image in range(images):
            out_ref[image * devices + device, :, :channels] = pre
            out_ref[image * devices + device, :, channels:] = block


def final_kernel(recv_ref, proj_rep_ref, conv_out_ref, proj_out_ref):
    sources, width, _ = recv_ref.shape
    taps, span, channels = conv_out_ref.shape
    latents = proj_out_ref.shape[0]
    lanes = proj_rep_ref.shape[0]
    devices = channels // span
    images = sources // devices
    count = sources * width
    mine = lax.axis_index("seq")
    half = latents * width

    pre_wide = recv_ref[:, :, :channels].astype(FLOAT).reshape(count, channels)
    tail = recv_ref[:, :, channels:].astype(FLOAT)
    proj_rep = proj_rep_ref[...]
    sigmoid_v = jax.nn.sigmoid(pre_wide)
    act_low = (pre_wide * sigmoid_v).astype(HALFWORD)
    lane = iota((count, lanes), 1)
    match = (
        (lane >= span)
        & (lane < span + half)
        & (lax.rem(iota((count, lanes), 0), width) == lax.rem(lane, width))
    )
    latent_pre = jnp.where(match, dot(act_low, proj_rep, 1, 1), 0.0)
    latent_pre = jnp.sum(latent_pre.reshape(sources, width, lanes), axis=1)
    shares = tail.reshape(images, devices, width, lanes)
    latent = jnp.sum(shares, axis=1).reshape(sources, lanes)
    latent = latent + pltpu.roll(latent, lanes - half, 1)
    halves = [(levels_one - 1.0) * 1.001 / 2.0 for levels_one in fsq_levels]
    _, channel, _ = lane_places(sources, lanes, span, latents, width)
    shift = jnp.zeros((sources, lanes), FLOAT)
    slope = jnp.zeros((sources, lanes), FLOAT)
    for index, (levels_one, bins_one, half_width) in enumerate(zip(fsq_levels, fsq_bins, halves)):
        ratio_one = (0.5 if levels_one % 2.0 == 0.0 else 0.0) / half_width
        shift_one = 0.5 * math.log((1.0 + ratio_one) / (1.0 - ratio_one))
        shift = jnp.where(channel == index, shift_one, shift)
        slope = jnp.where(channel == index, half_width / bins_one, slope)
    tanh_val = jnp.tanh(latent_pre + shift)
    latent_grad = latent * (slope * (1.0 - tanh_val * tanh_val))
    wide = jnp.broadcast_to(latent_grad.reshape(sources, 1, lanes), (sources, width, lanes))
    wide = jnp.where(match, wide.reshape(count, lanes), 0.0).astype(HALFWORD)
    act_grad = dot(wide, proj_rep)
    pre_grad = (act_grad * sigmoid_v * (1.0 + pre_wide * (1.0 - sigmoid_v))).astype(HALFWORD)

    pick = jnp.where(iota((span, lanes), 0) == iota((span, lanes), 1), 1.0, 0.0).astype(HALFWORD)
    inputs = dot(pick, tail.reshape(count, lanes).astype(HALFWORD), 1, 1)
    position = iota((span, count), 1)
    place_x = lax.rem(position, width)
    place_y = lax.rem(lax.div(position, width), devices)
    windows = []
    for row_off in (-1, 0, 1):
        for col_off in (-1, 0, 1):
            step = row_off * width + col_off
            window = pltpu.roll(inputs, -step % count, 1) if step else inputs
            valid = (
                (place_x + col_off >= 0)
                & (place_x + col_off < width)
                & (place_y + row_off >= 0)
                & (place_y + row_off < devices)
            )
            windows.append(jnp.where(valid, window, 0.0))
    windows = jnp.concatenate(windows, axis=0).astype(HALFWORD)
    conv_out_ref[...] = dot(windows, pre_grad).reshape(taps, span, channels)
    proj_term = dot(wide, act_low, 0, 0)[span : span + half]
    proj_term = jnp.sum(proj_term.reshape(latents, width, channels), axis=1)
    proj_out_ref[...] = pltpu.roll(proj_term, lax.rem(channels - mine * span, channels), 1)[:, :span]


def call(kernel, outs, inputs, in_specs=None, flops=1 << 22):
    whole = pl.BlockSpec(memory_space=pltpu.VMEM)
    nbytes = sum(math.prod(one.shape) * one.dtype.itemsize for one in (*inputs, *outs))
    return pl.pallas_call(
        kernel,
        grid=(1,),
        out_shape=outs,
        in_specs=in_specs or [whole] * len(inputs),
        out_specs=[whole] * len(outs),
        compiler_params=pltpu.CompilerParams(vmem_limit_bytes=16 << 20),
        cost_estimate=pl.CostEstimate(flops=flops, bytes_accessed=nbytes, transcendentals=0),
    )(*inputs)


def gather_plan(
    attn_queries,
    attn_keys,
    attn_values,
    out_grad,
    fold_maps,
    dec_grad,
    conv_input,
    pre_act,
    proj_weight,
):
    devices, images = lax.axis_size("seq"), lax.axis_size("dp")
    width, channels, latents = pre_act.shape[2], pre_act.shape[3], proj_weight.shape[0]
    span = channels // devices
    split_at = HALF * HEAD_DIM
    heads = (attn_queries, attn_keys, attn_values, out_grad)
    struct = jax.ShapeDtypeStruct
    columns = [pl.BlockSpec((1, 1, width, split_at), lambda step: (0, 0, 0, 1))] * 4
    rows = [pl.BlockSpec((1, 1, width, split_at), lambda step: (0, 0, 0, 0))] * 4
    whole = pl.BlockSpec(memory_space=pltpu.VMEM)
    (packed,) = call(
        pack_kernel, [struct((devices, 4, width, HEAD_DIM), HALFWORD)], heads, columns
    )
    column = lax.all_to_all(packed, "seq", split_axis=0, concat_axis=0, tiled=True)
    row_share, fold_own, conv_blocks, proj_rep = call(
        local_kernel,
        [
            struct((width, LANES), FLOAT),
            struct((3, LANES, HEAD_DIM), HALFWORD),
            struct((devices, width, LANES), FLOAT),
            struct((LANES, channels), HALFWORD),
        ],
        (*heads, fold_maps, dec_grad, conv_input, proj_weight),
        rows + [whole] * 4,
    )
    (shared,) = call(
        column_kernel,
        [struct((images * devices, width, channels + LANES), HALFWORD)],
        (column, fold_own, row_share, conv_blocks, pre_act),
    )
    spread = lax.all_to_all(shared, ("dp", "seq"), split_axis=0, concat_axis=0, tiled=True)
    conv_out, proj_out = call(
        final_kernel,
        [struct((9, span, channels), FLOAT), struct((latents, span), FLOAT)],
        (spread, proj_rep),
    )
    return (jnp.transpose(conv_out, (1, 0, 2)), jnp.transpose(proj_out, (1, 0)))


def on_device(*arrays):
    queries, conv_input, proj_weight = arrays[0], arrays[6], arrays[8]
    devices, images = lax.axis_size("seq"), lax.axis_size("dp")
    rows, width, channels = conv_input.shape[1:]
    latents = proj_weight.shape[0]
    heads = queries.shape[3] // HEAD_DIM - HALF
    positions = images * devices * rows * width
    fits = (
        (conv_input.shape[0], rows, width, heads) == (1, 1, devices, devices)
        and (HALF * 2, width % 8) == (queries.shape[3] // HEAD_DIM, 0)
        and channels // devices + 2 * latents * width == LANES
    )
    if fits and positions * channels * 2 <= 9 * channels * channels * 4:
        return gather_plan(*arrays)
    return reduce_plan(*arrays)


def solution(mesh):
    return jax.shard_map(
        on_device,
        mesh=mesh,
        in_specs=(
            P("dp", "seq", None, None),
            P("dp", "seq", None, None),
            P("dp", "seq", None, None),
            P("dp", "seq", None, None),
            P(),
            P("dp", None, "seq", None),
            P("dp", "seq", None, None),
            P("dp", "seq", None, None),
            P(),
        ),
        out_specs=(P("seq", None, None), P("seq", None)),
        check_vma=False,
    )
```

```python
import functools
import math

import jax
import jax.numpy as jnp
from jax import lax
from jax.experimental import pallas as pl
from jax.experimental.pallas import tpu as pltpu
from jax.sharding import PartitionSpec as P

HEAD_DIM = 128
HALF = 8


fsq_levels = (8.0, 8.0, 8.0, 5.0, 5.0, 5.0)
fsq_bins = (4.0, 4.0, 4.0, 2.0, 2.0, 2.0)


def padded_2(block, sides, width):
    for axis, dim in sides:
        count = lax.axis_size(axis)
        forward = [(i, i + 1) for i in range(count - 1)]
        backward = [(target, source) for source, target in forward]
        low = lax.ppermute(
            lax.slice_in_dim(block, block.shape[dim] - width, None, axis=dim), axis, forward
        )
        high = lax.ppermute(lax.slice_in_dim(block, 0, width, axis=dim), axis, backward)
        block = jnp.concatenate([low, block, high], axis=dim)
    return block


def bound_tables():
    halves = [(levels_one - 1.0) * 1.001 / 2.0 for levels_one in fsq_levels]
    shifts = []
    for levels_one, half_width in zip(fsq_levels, halves):
        offset_one = 0.5 if levels_one % 2.0 == 0.0 else 0.0
        ratio_one = offset_one / half_width
        shifts.append(0.5 * math.log((1.0 + ratio_one) / (1.0 - ratio_one)))
    return (
        jnp.array(halves, jnp.float32),
        jnp.array(shifts, jnp.float32),
        jnp.array(fsq_bins, jnp.float32),
    )


def attend_back(queries, keys_in, values_in, grads_in):
    scaling = 1.0 / math.sqrt(queries.shape[-1])
    length = queries.shape[1]
    scores = (
        jnp.einsum("blhd,bmhd->bhlm", queries, keys_in, preferred_element_type=jnp.float32)
        * scaling
    )
    causal = jnp.arange(length)[:, None] >= jnp.arange(length)[None, :]
    scores = jnp.where(causal, scores, -jnp.inf)
    exp_scores = jnp.exp(scores - jnp.max(scores, axis=-1, keepdims=True))
    attn_probs = exp_scores / jnp.sum(exp_scores, axis=-1, keepdims=True)
    probs_low = attn_probs.astype(jnp.bfloat16)
    dprobs = jnp.einsum("blhd,bmhd->bhlm", grads_in, values_in, preferred_element_type=jnp.float32)
    rowdot = jnp.sum(attn_probs * dprobs, axis=-1, keepdims=True)
    dscore = (attn_probs * (dprobs - rowdot) * scaling).astype(jnp.bfloat16)
    grad_query = jnp.einsum(
        "bhlm,bmhd->blhd", dscore, keys_in, preferred_element_type=jnp.float32
    ).astype(jnp.bfloat16)
    grad_key = jnp.einsum(
        "bhlm,blhd->bmhd", dscore, queries, preferred_element_type=jnp.float32
    ).astype(jnp.bfloat16)
    grad_value = jnp.einsum(
        "bhlm,blhd->bmhd", probs_low, grads_in, preferred_element_type=jnp.float32
    ).astype(jnp.bfloat16)
    return (grad_query, grad_key, grad_value)


def fold_sum(grads, maps):
    total = jnp.einsum("cw,iyxw->icyx", maps[0], grads[0], preferred_element_type=jnp.float32)
    total = total + jnp.einsum(
        "cw,iyxw->icyx", maps[1], grads[1], preferred_element_type=jnp.float32
    )
    return total + jnp.einsum(
        "cw,iyxw->icyx", maps[2], grads[2], preferred_element_type=jnp.float32
    )


def reduce_plan(
    attn_queries,
    attn_keys,
    attn_values,
    out_grad,
    fold_maps,
    dec_grad,
    conv_input,
    pre_act,
    proj_weight,
):
    split_at = HALF * HEAD_DIM
    width_cols = attn_queries.shape[2]
    rim_rows = padded_2(conv_input, (("seq", 1),), 1)
    column_parts = (
        lax.all_to_all(
            attn_queries[..., split_at:], "seq", split_axis=2, concat_axis=1, tiled=True
        ),
        lax.all_to_all(attn_keys[..., split_at:], "seq", split_axis=2, concat_axis=1, tiled=True),
        lax.all_to_all(attn_values[..., split_at:], "seq", split_axis=2, concat_axis=1, tiled=True),
        lax.all_to_all(out_grad[..., split_at:], "seq", split_axis=2, concat_axis=1, tiled=True),
    )

    def row_heads(array_in):
        return array_in[0, :, :, :split_at].reshape(array_in.shape[1], width_cols, HALF, HEAD_DIM)

    row_grads = attend_back(
        row_heads(attn_queries), row_heads(attn_keys), row_heads(attn_values), row_heads(out_grad)
    )
    row_grads = [grad_one.reshape(1, 1, width_cols, split_at) for grad_one in row_grads]
    grid_rows = column_parts[0].shape[1]
    col_count = column_parts[0].shape[2]

    def col_heads(array_in):
        return jnp.transpose(array_in[0], (1, 0, 2)).reshape(col_count, grid_rows, HALF, HEAD_DIM)

    col_grads = attend_back(
        col_heads(column_parts[0]),
        col_heads(column_parts[1]),
        col_heads(column_parts[2]),
        col_heads(column_parts[3]),
    )
    col_grads = [
        jnp.transpose(grad_one.reshape(col_count, grid_rows, split_at), (1, 0, 2))[None]
        for grad_one in col_grads
    ]
    latent_col = fold_sum(col_grads, fold_maps[:, :, split_at:])
    latent_rows = lax.all_to_all(latent_col, "seq", split_axis=2, concat_axis=3, tiled=True)
    latent = fold_sum(row_grads, fold_maps[:, :, :split_at]) + latent_rows
    halves, shifts, bins_arr = bound_tables()
    pre_wide = pre_act.astype(jnp.float32)
    sigmoid_v = jax.nn.sigmoid(pre_wide)
    act_low = (pre_wide * sigmoid_v).astype(jnp.bfloat16)
    latent_pre = jnp.einsum(
        "iyxj,cj->icyx", act_low, proj_weight, preferred_element_type=jnp.float32
    )
    tanh_val = jnp.tanh(latent_pre + shifts[None, :, None, None])
    slope_fsq = (halves / bins_arr)[None, :, None, None] * (1.0 - tanh_val * tanh_val)
    latent_grad = ((latent + dec_grad) * slope_fsq).astype(jnp.bfloat16)
    proj_term = jnp.einsum(
        "icyx,iyxj->jc", latent_grad, act_low, preferred_element_type=jnp.float32
    )
    act_grad = jnp.einsum(
        "icyx,cj->iyxj", latent_grad, proj_weight, preferred_element_type=jnp.float32
    )
    pre_grad = (act_grad * sigmoid_v * (1.0 + pre_wide * (1.0 - sigmoid_v))).astype(jnp.bfloat16)
    padded = jnp.pad(rim_rows, ((0, 0), (0, 0), (1, 1), (0, 0)))
    windows = jnp.stack(
        [
            padded[0, row_off, col_off : col_off + width_cols]
            for row_off in range(3)
            for col_off in range(3)
        ]
    )
    conv_term = jnp.einsum(
        "kpa,pb->akb", windows, pre_grad[0, 0], preferred_element_type=jnp.float32
    )
    shares = (
        lax.psum_scatter(conv_term, "seq", scatter_dimension=0, tiled=True),
        lax.psum_scatter(proj_term, "seq", scatter_dimension=0, tiled=True),
    )
    conv_out, proj_out = lax.psum((shares[0], shares[1]), "dp")
    return (conv_out, proj_out)


LANES = 128
FLOAT = jnp.float32
HALFWORD = jnp.bfloat16


def dot(lhs, rhs, lhs_dim=1, rhs_dim=0, precision=None):
    return lax.dot_general(
        lhs,
        rhs,
        (((lhs_dim,), (rhs_dim,)), ((), ())),
        precision=precision,
        preferred_element_type=FLOAT,
    )


def iota(shape, axis):
    return lax.broadcasted_iota(jnp.int32, shape, axis)


def attend_tile(queries, keys_in, values_in, grads_in, allowed):
    scaling = 1.0 / math.sqrt(queries.shape[-1])
    scores = jnp.where(allowed, dot(queries, keys_in, 1, 1) * scaling, -jnp.inf)
    exp_scores = jnp.exp(scores - jnp.max(scores, axis=-1, keepdims=True))
    attn_probs = exp_scores / jnp.sum(exp_scores, axis=-1, keepdims=True)
    dprobs = dot(grads_in, values_in, 1, 1)
    rowdot = jnp.sum(attn_probs * dprobs, axis=-1, keepdims=True)
    dscore = (attn_probs * (dprobs - rowdot) * scaling).astype(HALFWORD)
    return (
        dot(dscore, keys_in).astype(HALFWORD),
        dot(dscore, queries, 0, 0).astype(HALFWORD),
        dot(attn_probs.astype(HALFWORD), grads_in, 0, 0).astype(HALFWORD),
    )


def lane_places(rows, lanes, start, latents, width):
    lane = iota((rows, lanes), 1)
    inside = lane >= start
    offset = lax.rem(jnp.maximum(lane - start, 0), latents * width)
    return inside, lax.div(offset, width), lax.rem(offset, width)


def pack_kernel(query_ref, key_ref, value_ref, grad_ref, out_ref, held, sem, out_sem):
    copies = []
    for step in range(out_ref.shape[0]):
        lanes = pl.ds((HALF + step) * HEAD_DIM, HEAD_DIM)
        for part, ref in enumerate((query_ref, key_ref, value_ref, grad_ref)):
            copies.append(pltpu.make_async_copy(ref.at[0, 0, :, lanes], held.at[step, part], sem))
    for copy in copies:
        copy.start()
    for copy in copies:
        copy.wait()
    last = pltpu.make_async_copy(held, out_ref, out_sem)
    last.start()
    last.wait()


def local_kernel(
    query_ref,
    key_ref,
    value_ref,
    grad_ref,
    fold_ref,
    dec_ref,
    conv_ref,
    proj_ref,
    row_ref,
    fold_own_ref,
    conv_out_ref,
    proj_rep_ref,
):
    width = query_ref.shape[2]
    latents = fold_ref.shape[1]
    devices, _, lanes = conv_out_ref.shape
    span = conv_ref.shape[3] // devices
    mine = lax.axis_index("seq")

    def stacked(ref):
        return jnp.concatenate(
            [
                ref[0, 0, :, head * HEAD_DIM : (head + 1) * HEAD_DIM].astype(FLOAT)
                for head in range(HALF)
            ],
            axis=0,
        ).astype(HALFWORD)

    count = HALF * width
    row, col = iota((count, count), 0), iota((count, count), 1)
    allowed = (lax.div(row, width) == lax.div(col, width)) & (col <= row)
    grads = attend_tile(
        stacked(query_ref), stacked(key_ref), stacked(value_ref), stacked(grad_ref), allowed
    )
    inside, channel, place = lane_places(width, lanes, span, latents, width)
    lane = iota((lanes, latents), 0)
    spread_at = lax.rem(jnp.maximum(lane - span, 0), latents * width)
    hit = (lane >= span) & (lax.div(spread_at, width) == iota((lanes, latents), 1))
    spread = jnp.where(hit, 1.0, 0.0).astype(HALFWORD)
    once = jnp.where(hit & (lane < span + latents * width), 1.0, 0.0).astype(HALFWORD)
    split_at = HALF * HEAD_DIM
    total = jnp.zeros((width, lanes), FLOAT)
    for part in range(3):
        maps = dot(spread, fold_ref[part, :, :split_at]).astype(HALFWORD)
        wide = grads[part].astype(FLOAT)
        wide = jnp.concatenate(
            [wide[head * width : (head + 1) * width] for head in range(HALF)], axis=1
        ).astype(HALFWORD)
        total = total + dot(wide, maps, 1, 1)
        own = fold_ref[part, :, pl.ds(pl.multiple_of(split_at + mine * HEAD_DIM, HEAD_DIM), HEAD_DIM)]
        fold_own_ref[part] = dot(spread, own).astype(HALFWORD)
    total = jnp.where(inside & (iota((width, lanes), 0) == place), total, 0.0)
    decoder = dec_ref[0, :, 0, :]
    column = jnp.where(
        iota((width, lanes), 0) == lax.rem(iota((width, lanes), 1), width), 1.0, 0.0
    )
    decoder = dot(decoder, column, precision=lax.Precision.HIGHEST)
    _, channel, _ = lane_places(latents, lanes, span, latents, width)
    keep = (iota((latents, lanes), 1) >= span) & (iota((latents, lanes), 0) == channel)
    vector = jnp.sum(total, axis=0, keepdims=True) + jnp.sum(
        jnp.where(keep, decoder, 0.0), axis=0, keepdims=True
    )
    row_ref[...] = jnp.where(iota((width, lanes), 0) == mine, vector, 0.0)
    proj_rep_ref[...] = dot(once, proj_ref[...]).astype(HALFWORD)
    for device in range(devices):
        first = device * span
        block = conv_ref[0, 0, :, first // lanes * lanes : first // lanes * lanes + lanes].astype(FLOAT)
        if first % lanes:
            block = pltpu.roll(block, lanes - first % lanes, 1)
        conv_out_ref[device] = block


def column_kernel(recv_ref, fold_ref, row_ref, conv_ref, pre_ref, out_ref):
    rows, _, width, _ = recv_ref.shape
    devices, _, lanes = conv_ref.shape
    channels = pre_ref.shape[3]
    images = out_ref.shape[0] // devices
    span = channels // devices
    half = (lanes - span) // 2
    count = rows * width

    def stacked(part):
        return recv_ref[:, part].astype(FLOAT).reshape(count, HEAD_DIM).astype(HALFWORD)

    row, col = iota((count, count), 0), iota((count, count), 1)
    allowed = (lax.rem(row, width) == lax.rem(col, width)) & (col <= row)
    grads = attend_tile(stacked(0), stacked(1), stacked(2), stacked(3), allowed)
    total = dot(grads[0], fold_ref[0], 1, 1)
    total = total + dot(grads[1], fold_ref[1], 1, 1)
    total = total + dot(grads[2], fold_ref[2], 1, 1)
    match = lax.rem(iota((count, lanes), 0), width) == lax.rem(iota((count, lanes), 1), width)
    total = jnp.where(match, total, 0.0).reshape(rows, width, lanes)
    share = jnp.sum(total, axis=1) + row_ref[...]
    high = share.astype(HALFWORD).astype(FLOAT)
    lane = iota((rows, lanes), 1)
    pair = jnp.where(lane < span + half, high, share - high)
    pre = pre_ref[0, 0]
    for device in range(devices):
        block = jnp.where(lane < span, conv_ref[device], pair).astype(HALFWORD)
        for image in range(images):
            out_ref[image * devices + device, :, :channels] = pre
            out_ref[image * devices + device, :, channels:] = block


def final_kernel(recv_ref, proj_rep_ref, conv_out_ref, proj_out_ref):
    sources, width, _ = recv_ref.shape
    taps, span, channels = conv_out_ref.shape
    latents = proj_out_ref.shape[0]
    lanes = proj_rep_ref.shape[0]
    devices = channels // span
    images = sources // devices
    count = sources * width
    mine = lax.axis_index("seq")
    half = latents * width

    pre_wide = recv_ref[:, :, :channels].astype(FLOAT).reshape(count, channels)
    tail = recv_ref[:, :, channels:].astype(FLOAT)
    proj_rep = proj_rep_ref[...]
    sigmoid_v = jax.nn.sigmoid(pre_wide)
    act_low = (pre_wide * sigmoid_v).astype(HALFWORD)
    lane = iota((count, lanes), 1)
    match = (
        (lane >= span)
        & (lane < span + half)
        & (lax.rem(iota((count, lanes), 0), width) == lax.rem(lane, width))
    )
    latent_pre = jnp.where(match, dot(act_low, proj_rep, 1, 1), 0.0)
    latent_pre = jnp.sum(latent_pre.reshape(sources, width, lanes), axis=1)
    shares = tail.reshape(images, devices, width, lanes)
    latent = jnp.sum(shares, axis=1).reshape(sources, lanes)
    latent = latent + pltpu.roll(latent, lanes - half, 1)
    halves = [(levels_one - 1.0) * 1.001 / 2.0 for levels_one in fsq_levels]
    _, channel, _ = lane_places(sources, lanes, span, latents, width)
    shift = jnp.zeros((sources, lanes), FLOAT)
    slope = jnp.zeros((sources, lanes), FLOAT)
    for index, (levels_one, bins_one, half_width) in enumerate(zip(fsq_levels, fsq_bins, halves)):
        ratio_one = (0.5 if levels_one % 2.0 == 0.0 else 0.0) / half_width
        shift_one = 0.5 * math.log((1.0 + ratio_one) / (1.0 - ratio_one))
        shift = jnp.where(channel == index, shift_one, shift)
        slope = jnp.where(channel == index, half_width / bins_one, slope)
    tanh_val = jnp.tanh(latent_pre + shift)
    latent_grad = latent * (slope * (1.0 - tanh_val * tanh_val))
    wide = jnp.broadcast_to(latent_grad.reshape(sources, 1, lanes), (sources, width, lanes))
    wide = jnp.where(match, wide.reshape(count, lanes), 0.0).astype(HALFWORD)
    act_grad = dot(wide, proj_rep)
    pre_grad = (act_grad * sigmoid_v * (1.0 + pre_wide * (1.0 - sigmoid_v))).astype(HALFWORD)

    pick = jnp.where(iota((span, lanes), 0) == iota((span, lanes), 1), 1.0, 0.0).astype(HALFWORD)
    inputs = dot(pick, tail.reshape(count, lanes).astype(HALFWORD), 1, 1)
    position = iota((span, count), 1)
    place_x = lax.rem(position, width)
    place_y = lax.rem(lax.div(position, width), devices)
    windows = []
    for row_off in (-1, 0, 1):
        for col_off in (-1, 0, 1):
            step = row_off * width + col_off
            window = pltpu.roll(inputs, -step % count, 1) if step else inputs
            valid = (
                (place_x + col_off >= 0)
                & (place_x + col_off < width)
                & (place_y + row_off >= 0)
                & (place_y + row_off < devices)
            )
            windows.append(jnp.where(valid, window, 0.0))
    windows = jnp.concatenate(windows, axis=0).astype(HALFWORD)
    conv_out_ref[...] = dot(windows, pre_grad).reshape(taps, span, channels)
    proj_term = dot(wide, act_low, 0, 0)[span : span + half]
    proj_term = jnp.sum(proj_term.reshape(latents, width, channels), axis=1)
    proj_out_ref[...] = pltpu.roll(proj_term, lax.rem(channels - mine * span, channels), 1)[:, :span]


def call(kernel, outs, inputs, in_specs=None, flops=1 << 22):
    whole = pl.BlockSpec(memory_space=pltpu.VMEM)
    nbytes = sum(math.prod(one.shape) * one.dtype.itemsize for one in (*inputs, *outs))
    return pl.pallas_call(
        kernel,
        grid=(1,),
        out_shape=outs,
        in_specs=in_specs or [whole] * len(inputs),
        out_specs=[whole] * len(outs),
        compiler_params=pltpu.CompilerParams(vmem_limit_bytes=16 << 20),
        cost_estimate=pl.CostEstimate(flops=flops, bytes_accessed=nbytes, transcendentals=0),
    )(*inputs)


def gather_plan(
    attn_queries,
    attn_keys,
    attn_values,
    out_grad,
    fold_maps,
    dec_grad,
    conv_input,
    pre_act,
    proj_weight,
):
    devices, images = lax.axis_size("seq"), lax.axis_size("dp")
    width, channels, latents = pre_act.shape[2], pre_act.shape[3], proj_weight.shape[0]
    span = channels // devices
    split_at = HALF * HEAD_DIM
    heads = (attn_queries, attn_keys, attn_values, out_grad)
    struct = jax.ShapeDtypeStruct
    columns = [pl.BlockSpec((1, 1, width, split_at), lambda step: (0, 0, 0, 1))] * 4
    rows = [pl.BlockSpec((1, 1, width, split_at), lambda step: (0, 0, 0, 0))] * 4
    whole = pl.BlockSpec(memory_space=pltpu.VMEM)
    packed = pl.pallas_call(
        pack_kernel,
        out_shape=struct((devices, 4, width, HEAD_DIM), HALFWORD),
        in_specs=[pl.BlockSpec(memory_space=pltpu.HBM)] * 4,
        out_specs=pl.BlockSpec(memory_space=pltpu.HBM),
        scratch_shapes=[pltpu.VMEM((devices, 4, width, HEAD_DIM), HALFWORD), pltpu.SemaphoreType.DMA, pltpu.SemaphoreType.DMA],
    )(*heads)
    column = lax.all_to_all(packed, "seq", split_axis=0, concat_axis=0, tiled=True)
    row_share, fold_own, conv_blocks, proj_rep = call(
        local_kernel,
        [
            struct((width, LANES), FLOAT),
            struct((3, LANES, HEAD_DIM), HALFWORD),
            struct((devices, width, LANES), FLOAT),
            struct((LANES, channels), HALFWORD),
        ],
        (*heads, fold_maps, dec_grad, conv_input, proj_weight),
        rows + [whole] * 4,
    )
    (shared,) = call(
        column_kernel,
        [struct((images * devices, width, channels + LANES), HALFWORD)],
        (column, fold_own, row_share, conv_blocks, pre_act),
    )
    spread = lax.all_to_all(shared, ("dp", "seq"), split_axis=0, concat_axis=0, tiled=True)
    conv_out, proj_out = call(
        final_kernel,
        [struct((9, span, channels), FLOAT), struct((latents, span), FLOAT)],
        (spread, proj_rep),
    )
    return (jnp.transpose(conv_out, (1, 0, 2)), jnp.transpose(proj_out, (1, 0)))


def on_device(*arrays):
    queries, conv_input, proj_weight = arrays[0], arrays[6], arrays[8]
    devices, images = lax.axis_size("seq"), lax.axis_size("dp")
    rows, width, channels = conv_input.shape[1:]
    latents = proj_weight.shape[0]
    heads = queries.shape[3] // HEAD_DIM - HALF
    positions = images * devices * rows * width
    fits = (
        (conv_input.shape[0], rows, width, heads) == (1, 1, devices, devices)
        and (HALF * 2, width % 8) == (queries.shape[3] // HEAD_DIM, 0)
        and channels // devices + 2 * latents * width == LANES
    )
    if fits and positions * channels * 2 <= 9 * channels * channels * 4:
        return gather_plan(*arrays)
    return reduce_plan(*arrays)


def solution(mesh):
    return jax.shard_map(
        on_device,
        mesh=mesh,
        in_specs=(
            P("dp", "seq", None, None),
            P("dp", "seq", None, None),
            P("dp", "seq", None, None),
            P("dp", "seq", None, None),
            P(),
            P("dp", None, "seq", None),
            P("dp", "seq", None, None),
            P("dp", "seq", None, None),
            P(),
        ),
        out_specs=(P("seq", None, None), P("seq", None)),
        check_vma=False,
    )
```

```python
import functools
import math

import jax
import jax.numpy as jnp
from jax import lax
from jax.experimental import pallas as pl
from jax.experimental.pallas import tpu as pltpu
from jax.sharding import PartitionSpec as P

HEAD_DIM = 128
HALF = 8


fsq_levels = (8.0, 8.0, 8.0, 5.0, 5.0, 5.0)
fsq_bins = (4.0, 4.0, 4.0, 2.0, 2.0, 2.0)


def padded_2(block, sides, width):
    for axis, dim in sides:
        count = lax.axis_size(axis)
        forward = [(i, i + 1) for i in range(count - 1)]
        backward = [(target, source) for source, target in forward]
        low = lax.ppermute(
            lax.slice_in_dim(block, block.shape[dim] - width, None, axis=dim), axis, forward
        )
        high = lax.ppermute(lax.slice_in_dim(block, 0, width, axis=dim), axis, backward)
        block = jnp.concatenate([low, block, high], axis=dim)
    return block


def bound_tables():
    halves = [(levels_one - 1.0) * 1.001 / 2.0 for levels_one in fsq_levels]
    shifts = []
    for levels_one, half_width in zip(fsq_levels, halves):
        offset_one = 0.5 if levels_one % 2.0 == 0.0 else 0.0
        ratio_one = offset_one / half_width
        shifts.append(0.5 * math.log((1.0 + ratio_one) / (1.0 - ratio_one)))
    return (
        jnp.array(halves, jnp.float32),
        jnp.array(shifts, jnp.float32),
        jnp.array(fsq_bins, jnp.float32),
    )


def attend_back(queries, keys_in, values_in, grads_in):
    scaling = 1.0 / math.sqrt(queries.shape[-1])
    length = queries.shape[1]
    scores = (
        jnp.einsum("blhd,bmhd->bhlm", queries, keys_in, preferred_element_type=jnp.float32)
        * scaling
    )
    causal = jnp.arange(length)[:, None] >= jnp.arange(length)[None, :]
    scores = jnp.where(causal, scores, -jnp.inf)
    exp_scores = jnp.exp(scores - jnp.max(scores, axis=-1, keepdims=True))
    attn_probs = exp_scores / jnp.sum(exp_scores, axis=-1, keepdims=True)
    probs_low = attn_probs.astype(jnp.bfloat16)
    dprobs = jnp.einsum("blhd,bmhd->bhlm", grads_in, values_in, preferred_element_type=jnp.float32)
    rowdot = jnp.sum(attn_probs * dprobs, axis=-1, keepdims=True)
    dscore = (attn_probs * (dprobs - rowdot) * scaling).astype(jnp.bfloat16)
    grad_query = jnp.einsum(
        "bhlm,bmhd->blhd", dscore, keys_in, preferred_element_type=jnp.float32
    ).astype(jnp.bfloat16)
    grad_key = jnp.einsum(
        "bhlm,blhd->bmhd", dscore, queries, preferred_element_type=jnp.float32
    ).astype(jnp.bfloat16)
    grad_value = jnp.einsum(
        "bhlm,blhd->bmhd", probs_low, grads_in, preferred_element_type=jnp.float32
    ).astype(jnp.bfloat16)
    return (grad_query, grad_key, grad_value)


def fold_sum(grads, maps):
    total = jnp.einsum("cw,iyxw->icyx", maps[0], grads[0], preferred_element_type=jnp.float32)
    total = total + jnp.einsum(
        "cw,iyxw->icyx", maps[1], grads[1], preferred_element_type=jnp.float32
    )
    return total + jnp.einsum(
        "cw,iyxw->icyx", maps[2], grads[2], preferred_element_type=jnp.float32
    )


def reduce_plan(
    attn_queries,
    attn_keys,
    attn_values,
    out_grad,
    fold_maps,
    dec_grad,
    conv_input,
    pre_act,
    proj_weight,
):
    split_at = HALF * HEAD_DIM
    width_cols = attn_queries.shape[2]
    rim_rows = padded_2(conv_input, (("seq", 1),), 1)
    column_parts = (
        lax.all_to_all(
            attn_queries[..., split_at:], "seq", split_axis=2, concat_axis=1, tiled=True
        ),
        lax.all_to_all(attn_keys[..., split_at:], "seq", split_axis=2, concat_axis=1, tiled=True),
        lax.all_to_all(attn_values[..., split_at:], "seq", split_axis=2, concat_axis=1, tiled=True),
        lax.all_to_all(out_grad[..., split_at:], "seq", split_axis=2, concat_axis=1, tiled=True),
    )

    def row_heads(array_in):
        return array_in[0, :, :, :split_at].reshape(array_in.shape[1], width_cols, HALF, HEAD_DIM)

    row_grads = attend_back(
        row_heads(attn_queries), row_heads(attn_keys), row_heads(attn_values), row_heads(out_grad)
    )
    row_grads = [grad_one.reshape(1, 1, width_cols, split_at) for grad_one in row_grads]
    grid_rows = column_parts[0].shape[1]
    col_count = column_parts[0].shape[2]

    def col_heads(array_in):
        return jnp.transpose(array_in[0], (1, 0, 2)).reshape(col_count, grid_rows, HALF, HEAD_DIM)

    col_grads = attend_back(
        col_heads(column_parts[0]),
        col_heads(column_parts[1]),
        col_heads(column_parts[2]),
        col_heads(column_parts[3]),
    )
    col_grads = [
        jnp.transpose(grad_one.reshape(col_count, grid_rows, split_at), (1, 0, 2))[None]
        for grad_one in col_grads
    ]
    latent_col = fold_sum(col_grads, fold_maps[:, :, split_at:])
    latent_rows = lax.all_to_all(latent_col, "seq", split_axis=2, concat_axis=3, tiled=True)
    latent = fold_sum(row_grads, fold_maps[:, :, :split_at]) + latent_rows
    halves, shifts, bins_arr = bound_tables()
    pre_wide = pre_act.astype(jnp.float32)
    sigmoid_v = jax.nn.sigmoid(pre_wide)
    act_low = (pre_wide * sigmoid_v).astype(jnp.bfloat16)
    latent_pre = jnp.einsum(
        "iyxj,cj->icyx", act_low, proj_weight, preferred_element_type=jnp.float32
    )
    tanh_val = jnp.tanh(latent_pre + shifts[None, :, None, None])
    slope_fsq = (halves / bins_arr)[None, :, None, None] * (1.0 - tanh_val * tanh_val)
    latent_grad = ((latent + dec_grad) * slope_fsq).astype(jnp.bfloat16)
    proj_term = jnp.einsum(
        "icyx,iyxj->jc", latent_grad, act_low, preferred_element_type=jnp.float32
    )
    act_grad = jnp.einsum(
        "icyx,cj->iyxj", latent_grad, proj_weight, preferred_element_type=jnp.float32
    )
    pre_grad = (act_grad * sigmoid_v * (1.0 + pre_wide * (1.0 - sigmoid_v))).astype(jnp.bfloat16)
    padded = jnp.pad(rim_rows, ((0, 0), (0, 0), (1, 1), (0, 0)))
    windows = jnp.stack(
        [
            padded[0, row_off, col_off : col_off + width_cols]
            for row_off in range(3)
            for col_off in range(3)
        ]
    )
    conv_term = jnp.einsum(
        "kpa,pb->akb", windows, pre_grad[0, 0], preferred_element_type=jnp.float32
    )
    shares = (
        lax.psum_scatter(conv_term, "seq", scatter_dimension=0, tiled=True),
        lax.psum_scatter(proj_term, "seq", scatter_dimension=0, tiled=True),
    )
    conv_out, proj_out = lax.psum((shares[0], shares[1]), "dp")
    return (conv_out, proj_out)


LANES = 128
FLOAT = jnp.float32
HALFWORD = jnp.bfloat16


def dot(lhs, rhs, lhs_dim=1, rhs_dim=0, precision=None):
    return lax.dot_general(
        lhs,
        rhs,
        (((lhs_dim,), (rhs_dim,)), ((), ())),
        precision=precision,
        preferred_element_type=FLOAT,
    )


def iota(shape, axis):
    return lax.broadcasted_iota(jnp.int32, shape, axis)


def attend_tile(queries, keys_in, values_in, grads_in, allowed):
    scaling = 1.0 / math.sqrt(queries.shape[-1])
    scores = jnp.where(allowed, dot(queries, keys_in, 1, 1) * scaling, -jnp.inf)
    exp_scores = jnp.exp(scores - jnp.max(scores, axis=-1, keepdims=True))
    attn_probs = exp_scores / jnp.sum(exp_scores, axis=-1, keepdims=True)
    dprobs = dot(grads_in, values_in, 1, 1)
    rowdot = jnp.sum(attn_probs * dprobs, axis=-1, keepdims=True)
    dscore = (attn_probs * (dprobs - rowdot) * scaling).astype(HALFWORD)
    return (
        dot(dscore, keys_in).astype(HALFWORD),
        dot(dscore, queries, 0, 0).astype(HALFWORD),
        dot(attn_probs.astype(HALFWORD), grads_in, 0, 0).astype(HALFWORD),
    )


def lane_places(rows, lanes, start, latents, width):
    lane = iota((rows, lanes), 1)
    inside = lane >= start
    offset = lax.rem(jnp.maximum(lane - start, 0), latents * width)
    return inside, lax.div(offset, width), lax.rem(offset, width)


def pack_kernel(order, query_ref, key_ref, value_ref, grad_ref, out_ref, held, sem, out_sem):
    copies = []
    for slot, device in enumerate(order):
        lanes = pl.ds((HALF + device) * HEAD_DIM, HEAD_DIM)
        for part, ref in enumerate((query_ref, key_ref, value_ref, grad_ref)):
            copies.append(pltpu.make_async_copy(ref.at[0, 0, :, lanes], held.at[slot, part], sem))
    for copy in copies:
        copy.start()
    for copy in copies:
        copy.wait()
    last = pltpu.make_async_copy(held, out_ref, out_sem)
    last.start()
    last.wait()


def local_kernel(
    query_ref,
    key_ref,
    value_ref,
    grad_ref,
    fold_ref,
    dec_ref,
    conv_ref,
    proj_ref,
    row_ref,
    fold_own_ref,
    conv_out_ref,
    proj_rep_ref,
):
    width = query_ref.shape[2]
    latents = fold_ref.shape[1]
    devices, _, lanes = conv_out_ref.shape
    span = conv_ref.shape[3] // devices
    mine = lax.axis_index("seq")

    def stacked(ref):
        return jnp.concatenate(
            [
                ref[0, 0, :, head * HEAD_DIM : (head + 1) * HEAD_DIM].astype(FLOAT)
                for head in range(HALF)
            ],
            axis=0,
        ).astype(HALFWORD)

    count = HALF * width
    row, col = iota((count, count), 0), iota((count, count), 1)
    allowed = (lax.div(row, width) == lax.div(col, width)) & (col <= row)
    grads = attend_tile(
        stacked(query_ref), stacked(key_ref), stacked(value_ref), stacked(grad_ref), allowed
    )
    inside, channel, place = lane_places(width, lanes, span, latents, width)
    lane = iota((lanes, latents), 0)
    spread_at = lax.rem(jnp.maximum(lane - span, 0), latents * width)
    hit = (lane >= span) & (lax.div(spread_at, width) == iota((lanes, latents), 1))
    spread = jnp.where(hit, 1.0, 0.0).astype(HALFWORD)
    once = jnp.where(hit & (lane < span + latents * width), 1.0, 0.0).astype(HALFWORD)
    split_at = HALF * HEAD_DIM
    total = jnp.zeros((width, lanes), FLOAT)
    for part in range(3):
        maps = dot(spread, fold_ref[part, :, :split_at]).astype(HALFWORD)
        wide = grads[part].astype(FLOAT)
        wide = jnp.concatenate(
            [wide[head * width : (head + 1) * width] for head in range(HALF)], axis=1
        ).astype(HALFWORD)
        total = total + dot(wide, maps, 1, 1)
        own = fold_ref[part, :, pl.ds(pl.multiple_of(split_at + mine * HEAD_DIM, HEAD_DIM), HEAD_DIM)]
        fold_own_ref[part] = dot(spread, own).astype(HALFWORD)
    total = jnp.where(inside & (iota((width, lanes), 0) == place), total, 0.0)
    decoder = dec_ref[0, :, 0, :]
    column = jnp.where(
        iota((width, lanes), 0) == lax.rem(iota((width, lanes), 1), width), 1.0, 0.0
    )
    decoder = dot(decoder, column, precision=lax.Precision.HIGHEST)
    _, channel, _ = lane_places(latents, lanes, span, latents, width)
    keep = (iota((latents, lanes), 1) >= span) & (iota((latents, lanes), 0) == channel)
    vector = jnp.sum(total, axis=0, keepdims=True) + jnp.sum(
        jnp.where(keep, decoder, 0.0), axis=0, keepdims=True
    )
    row_ref[...] = jnp.where(iota((width, lanes), 0) == mine, vector, 0.0)
    proj_rep_ref[...] = dot(once, proj_ref[...]).astype(HALFWORD)
    for device in range(devices):
        first = device * span
        block = conv_ref[0, 0, :, first // lanes * lanes : first // lanes * lanes + lanes].astype(FLOAT)
        if first % lanes:
            block = pltpu.roll(block, lanes - first % lanes, 1)
        conv_out_ref[device] = block


def column_kernel(seq_order, all_order, recv_ref, fold_ref, row_ref, conv_ref, pre_ref, out_ref):
    rows, _, width, _ = recv_ref.shape
    devices, _, lanes = conv_ref.shape
    channels = pre_ref.shape[3]
    images = out_ref.shape[0] // devices
    span = channels // devices
    half = (lanes - span) // 2
    count = rows * width

    def stacked(part):
        tiles = [recv_ref[seq_order.index(source), part].astype(FLOAT) for source in range(rows)]
        return jnp.concatenate(tiles, axis=0).astype(HALFWORD)

    row, col = iota((count, count), 0), iota((count, count), 1)
    allowed = (lax.rem(row, width) == lax.rem(col, width)) & (col <= row)
    grads = attend_tile(stacked(0), stacked(1), stacked(2), stacked(3), allowed)
    total = dot(grads[0], fold_ref[0], 1, 1)
    total = total + dot(grads[1], fold_ref[1], 1, 1)
    total = total + dot(grads[2], fold_ref[2], 1, 1)
    match = lax.rem(iota((count, lanes), 0), width) == lax.rem(iota((count, lanes), 1), width)
    total = jnp.where(match, total, 0.0).reshape(rows, width, lanes)
    share = jnp.sum(total, axis=1) + row_ref[...]
    high = share.astype(HALFWORD).astype(FLOAT)
    lane = iota((rows, lanes), 1)
    pair = jnp.where(lane < span + half, high, share - high)
    pre = pre_ref[0, 0]
    for device in range(devices):
        block = jnp.where(lane < span, conv_ref[device], pair).astype(HALFWORD)
        for image in range(images):
            slot = all_order.index(image * devices + device)
            out_ref[slot, :, :channels] = pre
            out_ref[slot, :, channels:] = block


def final_kernel(all_order, recv_ref, proj_rep_ref, conv_out_ref, proj_out_ref):
    sources, width, _ = recv_ref.shape
    taps, span, channels = conv_out_ref.shape
    latents = proj_out_ref.shape[0]
    lanes = proj_rep_ref.shape[0]
    devices = channels // span
    images = sources // devices
    count = sources * width
    mine = lax.axis_index("seq")
    half = latents * width

    slots = [all_order.index(source) for source in range(sources)]
    pre_wide = jnp.concatenate([recv_ref[slot, :, :channels].astype(FLOAT) for slot in slots], axis=0)
    tail = jnp.concatenate([recv_ref[slot, :, channels:].astype(FLOAT) for slot in slots], axis=0)
    proj_rep = proj_rep_ref[...]
    sigmoid_v = jax.nn.sigmoid(pre_wide)
    act_low = (pre_wide * sigmoid_v).astype(HALFWORD)
    lane = iota((count, lanes), 1)
    match = (
        (lane >= span)
        & (lane < span + half)
        & (lax.rem(iota((count, lanes), 0), width) == lax.rem(lane, width))
    )
    latent_pre = jnp.where(match, dot(act_low, proj_rep, 1, 1), 0.0)
    latent_pre = jnp.sum(latent_pre.reshape(sources, width, lanes), axis=1)
    shares = tail.reshape(images, devices, width, lanes)
    latent = jnp.sum(shares, axis=1).reshape(sources, lanes)
    latent = latent + pltpu.roll(latent, lanes - half, 1)
    halves = [(levels_one - 1.0) * 1.001 / 2.0 for levels_one in fsq_levels]
    _, channel, _ = lane_places(sources, lanes, span, latents, width)
    shift = jnp.zeros((sources, lanes), FLOAT)
    slope = jnp.zeros((sources, lanes), FLOAT)
    for index, (levels_one, bins_one, half_width) in enumerate(zip(fsq_levels, fsq_bins, halves)):
        ratio_one = (0.5 if levels_one % 2.0 == 0.0 else 0.0) / half_width
        shift_one = 0.5 * math.log((1.0 + ratio_one) / (1.0 - ratio_one))
        shift = jnp.where(channel == index, shift_one, shift)
        slope = jnp.where(channel == index, half_width / bins_one, slope)
    tanh_val = jnp.tanh(latent_pre + shift)
    latent_grad = latent * (slope * (1.0 - tanh_val * tanh_val))
    wide = jnp.broadcast_to(latent_grad.reshape(sources, 1, lanes), (sources, width, lanes))
    wide = jnp.where(match, wide.reshape(count, lanes), 0.0).astype(HALFWORD)
    act_grad = dot(wide, proj_rep)
    pre_grad = (act_grad * sigmoid_v * (1.0 + pre_wide * (1.0 - sigmoid_v))).astype(HALFWORD)

    pick = jnp.where(iota((span, lanes), 0) == iota((span, lanes), 1), 1.0, 0.0).astype(HALFWORD)
    inputs = dot(pick, tail.reshape(count, lanes).astype(HALFWORD), 1, 1)
    position = iota((span, count), 1)
    place_x = lax.rem(position, width)
    place_y = lax.rem(lax.div(position, width), devices)
    windows = []
    for row_off in (-1, 0, 1):
        for col_off in (-1, 0, 1):
            step = row_off * width + col_off
            window = pltpu.roll(inputs, -step % count, 1) if step else inputs
            valid = (
                (place_x + col_off >= 0)
                & (place_x + col_off < width)
                & (place_y + row_off >= 0)
                & (place_y + row_off < devices)
            )
            windows.append(jnp.where(valid, window, 0.0))
    windows = jnp.concatenate(windows, axis=0).astype(HALFWORD)
    conv_out_ref[...] = dot(windows, pre_grad).reshape(taps, span, channels)
    proj_term = dot(wide, act_low, 0, 0)[span : span + half]
    proj_term = jnp.sum(proj_term.reshape(latents, width, channels), axis=1)
    proj_out_ref[...] = pltpu.roll(proj_term, lax.rem(channels - mine * span, channels), 1)[:, :span]


def call(kernel, outs, inputs, in_specs=None, flops=1 << 22):
    whole = pl.BlockSpec(memory_space=pltpu.VMEM)
    nbytes = sum(math.prod(one.shape) * one.dtype.itemsize for one in (*inputs, *outs))
    return pl.pallas_call(
        kernel,
        grid=(1,),
        out_shape=outs,
        in_specs=in_specs or [whole] * len(inputs),
        out_specs=[whole] * len(outs),
        compiler_params=pltpu.CompilerParams(vmem_limit_bytes=16 << 20),
        cost_estimate=pl.CostEstimate(flops=flops, bytes_accessed=nbytes, transcendentals=0),
    )(*inputs)


def gather_plan(
    attn_queries,
    attn_keys,
    attn_values,
    out_grad,
    fold_maps,
    dec_grad,
    conv_input,
    pre_act,
    proj_weight,
):
    devices, images = lax.axis_size("seq"), lax.axis_size("dp")
    width, channels, latents = pre_act.shape[2], pre_act.shape[3], proj_weight.shape[0]
    span = channels // devices
    split_at = HALF * HEAD_DIM
    heads = (attn_queries, attn_keys, attn_values, out_grad)
    struct = jax.ShapeDtypeStruct
    members = images * devices
    stride = 3 * members // 8 + 1
    seq_order = list(range(devices))
    all_order = [(members - 1 - stride * slot) % members for slot in range(members)]
    columns = [pl.BlockSpec((1, 1, width, split_at), lambda step: (0, 0, 0, 1))] * 4
    rows = [pl.BlockSpec((1, 1, width, split_at), lambda step: (0, 0, 0, 0))] * 4
    whole = pl.BlockSpec(memory_space=pltpu.VMEM)
    packed = pl.pallas_call(
        functools.partial(pack_kernel, seq_order),
        out_shape=struct((devices, 4, width, HEAD_DIM), HALFWORD),
        in_specs=[pl.BlockSpec(memory_space=pltpu.HBM)] * 4,
        out_specs=pl.BlockSpec(memory_space=pltpu.HBM),
        scratch_shapes=[pltpu.VMEM((devices, 4, width, HEAD_DIM), HALFWORD), pltpu.SemaphoreType.DMA, pltpu.SemaphoreType.DMA],
    )(*heads)
    column = lax.all_to_all(packed, "seq", split_axis=0, concat_axis=0, tiled=True)
    row_share, fold_own, conv_blocks, proj_rep = call(
        local_kernel,
        [
            struct((width, LANES), FLOAT),
            struct((3, LANES, HEAD_DIM), HALFWORD),
            struct((devices, width, LANES), FLOAT),
            struct((LANES, channels), HALFWORD),
        ],
        (*heads, fold_maps, dec_grad, conv_input, proj_weight),
        rows + [whole] * 4,
    )
    (shared,) = call(
        functools.partial(column_kernel, seq_order, all_order),
        [struct((images * devices, width, channels + LANES), HALFWORD)],
        (column, fold_own, row_share, conv_blocks, pre_act),
    )
    spread = lax.all_to_all(
        shared,
        ("dp", "seq"),
        split_axis=0,
        concat_axis=0,
        axis_index_groups=[all_order],
        tiled=True,
    )
    conv_out, proj_out = call(
        functools.partial(final_kernel, all_order),
        [struct((9, span, channels), FLOAT), struct((latents, span), FLOAT)],
        (spread, proj_rep),
    )
    return (jnp.transpose(conv_out, (1, 0, 2)), jnp.transpose(proj_out, (1, 0)))


def on_device(*arrays):
    queries, conv_input, proj_weight = arrays[0], arrays[6], arrays[8]
    devices, images = lax.axis_size("seq"), lax.axis_size("dp")
    rows, width, channels = conv_input.shape[1:]
    latents = proj_weight.shape[0]
    heads = queries.shape[3] // HEAD_DIM - HALF
    positions = images * devices * rows * width
    fits = (
        (conv_input.shape[0], rows, width, heads) == (1, 1, devices, devices)
        and (HALF * 2, width % 8) == (queries.shape[3] // HEAD_DIM, 0)
        and math.gcd(3 * images * devices // 8 + 1, images * devices) == 1
        and channels // devices + 2 * latents * width == LANES
    )
    if fits and positions * channels * 2 <= 9 * channels * channels * 4:
        return gather_plan(*arrays)
    return reduce_plan(*arrays)


def solution(mesh):
    return jax.shard_map(
        on_device,
        mesh=mesh,
        in_specs=(
            P("dp", "seq", None, None),
            P("dp", "seq", None, None),
            P("dp", "seq", None, None),
            P("dp", "seq", None, None),
            P(),
            P("dp", None, "seq", None),
            P("dp", "seq", None, None),
            P("dp", "seq", None, None),
            P(),
        ),
        out_specs=(P("seq", None, None), P("seq", None)),
        check_vma=False,
    )
```

```python
import functools
import math

import jax
import jax.numpy as jnp
from jax import lax
from jax.experimental import pallas as pl
from jax.experimental.pallas import tpu as pltpu
from jax.sharding import PartitionSpec as P

HEAD_DIM = 128
HALF = 8


fsq_levels = (8.0, 8.0, 8.0, 5.0, 5.0, 5.0)
fsq_bins = (4.0, 4.0, 4.0, 2.0, 2.0, 2.0)


def padded_2(block, sides, width):
    for axis, dim in sides:
        count = lax.axis_size(axis)
        forward = [(i, i + 1) for i in range(count - 1)]
        backward = [(target, source) for source, target in forward]
        low = lax.ppermute(
            lax.slice_in_dim(block, block.shape[dim] - width, None, axis=dim), axis, forward
        )
        high = lax.ppermute(lax.slice_in_dim(block, 0, width, axis=dim), axis, backward)
        block = jnp.concatenate([low, block, high], axis=dim)
    return block


def bound_tables():
    halves = [(levels_one - 1.0) * 1.001 / 2.0 for levels_one in fsq_levels]
    shifts = []
    for levels_one, half_width in zip(fsq_levels, halves):
        offset_one = 0.5 if levels_one % 2.0 == 0.0 else 0.0
        ratio_one = offset_one / half_width
        shifts.append(0.5 * math.log((1.0 + ratio_one) / (1.0 - ratio_one)))
    return (
        jnp.array(halves, jnp.float32),
        jnp.array(shifts, jnp.float32),
        jnp.array(fsq_bins, jnp.float32),
    )


def attend_back(queries, keys_in, values_in, grads_in):
    scaling = 1.0 / math.sqrt(queries.shape[-1])
    length = queries.shape[1]
    scores = (
        jnp.einsum("blhd,bmhd->bhlm", queries, keys_in, preferred_element_type=jnp.float32)
        * scaling
    )
    causal = jnp.arange(length)[:, None] >= jnp.arange(length)[None, :]
    scores = jnp.where(causal, scores, -jnp.inf)
    exp_scores = jnp.exp(scores - jnp.max(scores, axis=-1, keepdims=True))
    attn_probs = exp_scores / jnp.sum(exp_scores, axis=-1, keepdims=True)
    probs_low = attn_probs.astype(jnp.bfloat16)
    dprobs = jnp.einsum("blhd,bmhd->bhlm", grads_in, values_in, preferred_element_type=jnp.float32)
    rowdot = jnp.sum(attn_probs * dprobs, axis=-1, keepdims=True)
    dscore = (attn_probs * (dprobs - rowdot) * scaling).astype(jnp.bfloat16)
    grad_query = jnp.einsum(
        "bhlm,bmhd->blhd", dscore, keys_in, preferred_element_type=jnp.float32
    ).astype(jnp.bfloat16)
    grad_key = jnp.einsum(
        "bhlm,blhd->bmhd", dscore, queries, preferred_element_type=jnp.float32
    ).astype(jnp.bfloat16)
    grad_value = jnp.einsum(
        "bhlm,blhd->bmhd", probs_low, grads_in, preferred_element_type=jnp.float32
    ).astype(jnp.bfloat16)
    return (grad_query, grad_key, grad_value)


def fold_sum(grads, maps):
    total = jnp.einsum("cw,iyxw->icyx", maps[0], grads[0], preferred_element_type=jnp.float32)
    total = total + jnp.einsum(
        "cw,iyxw->icyx", maps[1], grads[1], preferred_element_type=jnp.float32
    )
    return total + jnp.einsum(
        "cw,iyxw->icyx", maps[2], grads[2], preferred_element_type=jnp.float32
    )


def reduce_plan(
    attn_queries,
    attn_keys,
    attn_values,
    out_grad,
    fold_maps,
    dec_grad,
    conv_input,
    pre_act,
    proj_weight,
):
    split_at = HALF * HEAD_DIM
    width_cols = attn_queries.shape[2]
    rim_rows = padded_2(conv_input, (("seq", 1),), 1)
    column_parts = (
        lax.all_to_all(
            attn_queries[..., split_at:], "seq", split_axis=2, concat_axis=1, tiled=True
        ),
        lax.all_to_all(attn_keys[..., split_at:], "seq", split_axis=2, concat_axis=1, tiled=True),
        lax.all_to_all(attn_values[..., split_at:], "seq", split_axis=2, concat_axis=1, tiled=True),
        lax.all_to_all(out_grad[..., split_at:], "seq", split_axis=2, concat_axis=1, tiled=True),
    )

    def row_heads(array_in):
        return array_in[0, :, :, :split_at].reshape(array_in.shape[1], width_cols, HALF, HEAD_DIM)

    row_grads = attend_back(
        row_heads(attn_queries), row_heads(attn_keys), row_heads(attn_values), row_heads(out_grad)
    )
    row_grads = [grad_one.reshape(1, 1, width_cols, split_at) for grad_one in row_grads]
    grid_rows = column_parts[0].shape[1]
    col_count = column_parts[0].shape[2]

    def col_heads(array_in):
        return jnp.transpose(array_in[0], (1, 0, 2)).reshape(col_count, grid_rows, HALF, HEAD_DIM)

    col_grads = attend_back(
        col_heads(column_parts[0]),
        col_heads(column_parts[1]),
        col_heads(column_parts[2]),
        col_heads(column_parts[3]),
    )
    col_grads = [
        jnp.transpose(grad_one.reshape(col_count, grid_rows, split_at), (1, 0, 2))[None]
        for grad_one in col_grads
    ]
    latent_col = fold_sum(col_grads, fold_maps[:, :, split_at:])
    latent_rows = lax.all_to_all(latent_col, "seq", split_axis=2, concat_axis=3, tiled=True)
    latent = fold_sum(row_grads, fold_maps[:, :, :split_at]) + latent_rows
    halves, shifts, bins_arr = bound_tables()
    pre_wide = pre_act.astype(jnp.float32)
    sigmoid_v = jax.nn.sigmoid(pre_wide)
    act_low = (pre_wide * sigmoid_v).astype(jnp.bfloat16)
    latent_pre = jnp.einsum(
        "iyxj,cj->icyx", act_low, proj_weight, preferred_element_type=jnp.float32
    )
    tanh_val = jnp.tanh(latent_pre + shifts[None, :, None, None])
    slope_fsq = (halves / bins_arr)[None, :, None, None] * (1.0 - tanh_val * tanh_val)
    latent_grad = ((latent + dec_grad) * slope_fsq).astype(jnp.bfloat16)
    proj_term = jnp.einsum(
        "icyx,iyxj->jc", latent_grad, act_low, preferred_element_type=jnp.float32
    )
    act_grad = jnp.einsum(
        "icyx,cj->iyxj", latent_grad, proj_weight, preferred_element_type=jnp.float32
    )
    pre_grad = (act_grad * sigmoid_v * (1.0 + pre_wide * (1.0 - sigmoid_v))).astype(jnp.bfloat16)
    padded = jnp.pad(rim_rows, ((0, 0), (0, 0), (1, 1), (0, 0)))
    windows = jnp.stack(
        [
            padded[0, row_off, col_off : col_off + width_cols]
            for row_off in range(3)
            for col_off in range(3)
        ]
    )
    conv_term = jnp.einsum(
        "kpa,pb->akb", windows, pre_grad[0, 0], preferred_element_type=jnp.float32
    )
    shares = (
        lax.psum_scatter(conv_term, "seq", scatter_dimension=0, tiled=True),
        lax.psum_scatter(proj_term, "seq", scatter_dimension=0, tiled=True),
    )
    conv_out, proj_out = lax.psum((shares[0], shares[1]), "dp")
    return (conv_out, proj_out)


LANES = 128
FLOAT = jnp.float32
HALFWORD = jnp.bfloat16


def dot(lhs, rhs, lhs_dim=1, rhs_dim=0, precision=None):
    return lax.dot_general(
        lhs,
        rhs,
        (((lhs_dim,), (rhs_dim,)), ((), ())),
        precision=precision,
        preferred_element_type=FLOAT,
    )


def iota(shape, axis):
    return lax.broadcasted_iota(jnp.int32, shape, axis)


def attend_tile(queries, keys_in, values_in, grads_in, allowed):
    scaling = 1.0 / math.sqrt(queries.shape[-1])
    scores = jnp.where(allowed, dot(queries, keys_in, 1, 1) * scaling, -jnp.inf)
    exp_scores = jnp.exp(scores - jnp.max(scores, axis=-1, keepdims=True))
    attn_probs = exp_scores / jnp.sum(exp_scores, axis=-1, keepdims=True)
    dprobs = dot(grads_in, values_in, 1, 1)
    rowdot = jnp.sum(attn_probs * dprobs, axis=-1, keepdims=True)
    dscore = (attn_probs * (dprobs - rowdot) * scaling).astype(HALFWORD)
    return (
        dot(dscore, keys_in).astype(HALFWORD),
        dot(dscore, queries, 0, 0).astype(HALFWORD),
        dot(attn_probs.astype(HALFWORD), grads_in, 0, 0).astype(HALFWORD),
    )


def div(value, count):
    if count & (count - 1) == 0:
        return lax.shift_right_logical(value, count.bit_length() - 1)
    return lax.div(value, count)


def rem(value, count):
    if count & (count - 1) == 0:
        return value & (count - 1)
    return lax.rem(value, count)


def lane_places(rows, lanes, start, latents, width):
    lane = iota((rows, lanes), 1)
    inside = lane >= start
    offset = rem(jnp.maximum(lane - start, 0), latents * width)
    return inside, div(offset, width), rem(offset, width)


def pack_kernel(order, query_ref, key_ref, value_ref, grad_ref, out_ref, held, sem, out_sem):
    copies = []
    for slot, device in enumerate(order):
        lanes = pl.ds((HALF + device) * HEAD_DIM, HEAD_DIM)
        for part, ref in enumerate((query_ref, key_ref, value_ref, grad_ref)):
            copies.append(pltpu.make_async_copy(ref.at[0, 0, :, lanes], held.at[slot, part], sem))
    for copy in copies:
        copy.start()
    for copy in copies:
        copy.wait()
    last = pltpu.make_async_copy(held, out_ref, out_sem)
    last.start()
    last.wait()


def local_kernel(
    query_ref,
    key_ref,
    value_ref,
    grad_ref,
    fold_ref,
    dec_ref,
    conv_ref,
    proj_ref,
    row_ref,
    fold_own_ref,
    conv_out_ref,
    proj_rep_ref,
):
    width = query_ref.shape[2]
    latents = fold_ref.shape[1]
    devices, _, lanes = conv_out_ref.shape
    span = conv_ref.shape[3] // devices
    mine = lax.axis_index("seq")

    def stacked(ref):
        return jnp.concatenate(
            [
                ref[0, 0, :, head * HEAD_DIM : (head + 1) * HEAD_DIM].astype(FLOAT)
                for head in range(HALF)
            ],
            axis=0,
        ).astype(HALFWORD)

    count = HALF * width
    row, col = iota((count, count), 0), iota((count, count), 1)
    allowed = (div(row, width) == div(col, width)) & (col <= row)
    grads = attend_tile(
        stacked(query_ref), stacked(key_ref), stacked(value_ref), stacked(grad_ref), allowed
    )
    inside, channel, place = lane_places(width, lanes, span, latents, width)
    lane = iota((lanes, latents), 0)
    spread_at = rem(jnp.maximum(lane - span, 0), latents * width)
    hit = (lane >= span) & (div(spread_at, width) == iota((lanes, latents), 1))
    spread = jnp.where(hit, 1.0, 0.0).astype(HALFWORD)
    once = jnp.where(hit & (lane < span + latents * width), 1.0, 0.0).astype(HALFWORD)
    split_at = HALF * HEAD_DIM
    total = jnp.zeros((width, lanes), FLOAT)
    for part in range(3):
        maps = dot(spread, fold_ref[part, :, :split_at]).astype(HALFWORD)
        wide = grads[part].astype(FLOAT)
        wide = jnp.concatenate(
            [wide[head * width : (head + 1) * width] for head in range(HALF)], axis=1
        ).astype(HALFWORD)
        total = total + dot(wide, maps, 1, 1)
        own = fold_ref[part, :, pl.ds(pl.multiple_of(split_at + mine * HEAD_DIM, HEAD_DIM), HEAD_DIM)]
        fold_own_ref[part] = dot(spread, own).astype(HALFWORD)
    total = jnp.where(inside & (iota((width, lanes), 0) == place), total, 0.0)
    decoder = dec_ref[0, :, 0, :]
    column = jnp.where(
        iota((width, lanes), 0) == rem(iota((width, lanes), 1), width), 1.0, 0.0
    )
    decoder = dot(decoder, column, precision=lax.Precision.HIGHEST)
    _, channel, _ = lane_places(latents, lanes, span, latents, width)
    keep = (iota((latents, lanes), 1) >= span) & (iota((latents, lanes), 0) == channel)
    vector = jnp.sum(total, axis=0, keepdims=True) + jnp.sum(
        jnp.where(keep, decoder, 0.0), axis=0, keepdims=True
    )
    row_ref[...] = jnp.where(iota((width, lanes), 0) == mine, vector, 0.0)
    proj_rep_ref[...] = dot(once, proj_ref[...]).astype(HALFWORD)
    for device in range(devices):
        first = device * span
        block = conv_ref[0, 0, :, first // lanes * lanes : first // lanes * lanes + lanes].astype(FLOAT)
        if first % lanes:
            block = pltpu.roll(block, lanes - first % lanes, 1)
        conv_out_ref[device] = block


def column_kernel(seq_order, all_order, recv_ref, fold_ref, row_ref, conv_ref, pre_ref, out_ref):
    rows, _, width, _ = recv_ref.shape
    devices, _, lanes = conv_ref.shape
    channels = pre_ref.shape[3]
    images = out_ref.shape[0] // devices
    span = channels // devices
    half = (lanes - span) // 2
    count = rows * width

    def stacked(part):
        tiles = [recv_ref[seq_order.index(source), part].astype(FLOAT) for source in range(rows)]
        return jnp.concatenate(tiles, axis=0).astype(HALFWORD)

    row, col = iota((count, count), 0), iota((count, count), 1)
    allowed = (rem(row, width) == rem(col, width)) & (col <= row)
    grads = attend_tile(stacked(0), stacked(1), stacked(2), stacked(3), allowed)
    total = dot(grads[0], fold_ref[0], 1, 1)
    total = total + dot(grads[1], fold_ref[1], 1, 1)
    total = total + dot(grads[2], fold_ref[2], 1, 1)
    match = iota((width, lanes), 0) == rem(iota((width, lanes), 1), width)
    total = jnp.where(match[None], total.reshape(rows, width, lanes), 0.0)
    share = jnp.sum(total, axis=1) + row_ref[...]
    high = share.astype(HALFWORD).astype(FLOAT)
    lane = iota((rows, lanes), 1)
    pair = jnp.where(lane < span + half, high, share - high)
    pre = pre_ref[0, 0]
    for device in range(devices):
        block = jnp.where(lane < span, conv_ref[device], pair).astype(HALFWORD)
        for image in range(images):
            slot = all_order.index(image * devices + device)
            out_ref[slot, :, :channels] = pre
            out_ref[slot, :, channels:] = block


def final_kernel(all_order, recv_ref, proj_rep_ref, conv_out_ref, proj_out_ref, stage, held, small, sem):
    sources, width, _ = recv_ref.shape
    taps, span, channels = conv_out_ref.shape
    latents = proj_out_ref.shape[0]
    lanes = proj_rep_ref.shape[0]
    devices = channels // span
    images = sources // devices
    count = sources * width
    mine = lax.axis_index("seq")
    half = latents * width

    slots = [all_order.index(source) for source in range(sources)]
    pre_wide = jnp.concatenate([recv_ref[slot, :, :channels].astype(FLOAT) for slot in slots], axis=0)
    tail = jnp.stack([recv_ref[slot, :, channels:].astype(FLOAT) for slot in slots], axis=0)
    pick = jnp.where(iota((span, lanes), 0) == iota((span, lanes), 1), 1.0, 0.0).astype(HALFWORD)
    inputs = dot(pick, tail.reshape(count, lanes).astype(HALFWORD), 1, 1)
    position = iota((8, count), 1)
    place_x = rem(position, width)
    place_y = rem(div(position, width), devices)
    for row_off in (-1, 0, 1):
        for col_off in (-1, 0, 1):
            step = row_off * width + col_off
            window = pltpu.roll(inputs, -step % count, 1) if step else inputs
            valid = (
                (place_x + col_off >= 0)
                & (place_x + col_off < width)
                & (place_y + row_off >= 0)
                & (place_y + row_off < devices)
            )
            window = jnp.where(valid[None], window.reshape(span // 8, 8, count), 0.0)
            tap = 3 * row_off + col_off + 4
            stage[pl.ds(tap * span, span), :] = window.reshape(span, count).astype(HALFWORD)
    proj_rep = proj_rep_ref[...]
    sigmoid_v = 0.5 + 0.5 * jnp.tanh(0.5 * pre_wide)
    act_wide = pre_wide * sigmoid_v
    act_low = act_wide.astype(HALFWORD)
    lane = iota((width, lanes), 1)
    match = (lane >= span) & (lane < span + half) & (iota((width, lanes), 0) == rem(lane, width))
    latent_pre = dot(act_low, proj_rep, 1, 1).reshape(sources, width, lanes)
    shares = tail.reshape(images, devices, width, lanes)
    latent = jnp.sum(shares, axis=1).reshape(sources, lanes)
    latent = latent + pltpu.roll(latent, lanes - half, 1)
    halves = [(levels_one - 1.0) * 1.001 / 2.0 for levels_one in fsq_levels]
    _, channel, _ = lane_places(width, lanes, span, latents, width)
    shift = jnp.zeros((width, lanes), FLOAT)
    slope = jnp.zeros((width, lanes), FLOAT)
    for index, (levels_one, bins_one, half_width) in enumerate(zip(fsq_levels, fsq_bins, halves)):
        ratio_one = (0.5 if levels_one % 2.0 == 0.0 else 0.0) / half_width
        shift_one = 0.5 * math.log((1.0 + ratio_one) / (1.0 - ratio_one))
        shift = jnp.where(channel == index, shift_one, shift)
        slope = jnp.where(channel == index, half_width / bins_one, slope)
    tanh_val = jnp.tanh(latent_pre + shift[None])
    slope = jnp.where(match, slope, 0.0)[None] * (1.0 - tanh_val * tanh_val)
    wide = jnp.broadcast_to(latent.reshape(sources, 1, lanes), (sources, width, lanes)) * slope
    wide = wide.reshape(count, lanes).astype(HALFWORD)
    act_grad = dot(wide, proj_rep)
    silu_grad = sigmoid_v + act_wide * (1.0 - sigmoid_v)
    pre_grad = (act_grad * silu_grad).astype(HALFWORD)

    proj_term = dot(wide, act_low, 0, 0)[span : span + half]
    proj_term = jnp.sum(proj_term.reshape(latents, width, channels), axis=1)
    small[...] = pltpu.roll(proj_term, rem(channels - mine * span, channels), 1)[:, :span]
    copies = [pltpu.make_async_copy(small, proj_out_ref, sem.at[3])]
    copies[0].start()
    for part in range(3):
        rows = pl.ds(3 * part, 3)
        windows = stage[3 * part * span : 3 * (part + 1) * span, :]
        held[rows] = dot(windows, pre_grad).reshape(3, span, channels)
        copies.append(pltpu.make_async_copy(held.at[rows], conv_out_ref.at[rows], sem.at[part]))
        copies[-1].start()
    for copy in copies:
        copy.wait()


def call(kernel, outs, inputs, in_specs=None, flops=1 << 22):
    whole = pl.BlockSpec(memory_space=pltpu.VMEM)
    nbytes = sum(math.prod(one.shape) * one.dtype.itemsize for one in (*inputs, *outs))
    return pl.pallas_call(
        kernel,
        grid=(1,),
        out_shape=outs,
        in_specs=in_specs or [whole] * len(inputs),
        out_specs=[whole] * len(outs),
        compiler_params=pltpu.CompilerParams(vmem_limit_bytes=16 << 20),
        cost_estimate=pl.CostEstimate(flops=flops, bytes_accessed=nbytes, transcendentals=0),
    )(*inputs)


def gather_plan(
    attn_queries,
    attn_keys,
    attn_values,
    out_grad,
    fold_maps,
    dec_grad,
    conv_input,
    pre_act,
    proj_weight,
):
    devices, images = lax.axis_size("seq"), lax.axis_size("dp")
    width, channels, latents = pre_act.shape[2], pre_act.shape[3], proj_weight.shape[0]
    span = channels // devices
    split_at = HALF * HEAD_DIM
    heads = (attn_queries, attn_keys, attn_values, out_grad)
    struct = jax.ShapeDtypeStruct
    members = images * devices
    stride = 3 * members // 8 + 1
    seq_order = [(1 - slot) % devices for slot in range(devices)]
    all_order = [(members - 1 - stride * slot) % members for slot in range(members)]
    columns = [pl.BlockSpec((1, 1, width, split_at), lambda step: (0, 0, 0, 1))] * 4
    rows = [pl.BlockSpec((1, 1, width, split_at), lambda step: (0, 0, 0, 0))] * 4
    whole = pl.BlockSpec(memory_space=pltpu.VMEM)
    packed = pl.pallas_call(
        functools.partial(pack_kernel, seq_order),
        out_shape=struct((devices, 4, width, HEAD_DIM), HALFWORD),
        in_specs=[pl.BlockSpec(memory_space=pltpu.HBM)] * 4,
        out_specs=pl.BlockSpec(memory_space=pltpu.HBM),
        scratch_shapes=[pltpu.VMEM((devices, 4, width, HEAD_DIM), HALFWORD), pltpu.SemaphoreType.DMA, pltpu.SemaphoreType.DMA],
    )(*heads)
    column = lax.all_to_all(packed, "seq", split_axis=0, concat_axis=0, axis_index_groups=[seq_order], tiled=True)
    row_share, fold_own, conv_blocks, proj_rep = call(
        local_kernel,
        [
            struct((width, LANES), FLOAT),
            struct((3, LANES, HEAD_DIM), HALFWORD),
            struct((devices, width, LANES), FLOAT),
            struct((LANES, channels), HALFWORD),
        ],
        (*heads, fold_maps, dec_grad, conv_input, proj_weight),
        rows + [whole] * 4,
    )
    (shared,) = call(
        functools.partial(column_kernel, seq_order, all_order),
        [struct((images * devices, width, channels + LANES), HALFWORD)],
        (column, fold_own, row_share, conv_blocks, pre_act),
    )
    spread = lax.all_to_all(
        shared,
        ("dp", "seq"),
        split_axis=0,
        concat_axis=0,
        axis_index_groups=[all_order],
        tiled=True,
    )
    outs = [struct((9, span, channels), FLOAT), struct((latents, span), FLOAT)]
    conv_out, proj_out = pl.pallas_call(
        functools.partial(final_kernel, all_order),
        out_shape=outs,
        in_specs=[whole] * 2,
        out_specs=[pl.BlockSpec(memory_space=pltpu.HBM)] * 2,
        scratch_shapes=[pltpu.VMEM((9 * span, images * devices * width), HALFWORD)]
        + [pltpu.VMEM(one.shape, one.dtype) for one in outs]
        + [pltpu.SemaphoreType.DMA((4,))],
        compiler_params=pltpu.CompilerParams(vmem_limit_bytes=16 << 20),
    )(spread, proj_rep)
    return (jnp.transpose(conv_out, (1, 0, 2)), jnp.transpose(proj_out, (1, 0)))


def on_device(*arrays):
    queries, conv_input, proj_weight = arrays[0], arrays[6], arrays[8]
    devices, images = lax.axis_size("seq"), lax.axis_size("dp")
    rows, width, channels = conv_input.shape[1:]
    latents = proj_weight.shape[0]
    heads = queries.shape[3] // HEAD_DIM - HALF
    positions = images * devices * rows * width
    fits = (
        (conv_input.shape[0], rows, width, heads) == (1, 1, devices, devices)
        and channels // devices % 8 == 0
        and (HALF * 2, width, images * devices % 8) == (queries.shape[3] // HEAD_DIM, 8, 0)
        and math.gcd(3 * images * devices // 8 + 1, images * devices) == 1
        and channels // devices + 2 * latents * width == LANES
    )
    if fits and positions * channels * 2 <= 9 * channels * channels * 4:
        return gather_plan(*arrays)
    return reduce_plan(*arrays)


def solution(mesh):
    return jax.shard_map(
        on_device,
        mesh=mesh,
        in_specs=(
            P("dp", "seq", None, None),
            P("dp", "seq", None, None),
            P("dp", "seq", None, None),
            P("dp", "seq", None, None),
            P(),
            P("dp", None, "seq", None),
            P("dp", "seq", None, None),
            P("dp", "seq", None, None),
            P(),
        ),
        out_specs=(P("seq", None, None), P("seq", None)),
        check_vma=False,
    )
```

```python
import functools
import math

import jax
import jax.numpy as jnp
from jax import lax
from jax.experimental import pallas as pl
from jax.experimental.pallas import tpu as pltpu
from jax.sharding import PartitionSpec as P

HEAD_DIM = 128
HALF = 8


fsq_levels = (8.0, 8.0, 8.0, 5.0, 5.0, 5.0)
fsq_bins = (4.0, 4.0, 4.0, 2.0, 2.0, 2.0)


def padded_2(block, sides, width):
    for axis, dim in sides:
        count = lax.axis_size(axis)
        forward = [(i, i + 1) for i in range(count - 1)]
        backward = [(target, source) for source, target in forward]
        low = lax.ppermute(
            lax.slice_in_dim(block, block.shape[dim] - width, None, axis=dim), axis, forward
        )
        high = lax.ppermute(lax.slice_in_dim(block, 0, width, axis=dim), axis, backward)
        block = jnp.concatenate([low, block, high], axis=dim)
    return block


def bound_tables():
    halves = [(levels_one - 1.0) * 1.001 / 2.0 for levels_one in fsq_levels]
    shifts = []
    for levels_one, half_width in zip(fsq_levels, halves):
        offset_one = 0.5 if levels_one % 2.0 == 0.0 else 0.0
        ratio_one = offset_one / half_width
        shifts.append(0.5 * math.log((1.0 + ratio_one) / (1.0 - ratio_one)))
    return (
        jnp.array(halves, jnp.float32),
        jnp.array(shifts, jnp.float32),
        jnp.array(fsq_bins, jnp.float32),
    )


def attend_back(queries, keys_in, values_in, grads_in):
    scaling = 1.0 / math.sqrt(queries.shape[-1])
    length = queries.shape[1]
    scores = (
        jnp.einsum("blhd,bmhd->bhlm", queries, keys_in, preferred_element_type=jnp.float32)
        * scaling
    )
    causal = jnp.arange(length)[:, None] >= jnp.arange(length)[None, :]
    scores = jnp.where(causal, scores, -jnp.inf)
    exp_scores = jnp.exp(scores - jnp.max(scores, axis=-1, keepdims=True))
    attn_probs = exp_scores / jnp.sum(exp_scores, axis=-1, keepdims=True)
    probs_low = attn_probs.astype(jnp.bfloat16)
    dprobs = jnp.einsum("blhd,bmhd->bhlm", grads_in, values_in, preferred_element_type=jnp.float32)
    rowdot = jnp.sum(attn_probs * dprobs, axis=-1, keepdims=True)
    dscore = (attn_probs * (dprobs - rowdot) * scaling).astype(jnp.bfloat16)
    grad_query = jnp.einsum(
        "bhlm,bmhd->blhd", dscore, keys_in, preferred_element_type=jnp.float32
    ).astype(jnp.bfloat16)
    grad_key = jnp.einsum(
        "bhlm,blhd->bmhd", dscore, queries, preferred_element_type=jnp.float32
    ).astype(jnp.bfloat16)
    grad_value = jnp.einsum(
        "bhlm,blhd->bmhd", probs_low, grads_in, preferred_element_type=jnp.float32
    ).astype(jnp.bfloat16)
    return (grad_query, grad_key, grad_value)


def fold_sum(grads, maps):
    total = jnp.einsum("cw,iyxw->icyx", maps[0], grads[0], preferred_element_type=jnp.float32)
    total = total + jnp.einsum(
        "cw,iyxw->icyx", maps[1], grads[1], preferred_element_type=jnp.float32
    )
    return total + jnp.einsum(
        "cw,iyxw->icyx", maps[2], grads[2], preferred_element_type=jnp.float32
    )


def reduce_plan(
    attn_queries,
    attn_keys,
    attn_values,
    out_grad,
    fold_maps,
    dec_grad,
    conv_input,
    pre_act,
    proj_weight,
):
    split_at = HALF * HEAD_DIM
    width_cols = attn_queries.shape[2]
    rim_rows = padded_2(conv_input, (("seq", 1),), 1)
    column_parts = (
        lax.all_to_all(
            attn_queries[..., split_at:], "seq", split_axis=2, concat_axis=1, tiled=True
        ),
        lax.all_to_all(attn_keys[..., split_at:], "seq", split_axis=2, concat_axis=1, tiled=True),
        lax.all_to_all(attn_values[..., split_at:], "seq", split_axis=2, concat_axis=1, tiled=True),
        lax.all_to_all(out_grad[..., split_at:], "seq", split_axis=2, concat_axis=1, tiled=True),
    )

    def row_heads(array_in):
        return array_in[0, :, :, :split_at].reshape(array_in.shape[1], width_cols, HALF, HEAD_DIM)

    row_grads = attend_back(
        row_heads(attn_queries), row_heads(attn_keys), row_heads(attn_values), row_heads(out_grad)
    )
    row_grads = [grad_one.reshape(1, 1, width_cols, split_at) for grad_one in row_grads]
    grid_rows = column_parts[0].shape[1]
    col_count = column_parts[0].shape[2]

    def col_heads(array_in):
        return jnp.transpose(array_in[0], (1, 0, 2)).reshape(col_count, grid_rows, HALF, HEAD_DIM)

    col_grads = attend_back(
        col_heads(column_parts[0]),
        col_heads(column_parts[1]),
        col_heads(column_parts[2]),
        col_heads(column_parts[3]),
    )
    col_grads = [
        jnp.transpose(grad_one.reshape(col_count, grid_rows, split_at), (1, 0, 2))[None]
        for grad_one in col_grads
    ]
    latent_col = fold_sum(col_grads, fold_maps[:, :, split_at:])
    latent_rows = lax.all_to_all(latent_col, "seq", split_axis=2, concat_axis=3, tiled=True)
    latent = fold_sum(row_grads, fold_maps[:, :, :split_at]) + latent_rows
    halves, shifts, bins_arr = bound_tables()
    pre_wide = pre_act.astype(jnp.float32)
    sigmoid_v = jax.nn.sigmoid(pre_wide)
    act_low = (pre_wide * sigmoid_v).astype(jnp.bfloat16)
    latent_pre = jnp.einsum(
        "iyxj,cj->icyx", act_low, proj_weight, preferred_element_type=jnp.float32
    )
    tanh_val = jnp.tanh(latent_pre + shifts[None, :, None, None])
    slope_fsq = (halves / bins_arr)[None, :, None, None] * (1.0 - tanh_val * tanh_val)
    latent_grad = ((latent + dec_grad) * slope_fsq).astype(jnp.bfloat16)
    proj_term = jnp.einsum(
        "icyx,iyxj->jc", latent_grad, act_low, preferred_element_type=jnp.float32
    )
    act_grad = jnp.einsum(
        "icyx,cj->iyxj", latent_grad, proj_weight, preferred_element_type=jnp.float32
    )
    pre_grad = (act_grad * sigmoid_v * (1.0 + pre_wide * (1.0 - sigmoid_v))).astype(jnp.bfloat16)
    padded = jnp.pad(rim_rows, ((0, 0), (0, 0), (1, 1), (0, 0)))
    windows = jnp.stack(
        [
            padded[0, row_off, col_off : col_off + width_cols]
            for row_off in range(3)
            for col_off in range(3)
        ]
    )
    conv_term = jnp.einsum(
        "kpa,pb->akb", windows, pre_grad[0, 0], preferred_element_type=jnp.float32
    )
    shares = (
        lax.psum_scatter(conv_term, "seq", scatter_dimension=0, tiled=True),
        lax.psum_scatter(proj_term, "seq", scatter_dimension=0, tiled=True),
    )
    conv_out, proj_out = lax.psum((shares[0], shares[1]), "dp")
    return (conv_out, proj_out)


LANES = 128
FLOAT = jnp.float32
HALFWORD = jnp.bfloat16


def dot(lhs, rhs, lhs_dim=1, rhs_dim=0, precision=None):
    return lax.dot_general(
        lhs,
        rhs,
        (((lhs_dim,), (rhs_dim,)), ((), ())),
        precision=precision,
        preferred_element_type=FLOAT,
    )


def iota(shape, axis):
    return lax.broadcasted_iota(jnp.int32, shape, axis)


def attend_tile(queries, keys_in, values_in, grads_in, allowed):
    scaling = 1.0 / math.sqrt(queries.shape[-1])
    scores = jnp.where(allowed, dot(queries, keys_in, 1, 1) * scaling, -jnp.inf)
    exp_scores = jnp.exp(scores - jnp.max(scores, axis=-1, keepdims=True))
    attn_probs = exp_scores / jnp.sum(exp_scores, axis=-1, keepdims=True)
    dprobs = dot(grads_in, values_in, 1, 1)
    rowdot = jnp.sum(attn_probs * dprobs, axis=-1, keepdims=True)
    dscore = (attn_probs * (dprobs - rowdot) * scaling).astype(HALFWORD)
    return (
        dot(dscore, keys_in).astype(HALFWORD),
        dot(dscore, queries, 0, 0).astype(HALFWORD),
        dot(attn_probs.astype(HALFWORD), grads_in, 0, 0).astype(HALFWORD),
    )


def div(value, count):
    if count & (count - 1) == 0:
        return lax.shift_right_logical(value, count.bit_length() - 1)
    return lax.div(value, count)


def rem(value, count):
    if count & (count - 1) == 0:
        return value & (count - 1)
    return lax.rem(value, count)


def lane_places(rows, lanes, start, latents, width):
    lane = iota((rows, lanes), 1)
    inside = lane >= start
    offset = rem(jnp.maximum(lane - start, 0), latents * width)
    return inside, div(offset, width), rem(offset, width)


def pack_kernel(order, query_ref, key_ref, value_ref, grad_ref, out_ref, held, sem, out_sem):
    copies = []
    for slot, device in enumerate(order):
        lanes = pl.ds((HALF + device) * HEAD_DIM, HEAD_DIM)
        for part, ref in enumerate((query_ref, key_ref, value_ref, grad_ref)):
            copies.append(pltpu.make_async_copy(ref.at[0, 0, :, lanes], held.at[slot, part], sem))
    for copy in copies:
        copy.start()
    for copy in copies:
        copy.wait()
    last = pltpu.make_async_copy(held, out_ref, out_sem)
    last.start()
    last.wait()


def local_kernel(
    query_ref,
    key_ref,
    value_ref,
    grad_ref,
    fold_ref,
    dec_ref,
    conv_ref,
    pre_ref,
    proj_ref,
    row_ref,
    slope_ref,
    fold_own_ref,
    conv_out_ref,
    proj_rep_ref,
):
    width = query_ref.shape[2]
    latents = fold_ref.shape[1]
    devices, _, lanes = conv_out_ref.shape
    span = conv_ref.shape[3] // devices
    mine = lax.axis_index("seq")

    def stacked(ref):
        return jnp.concatenate(
            [
                ref[0, 0, :, head * HEAD_DIM : (head + 1) * HEAD_DIM].astype(FLOAT)
                for head in range(HALF)
            ],
            axis=0,
        ).astype(HALFWORD)

    count = HALF * width
    row, col = iota((count, count), 0), iota((count, count), 1)
    allowed = (div(row, width) == div(col, width)) & (col <= row)
    grads = attend_tile(
        stacked(query_ref), stacked(key_ref), stacked(value_ref), stacked(grad_ref), allowed
    )
    inside, channel, place = lane_places(width, lanes, span, latents, width)
    lane = iota((lanes, latents), 0)
    spread_at = rem(jnp.maximum(lane - span, 0), latents * width)
    hit = (lane >= span) & (div(spread_at, width) == iota((lanes, latents), 1))
    spread = jnp.where(hit, 1.0, 0.0).astype(HALFWORD)
    once = jnp.where(hit & (lane < span + latents * width), 1.0, 0.0).astype(HALFWORD)
    split_at = HALF * HEAD_DIM
    total = jnp.zeros((width, lanes), FLOAT)
    for part in range(3):
        maps = dot(spread, fold_ref[part, :, :split_at]).astype(HALFWORD)
        wide = grads[part].astype(FLOAT)
        wide = jnp.concatenate(
            [wide[head * width : (head + 1) * width] for head in range(HALF)], axis=1
        ).astype(HALFWORD)
        total = total + dot(wide, maps, 1, 1)
        own = fold_ref[part, :, pl.ds(pl.multiple_of(split_at + mine * HEAD_DIM, HEAD_DIM), HEAD_DIM)]
        fold_own_ref[part] = dot(spread, own).astype(HALFWORD)
    total = jnp.where(inside & (iota((width, lanes), 0) == place), total, 0.0)
    decoder = dec_ref[0, :, 0, :]
    column = jnp.where(
        iota((width, lanes), 0) == rem(iota((width, lanes), 1), width), 1.0, 0.0
    )
    decoder = dot(decoder, column, precision=lax.Precision.HIGHEST)
    _, channel, _ = lane_places(latents, lanes, span, latents, width)
    keep = (iota((latents, lanes), 1) >= span) & (iota((latents, lanes), 0) == channel)
    vector = jnp.sum(total, axis=0, keepdims=True) + jnp.sum(
        jnp.where(keep, decoder, 0.0), axis=0, keepdims=True
    )
    row_ref[...] = jnp.where(iota((width, lanes), 0) == mine, vector, 0.0)
    proj_rep_ref[...] = dot(once, proj_ref[...]).astype(HALFWORD)
    pre_wide = pre_ref[0, 0].astype(FLOAT)
    act_low = (pre_wide * jax.nn.sigmoid(pre_wide)).astype(HALFWORD)
    proj_all = dot(spread, proj_ref[...]).astype(HALFWORD)
    latent_pre = dot(act_low, proj_all, 1, 1)
    halves = [(levels_one - 1.0) * 1.001 / 2.0 for levels_one in fsq_levels]
    _, channel, _ = lane_places(width, lanes, span, latents, width)
    shift = jnp.zeros((width, lanes), FLOAT)
    slope = jnp.zeros((width, lanes), FLOAT)
    for index, (levels_one, bins_one, half_width) in enumerate(zip(fsq_levels, fsq_bins, halves)):
        ratio_one = (0.5 if levels_one % 2.0 == 0.0 else 0.0) / half_width
        shift_one = 0.5 * math.log((1.0 + ratio_one) / (1.0 - ratio_one))
        shift = jnp.where(channel == index, shift_one, shift)
        slope = jnp.where(channel == index, half_width / bins_one, slope)
    tanh_val = jnp.tanh(latent_pre + shift)
    slope = slope * (1.0 - tanh_val * tanh_val)
    slope = jnp.where(inside & (iota((width, lanes), 0) == place), slope, 0.0)
    vector = jnp.sum(slope, axis=0, keepdims=True)
    slope_ref[...] = jnp.where(iota((width, lanes), 0) == mine, vector, 0.0)
    for device in range(devices):
        first = device * span
        block = conv_ref[0, 0, :, first // lanes * lanes : first // lanes * lanes + lanes].astype(FLOAT)
        if first % lanes:
            block = pltpu.roll(block, lanes - first % lanes, 1)
        conv_out_ref[device] = block


def column_kernel(
    seq_order, chip_order, recv_ref, fold_ref, row_ref, slope_ref, conv_ref, pre_ref, out_ref
):
    rows, _, width, _ = recv_ref.shape
    devices, _, lanes = conv_ref.shape
    channels = pre_ref.shape[3]
    span = channels // devices
    half = (lanes - span) // 2
    count = rows * width

    def stacked(part):
        tiles = [recv_ref[seq_order.index(source), part].astype(FLOAT) for source in range(rows)]
        return jnp.concatenate(tiles, axis=0).astype(HALFWORD)

    row, col = iota((count, count), 0), iota((count, count), 1)
    allowed = (rem(row, width) == rem(col, width)) & (col <= row)
    grads = attend_tile(stacked(0), stacked(1), stacked(2), stacked(3), allowed)
    total = dot(grads[0], fold_ref[0], 1, 1)
    total = total + dot(grads[1], fold_ref[1], 1, 1)
    total = total + dot(grads[2], fold_ref[2], 1, 1)
    match = iota((width, lanes), 0) == rem(iota((width, lanes), 1), width)
    total = jnp.where(match[None], total.reshape(rows, width, lanes), 0.0)
    share = jnp.sum(total, axis=1) + row_ref[...]
    lane = iota((rows, lanes), 1)

    def pair(value):
        high = value.astype(HALFWORD).astype(FLOAT)
        return jnp.where(lane < span + half, high, value - high)

    parts = (pair(share), pair(slope_ref[...]))
    pre = pre_ref[0, 0]
    chips = devices // 2
    for chip in range(chips):
        blocks = [
            jnp.where(lane < span, conv_ref[2 * chip + core], parts[core]).astype(HALFWORD)
            for core in range(2)
        ]
        for slot, member in enumerate(chip_order):
            if member % chips == chip:
                out_ref[slot, :, :channels] = pre
                out_ref[slot, :, channels : channels + lanes] = blocks[0]
                out_ref[slot, :, channels + lanes :] = blocks[1]


def final_kernel(
    chip_order, own_ref, other_ref, proj_rep_ref, conv_out_ref, proj_out_ref, stage, held, small, sem
):
    members, width, _ = own_ref.shape
    taps, span, channels = conv_out_ref.shape
    latents = proj_out_ref.shape[0]
    lanes = proj_rep_ref.shape[0]
    devices = channels // span
    chips = devices // 2
    sources = 2 * members
    images = sources // devices
    count = sources * width
    mine = lax.axis_index("seq")
    half = latents * width
    lane = iota((width, lanes), 1)
    match = (lane >= span) & (lane < span + half) & (iota((width, lanes), 0) == rem(lane, width))

    def finish(core):
        def rows(first, size):
            tiles = []
            for source in range(sources):
                image, place = divmod(source, devices)
                ref = own_ref if place % 2 == core else other_ref
                slot = chip_order.index(image * chips + place // 2)
                tiles.append(ref[slot, :, first : first + size].astype(FLOAT))
            return jnp.stack(tiles, axis=0)

        tails = [rows(channels, lanes), rows(channels + lanes, lanes)]
        pick = jnp.where(iota((span, lanes), 0) == iota((span, lanes), 1), 1.0, 0.0)
        inputs = dot(
            pick.astype(HALFWORD), tails[core].reshape(count, lanes).astype(HALFWORD), 1, 1
        )
        position = iota((8, count), 1)
        place_x = rem(position, width)
        place_y = rem(div(position, width), devices)
        for row_off in (-1, 0, 1):
            for col_off in (-1, 0, 1):
                step = row_off * width + col_off
                window = pltpu.roll(inputs, -step % count, 1) if step else inputs
                valid = (
                    (place_x + col_off >= 0)
                    & (place_x + col_off < width)
                    & (place_y + row_off >= 0)
                    & (place_y + row_off < devices)
                )
                window = jnp.where(valid[None], window.reshape(span // 8, 8, count), 0.0)
                tap = 3 * row_off + col_off + 4
                stage[pl.ds(tap * span, span), :] = window.reshape(span, count).astype(HALFWORD)
        proj_rep = proj_rep_ref[...]
        latent, slope = [
            jnp.sum(tail.reshape(images, devices, width, lanes), axis=1).reshape(sources, lanes)
            for tail in tails
        ]
        latent = latent + pltpu.roll(latent, lanes - half, 1)
        slope = slope + pltpu.roll(slope, lanes - half, 1)
        latent_grad = (latent * slope).reshape(sources, 1, lanes)
        wide = jnp.broadcast_to(latent_grad, (sources, width, lanes))
        wide = jnp.where(match[None], wide, 0.0).reshape(count, lanes).astype(HALFWORD)
        act_grad = dot(wide, proj_rep)
        pre_wide = rows(0, channels).reshape(count, channels)
        sigmoid_v = 0.5 + 0.5 * jnp.tanh(0.5 * pre_wide)
        act_wide = pre_wide * sigmoid_v
        act_low = act_wide.astype(HALFWORD)
        silu_grad = sigmoid_v + act_wide * (1.0 - sigmoid_v)
        pre_grad = (act_grad * silu_grad).astype(HALFWORD)
        proj_term = dot(wide, act_low, 0, 0)[span : span + half]
        proj_term = jnp.sum(proj_term.reshape(latents, width, channels), axis=1)
        turn = rem(channels - mine * span, channels)
        small[...] = pltpu.roll(proj_term, turn, 1)[:, :span]
        copies = [pltpu.make_async_copy(small, proj_out_ref, sem.at[3])]
        copies[0].start()
        for part in range(3):
            block = pl.ds(3 * part, 3)
            windows = stage[3 * part * span : 3 * (part + 1) * span, :]
            held[block] = dot(windows, pre_grad).reshape(3, span, channels)
            copies.append(
                pltpu.make_async_copy(held.at[block], conv_out_ref.at[block], sem.at[part])
            )
            copies[-1].start()
        for copy in copies:
            copy.wait()

    for core in range(2):
        pl.when(rem(mine, 2) == core)(functools.partial(finish, core))


def call(kernel, outs, inputs, in_specs=None, flops=1 << 22):
    whole = pl.BlockSpec(memory_space=pltpu.VMEM)
    nbytes = sum(math.prod(one.shape) * one.dtype.itemsize for one in (*inputs, *outs))
    return pl.pallas_call(
        kernel,
        grid=(1,),
        out_shape=outs,
        in_specs=in_specs or [whole] * len(inputs),
        out_specs=[whole] * len(outs),
        compiler_params=pltpu.CompilerParams(vmem_limit_bytes=16 << 20),
        cost_estimate=pl.CostEstimate(flops=flops, bytes_accessed=nbytes, transcendentals=0),
    )(*inputs)


def gather_plan(
    attn_queries,
    attn_keys,
    attn_values,
    out_grad,
    fold_maps,
    dec_grad,
    conv_input,
    pre_act,
    proj_weight,
):
    devices, images = lax.axis_size("seq"), lax.axis_size("dp")
    width, channels, latents = pre_act.shape[2], pre_act.shape[3], proj_weight.shape[0]
    span = channels // devices
    split_at = HALF * HEAD_DIM
    heads = (attn_queries, attn_keys, attn_values, out_grad)
    struct = jax.ShapeDtypeStruct
    members = images * devices
    chips = devices // 2
    seq_order = [(devices // 2 - 1 - slot) % devices for slot in range(devices)]
    chip_order = [(members // 2 - 1 + slot) % (members // 2) for slot in range(members // 2)]
    core_groups = [
        [member // chips * devices + member % chips * 2 + core for member in chip_order]
        for core in range(2)
    ]
    columns = [pl.BlockSpec((1, 1, width, split_at), lambda step: (0, 0, 0, 1))] * 4
    rows = [pl.BlockSpec((1, 1, width, split_at), lambda step: (0, 0, 0, 0))] * 4
    whole = pl.BlockSpec(memory_space=pltpu.VMEM)
    packed = pl.pallas_call(
        functools.partial(pack_kernel, seq_order),
        out_shape=struct((devices, 4, width, HEAD_DIM), HALFWORD),
        in_specs=[pl.BlockSpec(memory_space=pltpu.HBM)] * 4,
        out_specs=pl.BlockSpec(memory_space=pltpu.HBM),
        scratch_shapes=[pltpu.VMEM((devices, 4, width, HEAD_DIM), HALFWORD), pltpu.SemaphoreType.DMA, pltpu.SemaphoreType.DMA],
    )(*heads)
    column = lax.all_to_all(packed, "seq", split_axis=0, concat_axis=0, axis_index_groups=[seq_order], tiled=True)
    row_share, slopes, fold_own, conv_blocks, proj_rep = call(
        local_kernel,
        [
            struct((width, LANES), FLOAT),
            struct((width, LANES), FLOAT),
            struct((3, LANES, HEAD_DIM), HALFWORD),
            struct((devices, width, LANES), FLOAT),
            struct((LANES, channels), HALFWORD),
        ],
        (*heads, fold_maps, dec_grad, conv_input, pre_act, proj_weight),
        rows + [whole] * 5,
    )
    (shared,) = call(
        functools.partial(column_kernel, seq_order, chip_order),
        [struct((members // 2, width, channels + 2 * LANES), HALFWORD)],
        (column, fold_own, row_share, slopes, conv_blocks, pre_act),
    )
    spread = lax.all_to_all(
        shared,
        ("dp", "seq"),
        split_axis=0,
        concat_axis=0,
        axis_index_groups=core_groups,
        tiled=True,
    )
    partner = lax.ppermute(spread, "seq", [(one, one ^ 1) for one in range(devices)])
    outs = [struct((9, span, channels), FLOAT), struct((latents, span), FLOAT)]
    conv_out, proj_out = pl.pallas_call(
        functools.partial(final_kernel, chip_order),
        out_shape=outs,
        in_specs=[whole] * 3,
        out_specs=[pl.BlockSpec(memory_space=pltpu.HBM)] * 2,
        scratch_shapes=[pltpu.VMEM((9 * span, images * devices * width), HALFWORD)]
        + [pltpu.VMEM(one.shape, one.dtype) for one in outs]
        + [pltpu.SemaphoreType.DMA((4,))],
        compiler_params=pltpu.CompilerParams(vmem_limit_bytes=16 << 20),
    )(spread, partner, proj_rep)
    return (jnp.transpose(conv_out, (1, 0, 2)), jnp.transpose(proj_out, (1, 0)))


def on_device(*arrays):
    queries, conv_input, proj_weight = arrays[0], arrays[6], arrays[8]
    devices, images = lax.axis_size("seq"), lax.axis_size("dp")
    rows, width, channels = conv_input.shape[1:]
    latents = proj_weight.shape[0]
    heads = queries.shape[3] // HEAD_DIM - HALF
    positions = images * devices * rows * width
    fits = (
        (conv_input.shape[0], rows, width, heads) == (1, 1, devices, devices)
        and channels // devices % 8 == 0
        and (HALF * 2, width, images * devices % 8) == (queries.shape[3] // HEAD_DIM, 8, 0)
        and devices % 2 == 0
        and channels // devices + 2 * latents * width == LANES
    )
    if fits and positions * channels * 2 <= 9 * channels * channels * 4:
        return gather_plan(*arrays)
    return reduce_plan(*arrays)


def solution(mesh):
    return jax.shard_map(
        on_device,
        mesh=mesh,
        in_specs=(
            P("dp", "seq", None, None),
            P("dp", "seq", None, None),
            P("dp", "seq", None, None),
            P("dp", "seq", None, None),
            P(),
            P("dp", None, "seq", None),
            P("dp", "seq", None, None),
            P("dp", "seq", None, None),
            P(),
        ),
        out_specs=(P("seq", None, None), P("seq", None)),
        check_vma=False,
    )
```

```python
import functools
import math

import jax
import jax.numpy as jnp
from jax import lax
from jax.experimental import pallas as pl
from jax.experimental.pallas import tpu as pltpu
from jax.sharding import PartitionSpec as P

HEAD_DIM = 128
HALF = 8


fsq_levels = (8.0, 8.0, 8.0, 5.0, 5.0, 5.0)
fsq_bins = (4.0, 4.0, 4.0, 2.0, 2.0, 2.0)


def padded_2(block, sides, width):
    for axis, dim in sides:
        count = lax.axis_size(axis)
        forward = [(i, i + 1) for i in range(count - 1)]
        backward = [(target, source) for source, target in forward]
        low = lax.ppermute(
            lax.slice_in_dim(block, block.shape[dim] - width, None, axis=dim), axis, forward
        )
        high = lax.ppermute(lax.slice_in_dim(block, 0, width, axis=dim), axis, backward)
        block = jnp.concatenate([low, block, high], axis=dim)
    return block


def bound_tables():
    halves = [(levels_one - 1.0) * 1.001 / 2.0 for levels_one in fsq_levels]
    shifts = []
    for levels_one, half_width in zip(fsq_levels, halves):
        offset_one = 0.5 if levels_one % 2.0 == 0.0 else 0.0
        ratio_one = offset_one / half_width
        shifts.append(0.5 * math.log((1.0 + ratio_one) / (1.0 - ratio_one)))
    return (
        jnp.array(halves, jnp.float32),
        jnp.array(shifts, jnp.float32),
        jnp.array(fsq_bins, jnp.float32),
    )


def attend_back(queries, keys_in, values_in, grads_in):
    scaling = 1.0 / math.sqrt(queries.shape[-1])
    length = queries.shape[1]
    scores = (
        jnp.einsum("blhd,bmhd->bhlm", queries, keys_in, preferred_element_type=jnp.float32)
        * scaling
    )
    causal = jnp.arange(length)[:, None] >= jnp.arange(length)[None, :]
    scores = jnp.where(causal, scores, -jnp.inf)
    exp_scores = jnp.exp(scores - jnp.max(scores, axis=-1, keepdims=True))
    attn_probs = exp_scores / jnp.sum(exp_scores, axis=-1, keepdims=True)
    probs_low = attn_probs.astype(jnp.bfloat16)
    dprobs = jnp.einsum("blhd,bmhd->bhlm", grads_in, values_in, preferred_element_type=jnp.float32)
    rowdot = jnp.sum(attn_probs * dprobs, axis=-1, keepdims=True)
    dscore = (attn_probs * (dprobs - rowdot) * scaling).astype(jnp.bfloat16)
    grad_query = jnp.einsum(
        "bhlm,bmhd->blhd", dscore, keys_in, preferred_element_type=jnp.float32
    ).astype(jnp.bfloat16)
    grad_key = jnp.einsum(
        "bhlm,blhd->bmhd", dscore, queries, preferred_element_type=jnp.float32
    ).astype(jnp.bfloat16)
    grad_value = jnp.einsum(
        "bhlm,blhd->bmhd", probs_low, grads_in, preferred_element_type=jnp.float32
    ).astype(jnp.bfloat16)
    return (grad_query, grad_key, grad_value)


def fold_sum(grads, maps):
    total = jnp.einsum("cw,iyxw->icyx", maps[0], grads[0], preferred_element_type=jnp.float32)
    total = total + jnp.einsum(
        "cw,iyxw->icyx", maps[1], grads[1], preferred_element_type=jnp.float32
    )
    return total + jnp.einsum(
        "cw,iyxw->icyx", maps[2], grads[2], preferred_element_type=jnp.float32
    )


def reduce_plan(
    attn_queries,
    attn_keys,
    attn_values,
    out_grad,
    fold_maps,
    dec_grad,
    conv_input,
    pre_act,
    proj_weight,
):
    split_at = HALF * HEAD_DIM
    width_cols = attn_queries.shape[2]
    rim_rows = padded_2(conv_input, (("seq", 1),), 1)
    column_parts = (
        lax.all_to_all(
            attn_queries[..., split_at:], "seq", split_axis=2, concat_axis=1, tiled=True
        ),
        lax.all_to_all(attn_keys[..., split_at:], "seq", split_axis=2, concat_axis=1, tiled=True),
        lax.all_to_all(attn_values[..., split_at:], "seq", split_axis=2, concat_axis=1, tiled=True),
        lax.all_to_all(out_grad[..., split_at:], "seq", split_axis=2, concat_axis=1, tiled=True),
    )

    def row_heads(array_in):
        return array_in[0, :, :, :split_at].reshape(array_in.shape[1], width_cols, HALF, HEAD_DIM)

    row_grads = attend_back(
        row_heads(attn_queries), row_heads(attn_keys), row_heads(attn_values), row_heads(out_grad)
    )
    row_grads = [grad_one.reshape(1, 1, width_cols, split_at) for grad_one in row_grads]
    grid_rows = column_parts[0].shape[1]
    col_count = column_parts[0].shape[2]

    def col_heads(array_in):
        return jnp.transpose(array_in[0], (1, 0, 2)).reshape(col_count, grid_rows, HALF, HEAD_DIM)

    col_grads = attend_back(
        col_heads(column_parts[0]),
        col_heads(column_parts[1]),
        col_heads(column_parts[2]),
        col_heads(column_parts[3]),
    )
    col_grads = [
        jnp.transpose(grad_one.reshape(col_count, grid_rows, split_at), (1, 0, 2))[None]
        for grad_one in col_grads
    ]
    latent_col = fold_sum(col_grads, fold_maps[:, :, split_at:])
    latent_rows = lax.all_to_all(latent_col, "seq", split_axis=2, concat_axis=3, tiled=True)
    latent = fold_sum(row_grads, fold_maps[:, :, :split_at]) + latent_rows
    halves, shifts, bins_arr = bound_tables()
    pre_wide = pre_act.astype(jnp.float32)
    sigmoid_v = jax.nn.sigmoid(pre_wide)
    act_low = (pre_wide * sigmoid_v).astype(jnp.bfloat16)
    latent_pre = jnp.einsum(
        "iyxj,cj->icyx", act_low, proj_weight, preferred_element_type=jnp.float32
    )
    tanh_val = jnp.tanh(latent_pre + shifts[None, :, None, None])
    slope_fsq = (halves / bins_arr)[None, :, None, None] * (1.0 - tanh_val * tanh_val)
    latent_grad = ((latent + dec_grad) * slope_fsq).astype(jnp.bfloat16)
    proj_term = jnp.einsum(
        "icyx,iyxj->jc", latent_grad, act_low, preferred_element_type=jnp.float32
    )
    act_grad = jnp.einsum(
        "icyx,cj->iyxj", latent_grad, proj_weight, preferred_element_type=jnp.float32
    )
    pre_grad = (act_grad * sigmoid_v * (1.0 + pre_wide * (1.0 - sigmoid_v))).astype(jnp.bfloat16)
    padded = jnp.pad(rim_rows, ((0, 0), (0, 0), (1, 1), (0, 0)))
    windows = jnp.stack(
        [
            padded[0, row_off, col_off : col_off + width_cols]
            for row_off in range(3)
            for col_off in range(3)
        ]
    )
    conv_term = jnp.einsum(
        "kpa,pb->akb", windows, pre_grad[0, 0], preferred_element_type=jnp.float32
    )
    shares = (
        lax.psum_scatter(conv_term, "seq", scatter_dimension=0, tiled=True),
        lax.psum_scatter(proj_term, "seq", scatter_dimension=0, tiled=True),
    )
    conv_out, proj_out = lax.psum((shares[0], shares[1]), "dp")
    return (conv_out, proj_out)


LANES = 128
FLOAT = jnp.float32
HALFWORD = jnp.bfloat16


def dot(lhs, rhs, lhs_dim=1, rhs_dim=0, precision=None):
    return lax.dot_general(
        lhs,
        rhs,
        (((lhs_dim,), (rhs_dim,)), ((), ())),
        precision=precision,
        preferred_element_type=FLOAT,
    )


def iota(shape, axis):
    return lax.broadcasted_iota(jnp.int32, shape, axis)


def attend_tile(queries, keys_in, values_in, grads_in, allowed):
    scaling = 1.0 / math.sqrt(queries.shape[-1])
    scores = jnp.where(allowed, dot(queries, keys_in, 1, 1) * scaling, -jnp.inf)
    exp_scores = jnp.exp(scores - jnp.max(scores, axis=-1, keepdims=True))
    attn_probs = exp_scores / jnp.sum(exp_scores, axis=-1, keepdims=True)
    dprobs = dot(grads_in, values_in, 1, 1)
    rowdot = jnp.sum(attn_probs * dprobs, axis=-1, keepdims=True)
    dscore = (attn_probs * (dprobs - rowdot) * scaling).astype(HALFWORD)
    return (
        dot(dscore, keys_in).astype(HALFWORD),
        dot(dscore, queries, 0, 0).astype(HALFWORD),
        dot(attn_probs.astype(HALFWORD), grads_in, 0, 0).astype(HALFWORD),
    )


def div(value, count):
    if count & (count - 1) == 0:
        return lax.shift_right_logical(value, count.bit_length() - 1)
    return lax.div(value, count)


def rem(value, count):
    if count & (count - 1) == 0:
        return value & (count - 1)
    return lax.rem(value, count)


def lane_places(rows, lanes, start, latents, width):
    lane = iota((rows, lanes), 1)
    inside = lane >= start
    offset = rem(jnp.maximum(lane - start, 0), latents * width)
    return inside, div(offset, width), rem(offset, width)


def local_kernel(
    order,
    query_hbm,
    key_hbm,
    value_hbm,
    grad_hbm,
    fold_hbm,
    dec_hbm,
    conv_hbm,
    pre_hbm,
    proj_hbm,
    packed_ref,
    row_ref,
    slope_ref,
    fold_own_ref,
    conv_out_ref,
    proj_rep_ref,
    pre_out_ref,
    rows_ref,
    fold_ref,
    dec_ref,
    conv_ref,
    pre_ref,
    proj_ref,
    sem,
    pack_sem,
):
    split_at = HALF * HEAD_DIM
    heads = (query_hbm, key_hbm, value_hbm, grad_hbm)
    copies = [
        pltpu.make_async_copy(ref.at[0, 0, :, pl.ds(0, split_at)], rows_ref.at[part], sem)
        for part, ref in enumerate(heads)
    ]
    copies += [
        pltpu.make_async_copy(source, target, sem)
        for source, target in (
            (fold_hbm, fold_ref),
            (dec_hbm, dec_ref),
            (conv_hbm, conv_ref),
            (pre_hbm, pre_ref),
            (proj_hbm, proj_ref),
        )
    ]
    packs = []
    for slot, device in enumerate(order):
        lanes = pl.ds((HALF + device) * HEAD_DIM, HEAD_DIM)
        for part, ref in enumerate(heads):
            packs.append(
                pltpu.make_async_copy(ref.at[0, 0, :, lanes], packed_ref.at[slot, part], pack_sem)
            )
    for copy in copies + packs:
        copy.start()
    for copy in copies:
        copy.wait()
    width = query_hbm.shape[2]
    latents = fold_ref.shape[1]
    devices, _, lanes = conv_out_ref.shape
    span = conv_ref.shape[3] // devices
    mine = lax.axis_index("seq")

    def stacked(part):
        return jnp.concatenate(
            [
                rows_ref[part, :, head * HEAD_DIM : (head + 1) * HEAD_DIM].astype(FLOAT)
                for head in range(HALF)
            ],
            axis=0,
        ).astype(HALFWORD)

    count = HALF * width
    row, col = iota((count, count), 0), iota((count, count), 1)
    allowed = (div(row, width) == div(col, width)) & (col <= row)
    grads = attend_tile(
        stacked(0), stacked(1), stacked(2), stacked(3), allowed
    )
    inside, channel, place = lane_places(width, lanes, span, latents, width)
    lane = iota((lanes, latents), 0)
    spread_at = rem(jnp.maximum(lane - span, 0), latents * width)
    hit = (lane >= span) & (div(spread_at, width) == iota((lanes, latents), 1))
    spread = jnp.where(hit, 1.0, 0.0).astype(HALFWORD)
    once = jnp.where(hit & (lane < span + latents * width), 1.0, 0.0).astype(HALFWORD)
    compact = jnp.zeros((width, latents), FLOAT)
    for part in range(3):
        wide = grads[part].astype(FLOAT)
        wide = jnp.concatenate(
            [wide[head * width : (head + 1) * width] for head in range(HALF)], axis=1
        ).astype(HALFWORD)
        compact = compact + dot(wide, fold_ref[part, :, :split_at], 1, 1)
        own = fold_ref[part, :, pl.ds(pl.multiple_of(split_at + mine * HEAD_DIM, HEAD_DIM), HEAD_DIM)]
        fold_own_ref[part] = dot(spread, own).astype(HALFWORD)
    diagonal = inside & (iota((width, lanes), 0) == place)

    def spread_out(values):
        result = jnp.zeros((width, lanes), FLOAT)
        for index in range(latents):
            result = jnp.where(diagonal & (channel == index), values[:, index : index + 1], result)
        return result

    total = spread_out(compact)
    decoder = dec_ref[0, :, 0, :]
    column = jnp.where(
        iota((width, lanes), 0) == rem(iota((width, lanes), 1), width), 1.0, 0.0
    )
    decoder = dot(decoder, column, precision=lax.Precision.HIGHEST)
    _, owner, _ = lane_places(latents, lanes, span, latents, width)
    keep = (iota((latents, lanes), 1) >= span) & (iota((latents, lanes), 0) == owner)
    vector = jnp.sum(total, axis=0, keepdims=True) + jnp.sum(
        jnp.where(keep, decoder, 0.0), axis=0, keepdims=True
    )
    row_ref[...] = jnp.where(iota((width, lanes), 0) == mine, vector, 0.0)
    proj_rep_ref[...] = dot(once, proj_ref[...]).astype(HALFWORD)
    pre_out_ref[...] = pre_ref[...]
    pre_wide = pre_ref[0, 0].astype(FLOAT)
    act_low = (pre_wide * jax.nn.sigmoid(pre_wide)).astype(HALFWORD)
    latent_pre = spread_out(dot(act_low, proj_ref[...], 1, 1))
    halves = [(levels_one - 1.0) * 1.001 / 2.0 for levels_one in fsq_levels]
    shift = jnp.zeros((width, lanes), FLOAT)
    slope = jnp.zeros((width, lanes), FLOAT)
    for index, (levels_one, bins_one, half_width) in enumerate(zip(fsq_levels, fsq_bins, halves)):
        ratio_one = (0.5 if levels_one % 2.0 == 0.0 else 0.0) / half_width
        shift_one = 0.5 * math.log((1.0 + ratio_one) / (1.0 - ratio_one))
        shift = jnp.where(channel == index, shift_one, shift)
        slope = jnp.where(channel == index, half_width / bins_one, slope)
    tanh_val = jnp.tanh(latent_pre + shift)
    slope = slope * (1.0 - tanh_val * tanh_val)
    slope = jnp.where(diagonal, slope, 0.0)
    vector = jnp.sum(slope, axis=0, keepdims=True)
    slope_ref[...] = jnp.where(iota((width, lanes), 0) == mine, vector, 0.0)
    for device in range(devices):
        first = device * span
        block = conv_ref[0, 0, :, first // lanes * lanes : first // lanes * lanes + lanes].astype(FLOAT)
        if first % lanes:
            block = pltpu.roll(block, lanes - first % lanes, 1)
        conv_out_ref[device] = block
    for copy in packs:
        copy.wait()


def column_kernel(
    seq_order, chip_order, recv_ref, fold_ref, row_ref, slope_ref, conv_ref, pre_ref, out_ref
):
    rows, _, width, _ = recv_ref.shape
    devices, _, lanes = conv_ref.shape
    channels = pre_ref.shape[3]
    span = channels // devices
    half = (lanes - span) // 2
    count = rows * width

    def stacked(part):
        tiles = [recv_ref[seq_order.index(source), part].astype(FLOAT) for source in range(rows)]
        return jnp.concatenate(tiles, axis=0).astype(HALFWORD)

    row, col = iota((count, count), 0), iota((count, count), 1)
    allowed = (rem(row, width) == rem(col, width)) & (col <= row)
    grads = attend_tile(stacked(0), stacked(1), stacked(2), stacked(3), allowed)
    total = dot(grads[0], fold_ref[0], 1, 1)
    total = total + dot(grads[1], fold_ref[1], 1, 1)
    total = total + dot(grads[2], fold_ref[2], 1, 1)
    match = iota((width, lanes), 0) == rem(iota((width, lanes), 1), width)
    total = jnp.where(match[None], total.reshape(rows, width, lanes), 0.0)
    share = jnp.sum(total, axis=1) + row_ref[...]
    lane = iota((rows, lanes), 1)

    def pair(value):
        high = value.astype(HALFWORD).astype(FLOAT)
        return jnp.where(lane < span + half, high, value - high)

    parts = (pair(share), pair(slope_ref[...]))
    pre = pre_ref[0, 0]
    chips = devices // 2
    for chip in range(chips):
        blocks = [
            jnp.where(lane < span, conv_ref[2 * chip + core], parts[core]).astype(HALFWORD)
            for core in range(2)
        ]
        for slot, member in enumerate(chip_order):
            if member % chips == chip:
                out_ref[slot, :, :channels] = pre
                out_ref[slot, :, channels : channels + lanes] = blocks[0]
                out_ref[slot, :, channels + lanes :] = blocks[1]


def final_kernel(
    chip_order, own_ref, other_ref, proj_rep_ref, conv_out_ref, proj_out_ref, stage, held, small, sem
):
    members, width, _ = own_ref.shape
    taps, span, channels = conv_out_ref.shape
    latents = proj_out_ref.shape[0]
    lanes = proj_rep_ref.shape[0]
    devices = channels // span
    chips = devices // 2
    sources = 2 * members
    images = sources // devices
    count = sources * width
    mine = lax.axis_index("seq")
    half = latents * width
    lane = iota((width, lanes), 1)
    match = (lane >= span) & (lane < span + half) & (iota((width, lanes), 0) == rem(lane, width))

    def finish(core):
        def rows(first, size):
            tiles = []
            for source in range(sources):
                image, place = divmod(source, devices)
                ref = own_ref if place % 2 == core else other_ref
                slot = chip_order.index(image * chips + place // 2)
                tiles.append(ref[slot, :, first : first + size].astype(FLOAT))
            return jnp.stack(tiles, axis=0)

        tails = [rows(channels, lanes), rows(channels + lanes, lanes)]
        pick = jnp.where(iota((span, lanes), 0) == iota((span, lanes), 1), 1.0, 0.0)
        inputs = dot(
            pick.astype(HALFWORD), tails[core].reshape(count, lanes).astype(HALFWORD), 1, 1
        )
        position = iota((8, count), 1)
        place_x = rem(position, width)
        place_y = rem(div(position, width), devices)
        for row_off in (-1, 0, 1):
            for col_off in (-1, 0, 1):
                step = row_off * width + col_off
                window = pltpu.roll(inputs, -step % count, 1) if step else inputs
                valid = (
                    (place_x + col_off >= 0)
                    & (place_x + col_off < width)
                    & (place_y + row_off >= 0)
                    & (place_y + row_off < devices)
                )
                window = jnp.where(valid[None], window.reshape(span // 8, 8, count), 0.0)
                tap = 3 * row_off + col_off + 4
                stage[pl.ds(tap * span, span), :] = window.reshape(span, count).astype(HALFWORD)
        proj_rep = proj_rep_ref[...]
        latent, slope = [
            jnp.sum(tail.reshape(images, devices, width, lanes), axis=1).reshape(sources, lanes)
            for tail in tails
        ]
        latent = latent + pltpu.roll(latent, lanes - half, 1)
        slope = slope + pltpu.roll(slope, lanes - half, 1)
        latent_grad = (latent * slope).reshape(sources, 1, lanes)
        wide = jnp.broadcast_to(latent_grad, (sources, width, lanes))
        wide = jnp.where(match[None], wide, 0.0).reshape(count, lanes).astype(HALFWORD)
        act_grad = dot(wide, proj_rep)
        pre_wide = rows(0, channels).reshape(count, channels)
        sigmoid_v = 0.5 + 0.5 * jnp.tanh(0.5 * pre_wide)
        act_wide = pre_wide * sigmoid_v
        act_low = act_wide.astype(HALFWORD)
        silu_grad = sigmoid_v + act_wide * (1.0 - sigmoid_v)
        pre_grad = (act_grad * silu_grad).astype(HALFWORD)
        proj_term = dot(wide, act_low, 0, 0)[span : span + half]
        proj_term = jnp.sum(proj_term.reshape(latents, width, channels), axis=1)
        turn = rem(channels - mine * span, channels)
        small[...] = pltpu.roll(proj_term, turn, 1)[:, :span]
        copies = [pltpu.make_async_copy(small, proj_out_ref, sem.at[3])]
        copies[0].start()
        for part in range(3):
            block = pl.ds(3 * part, 3)
            windows = stage[3 * part * span : 3 * (part + 1) * span, :]
            held[block] = dot(windows, pre_grad).reshape(3, span, channels)
            copies.append(
                pltpu.make_async_copy(held.at[block], conv_out_ref.at[block], sem.at[part])
            )
            copies[-1].start()
        for copy in copies:
            copy.wait()

    for core in range(2):
        pl.when(rem(mine, 2) == core)(functools.partial(finish, core))


def call(kernel, outs, inputs, in_specs=None, flops=1 << 22):
    whole = pl.BlockSpec(memory_space=pltpu.VMEM)
    nbytes = sum(math.prod(one.shape) * one.dtype.itemsize for one in (*inputs, *outs))
    return pl.pallas_call(
        kernel,
        grid=(1,),
        out_shape=outs,
        in_specs=in_specs or [whole] * len(inputs),
        out_specs=[whole] * len(outs),
        compiler_params=pltpu.CompilerParams(vmem_limit_bytes=16 << 20),
        cost_estimate=pl.CostEstimate(flops=flops, bytes_accessed=nbytes, transcendentals=0),
    )(*inputs)


def gather_plan(
    attn_queries,
    attn_keys,
    attn_values,
    out_grad,
    fold_maps,
    dec_grad,
    conv_input,
    pre_act,
    proj_weight,
):
    devices, images = lax.axis_size("seq"), lax.axis_size("dp")
    width, channels, latents = pre_act.shape[2], pre_act.shape[3], proj_weight.shape[0]
    span = channels // devices
    split_at = HALF * HEAD_DIM
    heads = (attn_queries, attn_keys, attn_values, out_grad)
    struct = jax.ShapeDtypeStruct
    members = images * devices
    chips = devices // 2
    seq_order = [(devices // 2 - 1 - slot) % devices for slot in range(devices)]
    chip_order = [(members // 2 - 1 + slot) % (members // 2) for slot in range(members // 2)]
    core_groups = [
        [member // chips * devices + member % chips * 2 + core for member in chip_order]
        for core in range(2)
    ]
    columns = [pl.BlockSpec((1, 1, width, split_at), lambda step: (0, 0, 0, 1))] * 4
    whole = pl.BlockSpec(memory_space=pltpu.VMEM)
    inputs = (*heads, fold_maps, dec_grad, conv_input, pre_act, proj_weight)
    packed, row_share, slopes, fold_own, conv_blocks, proj_rep, pre_near = pl.pallas_call(
        functools.partial(local_kernel, seq_order),
        out_shape=[
            struct((devices, 4, width, HEAD_DIM), HALFWORD),
            struct((width, LANES), FLOAT),
            struct((width, LANES), FLOAT),
            struct((3, LANES, HEAD_DIM), HALFWORD),
            struct((devices, width, LANES), FLOAT),
            struct((LANES, channels), HALFWORD),
            struct(pre_act.shape, HALFWORD),
        ],
        in_specs=[pl.BlockSpec(memory_space=pltpu.HBM)] * len(inputs),
        out_specs=[whole] * 7,
        scratch_shapes=[pltpu.VMEM((4, width, split_at), HALFWORD)]
        + [pltpu.VMEM(one.shape, one.dtype) for one in inputs[4:]]
        + [pltpu.SemaphoreType.DMA, pltpu.SemaphoreType.DMA],
        compiler_params=pltpu.CompilerParams(vmem_limit_bytes=16 << 20),
    )(*[pltpu.with_memory_space_constraint(one, pltpu.HBM) for one in inputs])
    column = lax.all_to_all(packed, "seq", split_axis=0, concat_axis=0, axis_index_groups=[seq_order], tiled=True)
    (shared,) = call(
        functools.partial(column_kernel, seq_order, chip_order),
        [struct((members // 2, width, channels + 2 * LANES), HALFWORD)],
        (column, fold_own, row_share, slopes, conv_blocks, pre_near),
    )
    spread = lax.all_to_all(
        shared,
        ("dp", "seq"),
        split_axis=0,
        concat_axis=0,
        axis_index_groups=core_groups,
        tiled=True,
    )
    partner = lax.ppermute(spread, "seq", [(one, one ^ 1) for one in range(devices)])
    outs = [struct((9, span, channels), FLOAT), struct((latents, span), FLOAT)]
    conv_out, proj_out = pl.pallas_call(
        functools.partial(final_kernel, chip_order),
        out_shape=outs,
        in_specs=[whole] * 3,
        out_specs=[pl.BlockSpec(memory_space=pltpu.HBM)] * 2,
        scratch_shapes=[pltpu.VMEM((9 * span, images * devices * width), HALFWORD)]
        + [pltpu.VMEM(one.shape, one.dtype) for one in outs]
        + [pltpu.SemaphoreType.DMA((4,))],
        compiler_params=pltpu.CompilerParams(vmem_limit_bytes=16 << 20),
    )(spread, partner, proj_rep)
    return (jnp.transpose(conv_out, (1, 0, 2)), jnp.transpose(proj_out, (1, 0)))


def on_device(*arrays):
    queries, conv_input, proj_weight = arrays[0], arrays[6], arrays[8]
    devices, images = lax.axis_size("seq"), lax.axis_size("dp")
    rows, width, channels = conv_input.shape[1:]
    latents = proj_weight.shape[0]
    heads = queries.shape[3] // HEAD_DIM - HALF
    positions = images * devices * rows * width
    fits = (
        (conv_input.shape[0], rows, width, heads) == (1, 1, devices, devices)
        and channels // devices % 8 == 0
        and (HALF * 2, width, images * devices % 8) == (queries.shape[3] // HEAD_DIM, 8, 0)
        and devices % 2 == 0
        and channels // devices + 2 * latents * width == LANES
    )
    if fits and positions * channels * 2 <= 9 * channels * channels * 4:
        return gather_plan(*arrays)
    return reduce_plan(*arrays)


def solution(mesh):
    return jax.shard_map(
        on_device,
        mesh=mesh,
        in_specs=(
            P("dp", "seq", None, None),
            P("dp", "seq", None, None),
            P("dp", "seq", None, None),
            P("dp", "seq", None, None),
            P(),
            P("dp", None, "seq", None),
            P("dp", "seq", None, None),
            P("dp", "seq", None, None),
            P(),
        ),
        out_specs=(P("seq", None, None), P("seq", None)),
        check_vma=False,
    )
```

```python
import functools
import math

import jax
import jax.numpy as jnp
from jax import lax
from jax.experimental import pallas as pl
from jax.experimental.pallas import tpu as pltpu
from jax.sharding import PartitionSpec as P

HEAD_DIM = 128
HALF = 8


fsq_levels = (8.0, 8.0, 8.0, 5.0, 5.0, 5.0)
fsq_bins = (4.0, 4.0, 4.0, 2.0, 2.0, 2.0)


def padded_2(block, sides, width):
    for axis, dim in sides:
        count = lax.axis_size(axis)
        forward = [(i, i + 1) for i in range(count - 1)]
        backward = [(target, source) for source, target in forward]
        low = lax.ppermute(
            lax.slice_in_dim(block, block.shape[dim] - width, None, axis=dim), axis, forward
        )
        high = lax.ppermute(lax.slice_in_dim(block, 0, width, axis=dim), axis, backward)
        block = jnp.concatenate([low, block, high], axis=dim)
    return block


def bound_tables():
    halves = [(levels_one - 1.0) * 1.001 / 2.0 for levels_one in fsq_levels]
    shifts = []
    for levels_one, half_width in zip(fsq_levels, halves):
        offset_one = 0.5 if levels_one % 2.0 == 0.0 else 0.0
        ratio_one = offset_one / half_width
        shifts.append(0.5 * math.log((1.0 + ratio_one) / (1.0 - ratio_one)))
    return (
        jnp.array(halves, jnp.float32),
        jnp.array(shifts, jnp.float32),
        jnp.array(fsq_bins, jnp.float32),
    )


def attend_back(queries, keys_in, values_in, grads_in):
    scaling = 1.0 / math.sqrt(queries.shape[-1])
    length = queries.shape[1]
    scores = (
        jnp.einsum("blhd,bmhd->bhlm", queries, keys_in, preferred_element_type=jnp.float32)
        * scaling
    )
    causal = jnp.arange(length)[:, None] >= jnp.arange(length)[None, :]
    scores = jnp.where(causal, scores, -jnp.inf)
    exp_scores = jnp.exp(scores - jnp.max(scores, axis=-1, keepdims=True))
    attn_probs = exp_scores / jnp.sum(exp_scores, axis=-1, keepdims=True)
    probs_low = attn_probs.astype(jnp.bfloat16)
    dprobs = jnp.einsum("blhd,bmhd->bhlm", grads_in, values_in, preferred_element_type=jnp.float32)
    rowdot = jnp.sum(attn_probs * dprobs, axis=-1, keepdims=True)
    dscore = (attn_probs * (dprobs - rowdot) * scaling).astype(jnp.bfloat16)
    grad_query = jnp.einsum(
        "bhlm,bmhd->blhd", dscore, keys_in, preferred_element_type=jnp.float32
    ).astype(jnp.bfloat16)
    grad_key = jnp.einsum(
        "bhlm,blhd->bmhd", dscore, queries, preferred_element_type=jnp.float32
    ).astype(jnp.bfloat16)
    grad_value = jnp.einsum(
        "bhlm,blhd->bmhd", probs_low, grads_in, preferred_element_type=jnp.float32
    ).astype(jnp.bfloat16)
    return (grad_query, grad_key, grad_value)


def fold_sum(grads, maps):
    total = jnp.einsum("cw,iyxw->icyx", maps[0], grads[0], preferred_element_type=jnp.float32)
    total = total + jnp.einsum(
        "cw,iyxw->icyx", maps[1], grads[1], preferred_element_type=jnp.float32
    )
    return total + jnp.einsum(
        "cw,iyxw->icyx", maps[2], grads[2], preferred_element_type=jnp.float32
    )


def reduce_plan(
    attn_queries,
    attn_keys,
    attn_values,
    out_grad,
    fold_maps,
    dec_grad,
    conv_input,
    pre_act,
    proj_weight,
):
    split_at = HALF * HEAD_DIM
    width_cols = attn_queries.shape[2]
    rim_rows = padded_2(conv_input, (("seq", 1),), 1)
    column_parts = (
        lax.all_to_all(
            attn_queries[..., split_at:], "seq", split_axis=2, concat_axis=1, tiled=True
        ),
        lax.all_to_all(attn_keys[..., split_at:], "seq", split_axis=2, concat_axis=1, tiled=True),
        lax.all_to_all(attn_values[..., split_at:], "seq", split_axis=2, concat_axis=1, tiled=True),
        lax.all_to_all(out_grad[..., split_at:], "seq", split_axis=2, concat_axis=1, tiled=True),
    )

    def row_heads(array_in):
        return array_in[0, :, :, :split_at].reshape(array_in.shape[1], width_cols, HALF, HEAD_DIM)

    row_grads = attend_back(
        row_heads(attn_queries), row_heads(attn_keys), row_heads(attn_values), row_heads(out_grad)
    )
    row_grads = [grad_one.reshape(1, 1, width_cols, split_at) for grad_one in row_grads]
    grid_rows = column_parts[0].shape[1]
    col_count = column_parts[0].shape[2]

    def col_heads(array_in):
        return jnp.transpose(array_in[0], (1, 0, 2)).reshape(col_count, grid_rows, HALF, HEAD_DIM)

    col_grads = attend_back(
        col_heads(column_parts[0]),
        col_heads(column_parts[1]),
        col_heads(column_parts[2]),
        col_heads(column_parts[3]),
    )
    col_grads = [
        jnp.transpose(grad_one.reshape(col_count, grid_rows, split_at), (1, 0, 2))[None]
        for grad_one in col_grads
    ]
    latent_col = fold_sum(col_grads, fold_maps[:, :, split_at:])
    latent_rows = lax.all_to_all(latent_col, "seq", split_axis=2, concat_axis=3, tiled=True)
    latent = fold_sum(row_grads, fold_maps[:, :, :split_at]) + latent_rows
    halves, shifts, bins_arr = bound_tables()
    pre_wide = pre_act.astype(jnp.float32)
    sigmoid_v = jax.nn.sigmoid(pre_wide)
    act_low = (pre_wide * sigmoid_v).astype(jnp.bfloat16)
    latent_pre = jnp.einsum(
        "iyxj,cj->icyx", act_low, proj_weight, preferred_element_type=jnp.float32
    )
    tanh_val = jnp.tanh(latent_pre + shifts[None, :, None, None])
    slope_fsq = (halves / bins_arr)[None, :, None, None] * (1.0 - tanh_val * tanh_val)
    latent_grad = ((latent + dec_grad) * slope_fsq).astype(jnp.bfloat16)
    proj_term = jnp.einsum(
        "icyx,iyxj->jc", latent_grad, act_low, preferred_element_type=jnp.float32
    )
    act_grad = jnp.einsum(
        "icyx,cj->iyxj", latent_grad, proj_weight, preferred_element_type=jnp.float32
    )
    pre_grad = (act_grad * sigmoid_v * (1.0 + pre_wide * (1.0 - sigmoid_v))).astype(jnp.bfloat16)
    padded = jnp.pad(rim_rows, ((0, 0), (0, 0), (1, 1), (0, 0)))
    windows = jnp.stack(
        [
            padded[0, row_off, col_off : col_off + width_cols]
            for row_off in range(3)
            for col_off in range(3)
        ]
    )
    conv_term = jnp.einsum(
        "kpa,pb->akb", windows, pre_grad[0, 0], preferred_element_type=jnp.float32
    )
    shares = (
        lax.psum_scatter(conv_term, "seq", scatter_dimension=0, tiled=True),
        lax.psum_scatter(proj_term, "seq", scatter_dimension=0, tiled=True),
    )
    conv_out, proj_out = lax.psum((shares[0], shares[1]), "dp")
    return (conv_out, proj_out)


LANES = 128
FLOAT = jnp.float32
HALFWORD = jnp.bfloat16


def dot(lhs, rhs, lhs_dim=1, rhs_dim=0, precision=None):
    return lax.dot_general(
        lhs,
        rhs,
        (((lhs_dim,), (rhs_dim,)), ((), ())),
        precision=precision,
        preferred_element_type=FLOAT,
    )


def iota(shape, axis):
    return lax.broadcasted_iota(jnp.int32, shape, axis)


def attend_tile(queries, keys_in, values_in, grads_in, allowed):
    scaling = 1.0 / math.sqrt(queries.shape[-1])
    scores = jnp.where(allowed, dot(queries, keys_in, 1, 1) * scaling, -jnp.inf)
    exp_scores = jnp.exp(scores - jnp.max(scores, axis=-1, keepdims=True))
    attn_probs = exp_scores / jnp.sum(exp_scores, axis=-1, keepdims=True)
    dprobs = dot(grads_in, values_in, 1, 1)
    rowdot = jnp.sum(attn_probs * dprobs, axis=-1, keepdims=True)
    dscore = (attn_probs * (dprobs - rowdot) * scaling).astype(HALFWORD)
    return (
        dot(dscore, keys_in).astype(HALFWORD),
        dot(dscore, queries, 0, 0).astype(HALFWORD),
        dot(attn_probs.astype(HALFWORD), grads_in, 0, 0).astype(HALFWORD),
    )


def div(value, count):
    if count & (count - 1) == 0:
        return lax.shift_right_logical(value, count.bit_length() - 1)
    return lax.div(value, count)


def rem(value, count):
    if count & (count - 1) == 0:
        return value & (count - 1)
    return lax.rem(value, count)


def lane_places(rows, lanes, start, latents, width):
    lane = iota((rows, lanes), 1)
    inside = lane >= start
    offset = rem(jnp.maximum(lane - start, 0), latents * width)
    return inside, div(offset, width), rem(offset, width)


def local_kernel(
    order,
    query_hbm,
    key_hbm,
    value_hbm,
    grad_hbm,
    fold_hbm,
    dec_hbm,
    conv_hbm,
    pre_hbm,
    proj_hbm,
    packed_ref,
    row_ref,
    slope_ref,
    fold_own_ref,
    conv_out_ref,
    proj_rep_ref,
    pre_out_ref,
    rows_ref,
    fold_ref,
    dec_ref,
    conv_ref,
    pre_ref,
    proj_ref,
    sem,
    pack_sem,
):
    split_at = HALF * HEAD_DIM
    heads = (query_hbm, key_hbm, value_hbm, grad_hbm)
    copies = [
        pltpu.make_async_copy(ref.at[0, 0, :, pl.ds(0, split_at)], rows_ref.at[part], sem)
        for part, ref in enumerate(heads)
    ]
    copies += [
        pltpu.make_async_copy(source, target, sem)
        for source, target in (
            (fold_hbm, fold_ref),
            (dec_hbm, dec_ref),
            (conv_hbm, conv_ref),
            (pre_hbm, pre_ref),
            (proj_hbm, proj_ref),
        )
    ]
    packs = []
    for slot, device in enumerate(order):
        lanes = pl.ds((HALF + device) * HEAD_DIM, HEAD_DIM)
        for part, ref in enumerate(heads):
            packs.append(
                pltpu.make_async_copy(ref.at[0, 0, :, lanes], packed_ref.at[slot, part], pack_sem)
            )
    for copy in copies + packs:
        copy.start()
    for copy in copies:
        copy.wait()
    width = query_hbm.shape[2]
    latents = fold_ref.shape[1]
    devices, _, lanes = conv_out_ref.shape
    span = conv_ref.shape[3] // devices
    mine = lax.axis_index("seq")

    def stacked(part):
        return jnp.concatenate(
            [
                rows_ref[part, :, head * HEAD_DIM : (head + 1) * HEAD_DIM].astype(FLOAT)
                for head in range(HALF)
            ],
            axis=0,
        ).astype(HALFWORD)

    count = HALF * width
    row, col = iota((count, count), 0), iota((count, count), 1)
    allowed = (div(row, width) == div(col, width)) & (col <= row)
    grads = attend_tile(
        stacked(0), stacked(1), stacked(2), stacked(3), allowed
    )
    inside, channel, place = lane_places(width, lanes, span, latents, width)
    lane = iota((lanes, latents), 0)
    spread_at = rem(jnp.maximum(lane - span, 0), latents * width)
    hit = (lane >= span) & (div(spread_at, width) == iota((lanes, latents), 1))
    spread = jnp.where(hit, 1.0, 0.0).astype(HALFWORD)
    once = jnp.where(hit & (lane < span + latents * width), 1.0, 0.0).astype(HALFWORD)
    compact = jnp.zeros((width, latents), FLOAT)
    for part in range(3):
        wide = grads[part].astype(FLOAT)
        wide = jnp.concatenate(
            [wide[head * width : (head + 1) * width] for head in range(HALF)], axis=1
        ).astype(HALFWORD)
        compact = compact + dot(wide, fold_ref[part, :, :split_at], 1, 1)
        own = fold_ref[part, :, pl.ds(pl.multiple_of(split_at + mine * HEAD_DIM, HEAD_DIM), HEAD_DIM)]
        fold_own_ref[part] = dot(spread, own).astype(HALFWORD)
    diagonal = inside & (iota((width, lanes), 0) == place)

    def spread_out(values):
        result = jnp.zeros((width, lanes), FLOAT)
        for index in range(latents):
            result = jnp.where(diagonal & (channel == index), values[:, index : index + 1], result)
        return result

    total = spread_out(compact)
    decoder = dec_ref[0, :, 0, :]
    column = jnp.where(
        iota((width, lanes), 0) == rem(iota((width, lanes), 1), width), 1.0, 0.0
    )
    decoder = dot(decoder, column, precision=lax.Precision.HIGHEST)
    _, owner, _ = lane_places(latents, lanes, span, latents, width)
    keep = (iota((latents, lanes), 1) >= span) & (iota((latents, lanes), 0) == owner)
    vector = jnp.sum(total, axis=0, keepdims=True) + jnp.sum(
        jnp.where(keep, decoder, 0.0), axis=0, keepdims=True
    )
    row_ref[...] = jnp.where(iota((width, lanes), 0) == mine, vector, 0.0)
    proj_rep_ref[...] = dot(once, proj_ref[...]).astype(HALFWORD)
    pre_out_ref[...] = pre_ref[...]
    pre_wide = pre_ref[0, 0].astype(FLOAT)
    act_low = (pre_wide * jax.nn.sigmoid(pre_wide)).astype(HALFWORD)
    latent_pre = spread_out(dot(act_low, proj_ref[...], 1, 1))
    halves = [(levels_one - 1.0) * 1.001 / 2.0 for levels_one in fsq_levels]
    shift = jnp.zeros((width, lanes), FLOAT)
    slope = jnp.zeros((width, lanes), FLOAT)
    for index, (levels_one, bins_one, half_width) in enumerate(zip(fsq_levels, fsq_bins, halves)):
        ratio_one = (0.5 if levels_one % 2.0 == 0.0 else 0.0) / half_width
        shift_one = 0.5 * math.log((1.0 + ratio_one) / (1.0 - ratio_one))
        shift = jnp.where(channel == index, shift_one, shift)
        slope = jnp.where(channel == index, half_width / bins_one, slope)
    tanh_val = jnp.tanh(latent_pre + shift)
    slope = slope * (1.0 - tanh_val * tanh_val)
    slope = jnp.where(diagonal, slope, 0.0)
    vector = jnp.sum(slope, axis=0, keepdims=True)
    slope_ref[...] = jnp.where(iota((width, lanes), 0) == mine, vector, 0.0)
    for device in range(devices):
        first = device * span
        block = conv_ref[0, 0, :, first // lanes * lanes : first // lanes * lanes + lanes].astype(FLOAT)
        if first % lanes:
            block = pltpu.roll(block, lanes - first % lanes, 1)
        conv_out_ref[device] = block
    for copy in packs:
        copy.wait()


def column_kernel(
    seq_order, chip_order, recv_ref, fold_ref, row_ref, slope_ref, conv_ref, pre_ref, out_ref
):
    rows, _, width, _ = recv_ref.shape
    devices, _, lanes = conv_ref.shape
    channels = pre_ref.shape[3]
    span = channels // devices
    half = (lanes - span) // 2
    count = rows * width

    def stacked(part):
        tiles = [recv_ref[seq_order.index(source), part].astype(FLOAT) for source in range(rows)]
        return jnp.concatenate(tiles, axis=0).astype(HALFWORD)

    row, col = iota((count, count), 0), iota((count, count), 1)
    allowed = (rem(row, width) == rem(col, width)) & (col <= row)
    grads = attend_tile(stacked(0), stacked(1), stacked(2), stacked(3), allowed)
    total = dot(grads[0], fold_ref[0], 1, 1)
    total = total + dot(grads[1], fold_ref[1], 1, 1)
    total = total + dot(grads[2], fold_ref[2], 1, 1)
    match = iota((width, lanes), 0) == rem(iota((width, lanes), 1), width)
    total = jnp.where(match[None], total.reshape(rows, width, lanes), 0.0)
    share = jnp.sum(total, axis=1) + row_ref[...]
    lane = iota((rows, lanes), 1)

    def pair(value):
        high = value.astype(HALFWORD).astype(FLOAT)
        return jnp.where(lane < span + half, high, value - high)

    parts = (pair(share), pair(slope_ref[...]))
    pre = pre_ref[0, 0]
    chips = devices // 2
    for chip in range(chips):
        blocks = [
            jnp.where(lane < span, conv_ref[2 * chip + core], parts[core]).astype(HALFWORD)
            for core in range(2)
        ]
        for slot, member in enumerate(chip_order):
            if member % chips == chip:
                out_ref[slot, :, :channels] = pre
                out_ref[slot, :, channels : channels + lanes] = blocks[0]
                out_ref[slot, :, channels + lanes :] = blocks[1]


def final_kernel(
    chip_order, own_ref, other_ref, proj_rep_ref, conv_out_ref, proj_out_ref, stage, held, small, sem
):
    members, width, _ = own_ref.shape
    taps, span, channels = conv_out_ref.shape
    latents = proj_out_ref.shape[0]
    lanes = proj_rep_ref.shape[0]
    devices = channels // span
    chips = devices // 2
    sources = 2 * members
    images = sources // devices
    count = sources * width
    mine = lax.axis_index("seq")
    half = latents * width
    lane = iota((width, lanes), 1)
    match = (lane >= span) & (lane < span + half) & (iota((width, lanes), 0) == rem(lane, width))

    def finish(core):
        def rows(first, size):
            tiles = []
            for source in range(sources):
                image, place = divmod(source, devices)
                ref = own_ref if place % 2 == core else other_ref
                slot = chip_order.index(image * chips + place // 2)
                tiles.append(ref[slot, :, first : first + size].astype(FLOAT))
            return jnp.stack(tiles, axis=0)

        tails = [rows(channels, lanes), rows(channels + lanes, lanes)]
        pick = jnp.where(iota((span, lanes), 0) == iota((span, lanes), 1), 1.0, 0.0)
        inputs = dot(
            pick.astype(HALFWORD), tails[core].reshape(count, lanes).astype(HALFWORD), 1, 1
        )
        position = iota((8, count), 1)
        place_x = rem(position, width)
        place_y = rem(div(position, width), devices)
        for row_off in (-1, 0, 1):
            for col_off in (-1, 0, 1):
                step = row_off * width + col_off
                window = pltpu.roll(inputs, -step % count, 1) if step else inputs
                valid = (
                    (place_x + col_off >= 0)
                    & (place_x + col_off < width)
                    & (place_y + row_off >= 0)
                    & (place_y + row_off < devices)
                )
                window = jnp.where(valid[None], window.reshape(span // 8, 8, count), 0.0)
                tap = 3 * row_off + col_off + 4
                stage[pl.ds(tap * span, span), :] = window.reshape(span, count).astype(HALFWORD)
        proj_rep = proj_rep_ref[...]
        latent, slope = [
            jnp.sum(tail.reshape(images, devices, width, lanes), axis=1).reshape(sources, lanes)
            for tail in tails
        ]
        latent = latent + pltpu.roll(latent, lanes - half, 1)
        slope = slope + pltpu.roll(slope, lanes - half, 1)
        latent_grad = (latent * slope).reshape(sources, 1, lanes)
        wide = jnp.broadcast_to(latent_grad, (sources, width, lanes))
        wide = jnp.where(match[None], wide, 0.0).reshape(count, lanes).astype(HALFWORD)
        act_grad = dot(wide, proj_rep)
        pre_wide = rows(0, channels).reshape(count, channels)
        sigmoid_v = 0.5 + 0.5 * jnp.tanh(0.5 * pre_wide)
        act_wide = pre_wide * sigmoid_v
        act_low = act_wide.astype(HALFWORD)
        silu_grad = sigmoid_v + act_wide * (1.0 - sigmoid_v)
        pre_grad = (act_grad * silu_grad).astype(HALFWORD)
        copies = []
        for part in range(3):
            block = pl.ds(3 * part, 3)
            windows = stage[3 * part * span : 3 * (part + 1) * span, :]
            held[block] = dot(windows, pre_grad).reshape(3, span, channels)
            copies.append(
                pltpu.make_async_copy(held.at[block], conv_out_ref.at[block], sem.at[part])
            )
            copies[-1].start()
        proj_term = dot(wide, act_low, 0, 0)[span : span + half]
        proj_term = jnp.sum(proj_term.reshape(latents, width, channels), axis=1)
        turn = rem(channels - mine * span, channels)
        small[...] = pltpu.roll(proj_term, turn, 1)[:, :span]
        copies.append(pltpu.make_async_copy(small, proj_out_ref, sem.at[3]))
        copies[-1].start()
        for copy in copies:
            copy.wait()

    for core in range(2):
        pl.when(rem(mine, 2) == core)(functools.partial(finish, core))


def call(kernel, outs, inputs, in_specs=None, flops=1 << 22):
    whole = pl.BlockSpec(memory_space=pltpu.VMEM)
    nbytes = sum(math.prod(one.shape) * one.dtype.itemsize for one in (*inputs, *outs))
    return pl.pallas_call(
        kernel,
        grid=(1,),
        out_shape=outs,
        in_specs=in_specs or [whole] * len(inputs),
        out_specs=[whole] * len(outs),
        compiler_params=pltpu.CompilerParams(vmem_limit_bytes=16 << 20),
        cost_estimate=pl.CostEstimate(flops=flops, bytes_accessed=nbytes, transcendentals=0),
    )(*inputs)


def gather_plan(
    attn_queries,
    attn_keys,
    attn_values,
    out_grad,
    fold_maps,
    dec_grad,
    conv_input,
    pre_act,
    proj_weight,
):
    devices, images = lax.axis_size("seq"), lax.axis_size("dp")
    width, channels, latents = pre_act.shape[2], pre_act.shape[3], proj_weight.shape[0]
    span = channels // devices
    split_at = HALF * HEAD_DIM
    heads = (attn_queries, attn_keys, attn_values, out_grad)
    struct = jax.ShapeDtypeStruct
    members = images * devices
    chips = devices // 2
    seq_order = [(devices // 2 + 1 - slot) % devices for slot in range(devices)]
    chip_order = [(members // 2 - 1 - 3 * slot) % (members // 2) for slot in range(members // 2)]
    core_groups = [
        [member // chips * devices + member % chips * 2 + core for member in chip_order]
        for core in range(2)
    ]
    columns = [pl.BlockSpec((1, 1, width, split_at), lambda step: (0, 0, 0, 1))] * 4
    whole = pl.BlockSpec(memory_space=pltpu.VMEM)
    inputs = (*heads, fold_maps, dec_grad, conv_input, pre_act, proj_weight)
    packed, row_share, slopes, fold_own, conv_blocks, proj_rep, pre_near = pl.pallas_call(
        functools.partial(local_kernel, seq_order),
        out_shape=[
            struct((devices, 4, width, HEAD_DIM), HALFWORD),
            struct((width, LANES), FLOAT),
            struct((width, LANES), FLOAT),
            struct((3, LANES, HEAD_DIM), HALFWORD),
            struct((devices, width, LANES), FLOAT),
            struct((LANES, channels), HALFWORD),
            struct(pre_act.shape, HALFWORD),
        ],
        in_specs=[pl.BlockSpec(memory_space=pltpu.HBM)] * len(inputs),
        out_specs=[whole] * 7,
        scratch_shapes=[pltpu.VMEM((4, width, split_at), HALFWORD)]
        + [pltpu.VMEM(one.shape, one.dtype) for one in inputs[4:]]
        + [pltpu.SemaphoreType.DMA, pltpu.SemaphoreType.DMA],
        compiler_params=pltpu.CompilerParams(vmem_limit_bytes=16 << 20),
    )(*[pltpu.with_memory_space_constraint(one, pltpu.HBM) for one in inputs])
    column = lax.all_to_all(packed, "seq", split_axis=0, concat_axis=0, axis_index_groups=[seq_order], tiled=True)
    (shared,) = call(
        functools.partial(column_kernel, seq_order, chip_order),
        [struct((members // 2, width, channels + 2 * LANES), HALFWORD)],
        (column, fold_own, row_share, slopes, conv_blocks, pre_near),
    )
    spread = lax.all_to_all(
        shared,
        ("dp", "seq"),
        split_axis=0,
        concat_axis=0,
        axis_index_groups=core_groups,
        tiled=True,
    )
    partner = lax.ppermute(spread, "seq", [(one, one ^ 1) for one in range(devices)])
    outs = [struct((9, span, channels), FLOAT), struct((latents, span), FLOAT)]
    conv_out, proj_out = pl.pallas_call(
        functools.partial(final_kernel, chip_order),
        out_shape=outs,
        in_specs=[whole] * 3,
        out_specs=[pl.BlockSpec(memory_space=pltpu.HBM)] * 2,
        scratch_shapes=[pltpu.VMEM((9 * span, images * devices * width), HALFWORD)]
        + [pltpu.VMEM(one.shape, one.dtype) for one in outs]
        + [pltpu.SemaphoreType.DMA((4,))],
        compiler_params=pltpu.CompilerParams(vmem_limit_bytes=16 << 20),
    )(spread, partner, proj_rep)
    return (jnp.transpose(conv_out, (1, 0, 2)), jnp.transpose(proj_out, (1, 0)))


def on_device(*arrays):
    queries, conv_input, proj_weight = arrays[0], arrays[6], arrays[8]
    devices, images = lax.axis_size("seq"), lax.axis_size("dp")
    rows, width, channels = conv_input.shape[1:]
    latents = proj_weight.shape[0]
    heads = queries.shape[3] // HEAD_DIM - HALF
    positions = images * devices * rows * width
    fits = (
        (conv_input.shape[0], rows, width, heads) == (1, 1, devices, devices)
        and channels // devices % 8 == 0
        and (HALF * 2, width, images * devices % 8) == (queries.shape[3] // HEAD_DIM, 8, 0)
        and devices % 2 == 0
        and math.gcd(3, images * devices // 2) == 1
        and channels // devices + 2 * latents * width == LANES
    )
    if fits and positions * channels * 2 <= 9 * channels * channels * 4:
        return gather_plan(*arrays)
    return reduce_plan(*arrays)


def solution(mesh):
    return jax.shard_map(
        on_device,
        mesh=mesh,
        in_specs=(
            P("dp", "seq", None, None),
            P("dp", "seq", None, None),
            P("dp", "seq", None, None),
            P("dp", "seq", None, None),
            P(),
            P("dp", None, "seq", None),
            P("dp", "seq", None, None),
            P("dp", "seq", None, None),
            P(),
        ),
        out_specs=(P("seq", None, None), P("seq", None)),
        check_vma=False,
    )
```

```python
import functools
import math

import jax
import jax.numpy as jnp
from jax import lax
from jax.experimental import pallas as pl
from jax.experimental.pallas import tpu as pltpu
from jax.sharding import PartitionSpec as P

HEAD_DIM = 128
HALF = 8


fsq_levels = (8.0, 8.0, 8.0, 5.0, 5.0, 5.0)
fsq_bins = (4.0, 4.0, 4.0, 2.0, 2.0, 2.0)


def padded_2(block, sides, width):
    for axis, dim in sides:
        count = lax.axis_size(axis)
        forward = [(i, i + 1) for i in range(count - 1)]
        backward = [(target, source) for source, target in forward]
        low = lax.ppermute(
            lax.slice_in_dim(block, block.shape[dim] - width, None, axis=dim), axis, forward
        )
        high = lax.ppermute(lax.slice_in_dim(block, 0, width, axis=dim), axis, backward)
        block = jnp.concatenate([low, block, high], axis=dim)
    return block


def bound_tables():
    halves = [(levels_one - 1.0) * 1.001 / 2.0 for levels_one in fsq_levels]
    shifts = []
    for levels_one, half_width in zip(fsq_levels, halves):
        offset_one = 0.5 if levels_one % 2.0 == 0.0 else 0.0
        ratio_one = offset_one / half_width
        shifts.append(0.5 * math.log((1.0 + ratio_one) / (1.0 - ratio_one)))
    return (
        jnp.array(halves, jnp.float32),
        jnp.array(shifts, jnp.float32),
        jnp.array(fsq_bins, jnp.float32),
    )


def attend_back(queries, keys_in, values_in, grads_in):
    scaling = 1.0 / math.sqrt(queries.shape[-1])
    length = queries.shape[1]
    scores = (
        jnp.einsum("blhd,bmhd->bhlm", queries, keys_in, preferred_element_type=jnp.float32)
        * scaling
    )
    causal = jnp.arange(length)[:, None] >= jnp.arange(length)[None, :]
    scores = jnp.where(causal, scores, -jnp.inf)
    exp_scores = jnp.exp(scores - jnp.max(scores, axis=-1, keepdims=True))
    attn_probs = exp_scores / jnp.sum(exp_scores, axis=-1, keepdims=True)
    probs_low = attn_probs.astype(jnp.bfloat16)
    dprobs = jnp.einsum("blhd,bmhd->bhlm", grads_in, values_in, preferred_element_type=jnp.float32)
    rowdot = jnp.sum(attn_probs * dprobs, axis=-1, keepdims=True)
    dscore = (attn_probs * (dprobs - rowdot) * scaling).astype(jnp.bfloat16)
    grad_query = jnp.einsum(
        "bhlm,bmhd->blhd", dscore, keys_in, preferred_element_type=jnp.float32
    ).astype(jnp.bfloat16)
    grad_key = jnp.einsum(
        "bhlm,blhd->bmhd", dscore, queries, preferred_element_type=jnp.float32
    ).astype(jnp.bfloat16)
    grad_value = jnp.einsum(
        "bhlm,blhd->bmhd", probs_low, grads_in, preferred_element_type=jnp.float32
    ).astype(jnp.bfloat16)
    return (grad_query, grad_key, grad_value)


def fold_sum(grads, maps):
    total = jnp.einsum("cw,iyxw->icyx", maps[0], grads[0], preferred_element_type=jnp.float32)
    total = total + jnp.einsum(
        "cw,iyxw->icyx", maps[1], grads[1], preferred_element_type=jnp.float32
    )
    return total + jnp.einsum(
        "cw,iyxw->icyx", maps[2], grads[2], preferred_element_type=jnp.float32
    )


def reduce_plan(
    attn_queries,
    attn_keys,
    attn_values,
    out_grad,
    fold_maps,
    dec_grad,
    conv_input,
    pre_act,
    proj_weight,
):
    split_at = HALF * HEAD_DIM
    width_cols = attn_queries.shape[2]
    rim_rows = padded_2(conv_input, (("seq", 1),), 1)
    column_parts = (
        lax.all_to_all(
            attn_queries[..., split_at:], "seq", split_axis=2, concat_axis=1, tiled=True
        ),
        lax.all_to_all(attn_keys[..., split_at:], "seq", split_axis=2, concat_axis=1, tiled=True),
        lax.all_to_all(attn_values[..., split_at:], "seq", split_axis=2, concat_axis=1, tiled=True),
        lax.all_to_all(out_grad[..., split_at:], "seq", split_axis=2, concat_axis=1, tiled=True),
    )

    def row_heads(array_in):
        return array_in[0, :, :, :split_at].reshape(array_in.shape[1], width_cols, HALF, HEAD_DIM)

    row_grads = attend_back(
        row_heads(attn_queries), row_heads(attn_keys), row_heads(attn_values), row_heads(out_grad)
    )
    row_grads = [grad_one.reshape(1, 1, width_cols, split_at) for grad_one in row_grads]
    grid_rows = column_parts[0].shape[1]
    col_count = column_parts[0].shape[2]

    def col_heads(array_in):
        return jnp.transpose(array_in[0], (1, 0, 2)).reshape(col_count, grid_rows, HALF, HEAD_DIM)

    col_grads = attend_back(
        col_heads(column_parts[0]),
        col_heads(column_parts[1]),
        col_heads(column_parts[2]),
        col_heads(column_parts[3]),
    )
    col_grads = [
        jnp.transpose(grad_one.reshape(col_count, grid_rows, split_at), (1, 0, 2))[None]
        for grad_one in col_grads
    ]
    latent_col = fold_sum(col_grads, fold_maps[:, :, split_at:])
    latent_rows = lax.all_to_all(latent_col, "seq", split_axis=2, concat_axis=3, tiled=True)
    latent = fold_sum(row_grads, fold_maps[:, :, :split_at]) + latent_rows
    halves, shifts, bins_arr = bound_tables()
    pre_wide = pre_act.astype(jnp.float32)
    sigmoid_v = jax.nn.sigmoid(pre_wide)
    act_low = (pre_wide * sigmoid_v).astype(jnp.bfloat16)
    latent_pre = jnp.einsum(
        "iyxj,cj->icyx", act_low, proj_weight, preferred_element_type=jnp.float32
    )
    tanh_val = jnp.tanh(latent_pre + shifts[None, :, None, None])
    slope_fsq = (halves / bins_arr)[None, :, None, None] * (1.0 - tanh_val * tanh_val)
    latent_grad = ((latent + dec_grad) * slope_fsq).astype(jnp.bfloat16)
    proj_term = jnp.einsum(
        "icyx,iyxj->jc", latent_grad, act_low, preferred_element_type=jnp.float32
    )
    act_grad = jnp.einsum(
        "icyx,cj->iyxj", latent_grad, proj_weight, preferred_element_type=jnp.float32
    )
    pre_grad = (act_grad * sigmoid_v * (1.0 + pre_wide * (1.0 - sigmoid_v))).astype(jnp.bfloat16)
    padded = jnp.pad(rim_rows, ((0, 0), (0, 0), (1, 1), (0, 0)))
    windows = jnp.stack(
        [
            padded[0, row_off, col_off : col_off + width_cols]
            for row_off in range(3)
            for col_off in range(3)
        ]
    )
    conv_term = jnp.einsum(
        "kpa,pb->akb", windows, pre_grad[0, 0], preferred_element_type=jnp.float32
    )
    shares = (
        lax.psum_scatter(conv_term, "seq", scatter_dimension=0, tiled=True),
        lax.psum_scatter(proj_term, "seq", scatter_dimension=0, tiled=True),
    )
    conv_out, proj_out = lax.psum((shares[0], shares[1]), "dp")
    return (conv_out, proj_out)


LANES = 128
FLOAT = jnp.float32
HALFWORD = jnp.bfloat16


def dot(lhs, rhs, lhs_dim=1, rhs_dim=0, precision=None):
    return lax.dot_general(
        lhs,
        rhs,
        (((lhs_dim,), (rhs_dim,)), ((), ())),
        precision=precision,
        preferred_element_type=FLOAT,
    )


def iota(shape, axis):
    return lax.broadcasted_iota(jnp.int32, shape, axis)


def attend_tile(queries, keys_in, values_in, grads_in, allowed):
    scaling = 1.0 / math.sqrt(queries.shape[-1])
    scores = jnp.where(allowed, dot(queries, keys_in, 1, 1) * scaling, -jnp.inf)
    exp_scores = jnp.exp(scores - jnp.max(scores, axis=-1, keepdims=True))
    attn_probs = exp_scores / jnp.sum(exp_scores, axis=-1, keepdims=True)
    dprobs = dot(grads_in, values_in, 1, 1)
    rowdot = jnp.sum(attn_probs * dprobs, axis=-1, keepdims=True)
    dscore = (attn_probs * (dprobs - rowdot) * scaling).astype(HALFWORD)
    return (
        dot(dscore, keys_in).astype(HALFWORD),
        dot(dscore, queries, 0, 0).astype(HALFWORD),
        dot(attn_probs.astype(HALFWORD), grads_in, 0, 0).astype(HALFWORD),
    )


def div(value, count):
    if count & (count - 1) == 0:
        return lax.shift_right_logical(value, count.bit_length() - 1)
    return lax.div(value, count)


def rem(value, count):
    if count & (count - 1) == 0:
        return value & (count - 1)
    return lax.rem(value, count)


def lane_places(rows, lanes, start, latents, width):
    lane = iota((rows, lanes), 1)
    inside = lane >= start
    offset = rem(jnp.maximum(lane - start, 0), latents * width)
    return inside, div(offset, width), rem(offset, width)


def local_kernel(
    order,
    query_hbm,
    key_hbm,
    value_hbm,
    grad_hbm,
    fold_hbm,
    dec_hbm,
    conv_hbm,
    pre_hbm,
    proj_hbm,
    packed_ref,
    row_ref,
    slope_ref,
    fold_own_ref,
    conv_out_ref,
    proj_rep_ref,
    pre_out_ref,
    rows_ref,
    fold_ref,
    dec_ref,
    conv_ref,
    pre_ref,
    proj_ref,
    sem,
    rest_sem,
    pack_sem,
):
    split_at = HALF * HEAD_DIM
    heads = (query_hbm, key_hbm, value_hbm, grad_hbm)
    copies = [
        pltpu.make_async_copy(ref.at[0, 0, :, pl.ds(0, split_at)], rows_ref.at[part], sem)
        for part, ref in enumerate(heads)
    ]
    copies += [
        pltpu.make_async_copy(source, target, rest_sem)
        for source, target in (
            (fold_hbm, fold_ref),
            (dec_hbm, dec_ref),
            (conv_hbm, conv_ref),
            (pre_hbm, pre_ref),
            (proj_hbm, proj_ref),
        )
    ]
    packs = []
    for slot, device in enumerate(order):
        lanes = pl.ds((HALF + device) * HEAD_DIM, HEAD_DIM)
        for part, ref in enumerate(heads):
            packs.append(
                pltpu.make_async_copy(ref.at[0, 0, :, lanes], packed_ref.at[slot, part], pack_sem)
            )
    for copy in copies + packs:
        copy.start()
    for copy in copies[: len(heads)]:
        copy.wait()
    width = query_hbm.shape[2]
    latents = fold_ref.shape[1]
    devices, _, lanes = conv_out_ref.shape
    span = conv_ref.shape[3] // devices
    mine = lax.axis_index("seq")

    def stacked(part):
        return jnp.concatenate(
            [
                rows_ref[part, :, head * HEAD_DIM : (head + 1) * HEAD_DIM].astype(FLOAT)
                for head in range(HALF)
            ],
            axis=0,
        ).astype(HALFWORD)

    count = HALF * width
    row, col = iota((count, count), 0), iota((count, count), 1)
    allowed = (div(row, width) == div(col, width)) & (col <= row)
    grads = attend_tile(
        stacked(0), stacked(1), stacked(2), stacked(3), allowed
    )
    for copy in copies[len(heads) :]:
        copy.wait()
    inside, channel, place = lane_places(width, lanes, span, latents, width)
    lane = iota((lanes, latents), 0)
    spread_at = rem(jnp.maximum(lane - span, 0), latents * width)
    hit = (lane >= span) & (div(spread_at, width) == iota((lanes, latents), 1))
    spread = jnp.where(hit, 1.0, 0.0).astype(HALFWORD)
    once = jnp.where(hit & (lane < span + latents * width), 1.0, 0.0).astype(HALFWORD)
    compact = jnp.zeros((width, latents), FLOAT)
    for part in range(3):
        wide = grads[part].astype(FLOAT)
        wide = jnp.concatenate(
            [wide[head * width : (head + 1) * width] for head in range(HALF)], axis=1
        ).astype(HALFWORD)
        compact = compact + dot(wide, fold_ref[part, :, :split_at], 1, 1)
        own = fold_ref[part, :, pl.ds(pl.multiple_of(split_at + mine * HEAD_DIM, HEAD_DIM), HEAD_DIM)]
        fold_own_ref[part] = dot(spread, own).astype(HALFWORD)
    diagonal = inside & (iota((width, lanes), 0) == place)

    def spread_out(values):
        result = jnp.zeros((width, lanes), FLOAT)
        for index in range(latents):
            result = jnp.where(diagonal & (channel == index), values[:, index : index + 1], result)
        return result

    total = spread_out(compact)
    decoder = dec_ref[0, :, 0, :]
    column = jnp.where(
        iota((width, lanes), 0) == rem(iota((width, lanes), 1), width), 1.0, 0.0
    )
    decoder = dot(decoder, column, precision=lax.Precision.HIGHEST)
    _, owner, _ = lane_places(latents, lanes, span, latents, width)
    keep = (iota((latents, lanes), 1) >= span) & (iota((latents, lanes), 0) == owner)
    vector = jnp.sum(total, axis=0, keepdims=True) + jnp.sum(
        jnp.where(keep, decoder, 0.0), axis=0, keepdims=True
    )
    row_ref[...] = jnp.where(iota((width, lanes), 0) == mine, vector, 0.0)
    proj_rep_ref[...] = dot(once, proj_ref[...]).astype(HALFWORD)
    pre_out_ref[...] = pre_ref[...]
    pre_wide = pre_ref[0, 0].astype(FLOAT)
    act_low = (pre_wide * jax.nn.sigmoid(pre_wide)).astype(HALFWORD)
    latent_pre = spread_out(dot(act_low, proj_ref[...], 1, 1))
    halves = [(levels_one - 1.0) * 1.001 / 2.0 for levels_one in fsq_levels]
    shift = jnp.zeros((width, lanes), FLOAT)
    slope = jnp.zeros((width, lanes), FLOAT)
    for index, (levels_one, bins_one, half_width) in enumerate(zip(fsq_levels, fsq_bins, halves)):
        ratio_one = (0.5 if levels_one % 2.0 == 0.0 else 0.0) / half_width
        shift_one = 0.5 * math.log((1.0 + ratio_one) / (1.0 - ratio_one))
        shift = jnp.where(channel == index, shift_one, shift)
        slope = jnp.where(channel == index, half_width / bins_one, slope)
    tanh_val = jnp.tanh(latent_pre + shift)
    slope = slope * (1.0 - tanh_val * tanh_val)
    slope = jnp.where(diagonal, slope, 0.0)
    vector = jnp.sum(slope, axis=0, keepdims=True)
    slope_ref[...] = jnp.where(iota((width, lanes), 0) == mine, vector, 0.0)
    for device in range(devices):
        first = device * span
        block = conv_ref[0, 0, :, first // lanes * lanes : first // lanes * lanes + lanes].astype(FLOAT)
        if first % lanes:
            block = pltpu.roll(block, lanes - first % lanes, 1)
        conv_out_ref[device] = block
    for copy in packs:
        copy.wait()


def column_kernel(
    seq_order, chip_order, recv_ref, fold_ref, row_ref, slope_ref, conv_ref, pre_ref, out_ref
):
    rows, _, width, _ = recv_ref.shape
    devices, _, lanes = conv_ref.shape
    channels = pre_ref.shape[3]
    span = channels // devices
    half = (lanes - span) // 2
    count = rows * width

    def stacked(part):
        tiles = [recv_ref[seq_order.index(source), part].astype(FLOAT) for source in range(rows)]
        return jnp.concatenate(tiles, axis=0).astype(HALFWORD)

    row, col = iota((count, count), 0), iota((count, count), 1)
    allowed = (rem(row, width) == rem(col, width)) & (col <= row)
    grads = attend_tile(stacked(0), stacked(1), stacked(2), stacked(3), allowed)
    total = dot(grads[0], fold_ref[0], 1, 1)
    total = total + dot(grads[1], fold_ref[1], 1, 1)
    total = total + dot(grads[2], fold_ref[2], 1, 1)
    match = iota((width, lanes), 0) == rem(iota((width, lanes), 1), width)
    total = jnp.where(match[None], total.reshape(rows, width, lanes), 0.0)
    share = jnp.sum(total, axis=1) + row_ref[...]
    lane = iota((rows, lanes), 1)

    def pair(value):
        high = value.astype(HALFWORD).astype(FLOAT)
        return jnp.where(lane < span + half, high, value - high)

    parts = (pair(share), pair(slope_ref[...]))
    pre = pre_ref[0, 0]
    chips = devices // 2
    for chip in range(chips):
        blocks = [
            jnp.where(lane < span, conv_ref[2 * chip + core], parts[core]).astype(HALFWORD)
            for core in range(2)
        ]
        for slot, member in enumerate(chip_order):
            if member % chips == chip:
                out_ref[slot, :, :channels] = pre
                out_ref[slot, :, channels : channels + lanes] = blocks[0]
                out_ref[slot, :, channels + lanes :] = blocks[1]


def final_kernel(
    chip_order, own_ref, other_ref, proj_rep_ref, conv_out_ref, proj_out_ref, stage, held, small, sem
):
    members, width, _ = own_ref.shape
    taps, span, channels = conv_out_ref.shape
    latents = proj_out_ref.shape[0]
    lanes = proj_rep_ref.shape[0]
    devices = channels // span
    chips = devices // 2
    sources = 2 * members
    images = sources // devices
    count = sources * width
    mine = lax.axis_index("seq")
    half = latents * width
    lane = iota((width, lanes), 1)
    match = (lane >= span) & (lane < span + half) & (iota((width, lanes), 0) == rem(lane, width))

    def finish(core):
        def rows(first, size):
            tiles = []
            for source in range(sources):
                image, place = divmod(source, devices)
                ref = own_ref if place % 2 == core else other_ref
                slot = chip_order.index(image * chips + place // 2)
                tiles.append(ref[slot, :, first : first + size].astype(FLOAT))
            return jnp.stack(tiles, axis=0)

        tails = [rows(channels, lanes), rows(channels + lanes, lanes)]
        pick = jnp.where(iota((span, lanes), 0) == iota((span, lanes), 1), 1.0, 0.0)
        inputs = dot(
            pick.astype(HALFWORD), tails[core].reshape(count, lanes).astype(HALFWORD), 1, 1
        )
        position = iota((8, count), 1)
        place_x = rem(position, width)
        place_y = rem(div(position, width), devices)
        for row_off in (-1, 0, 1):
            for col_off in (-1, 0, 1):
                step = row_off * width + col_off
                window = pltpu.roll(inputs, -step % count, 1) if step else inputs
                valid = (
                    (place_x + col_off >= 0)
                    & (place_x + col_off < width)
                    & (place_y + row_off >= 0)
                    & (place_y + row_off < devices)
                )
                window = jnp.where(valid[None], window.reshape(span // 8, 8, count), 0.0)
                tap = 3 * row_off + col_off + 4
                stage[pl.ds(tap * span, span), :] = window.reshape(span, count).astype(HALFWORD)
        proj_rep = proj_rep_ref[...]
        latent, slope = [
            jnp.sum(tail.reshape(images, devices, width, lanes), axis=1).reshape(sources, lanes)
            for tail in tails
        ]
        latent = latent + pltpu.roll(latent, lanes - half, 1)
        slope = slope + pltpu.roll(slope, lanes - half, 1)
        latent_grad = (latent * slope).reshape(sources, 1, lanes)
        wide = jnp.broadcast_to(latent_grad, (sources, width, lanes))
        wide = jnp.where(match[None], wide, 0.0).reshape(count, lanes).astype(HALFWORD)
        act_grad = dot(wide, proj_rep)
        pre_wide = rows(0, channels).reshape(count, channels)
        sigmoid_v = 0.5 + 0.5 * jnp.tanh(0.5 * pre_wide)
        act_wide = pre_wide * sigmoid_v
        act_low = act_wide.astype(HALFWORD)
        silu_grad = sigmoid_v + act_wide * (1.0 - sigmoid_v)
        pre_grad = (act_grad * silu_grad).astype(HALFWORD)
        copies = []
        for part in range(3):
            block = pl.ds(3 * part, 3)
            windows = stage[3 * part * span : 3 * (part + 1) * span, :]
            held[block] = dot(windows, pre_grad).reshape(3, span, channels)
            copies.append(
                pltpu.make_async_copy(held.at[block], conv_out_ref.at[block], sem.at[part])
            )
            copies[-1].start()
        proj_term = dot(wide, act_low, 0, 0)[span : span + half]
        proj_term = jnp.sum(proj_term.reshape(latents, width, channels), axis=1)
        turn = rem(channels - mine * span, channels)
        small[...] = pltpu.roll(proj_term, turn, 1)[:, :span]
        copies.append(pltpu.make_async_copy(small, proj_out_ref, sem.at[3]))
        copies[-1].start()
        for copy in copies:
            copy.wait()

    for core in range(2):
        pl.when(rem(mine, 2) == core)(functools.partial(finish, core))


def call(kernel, outs, inputs, in_specs=None, flops=1 << 22):
    whole = pl.BlockSpec(memory_space=pltpu.VMEM)
    nbytes = sum(math.prod(one.shape) * one.dtype.itemsize for one in (*inputs, *outs))
    return pl.pallas_call(
        kernel,
        grid=(1,),
        out_shape=outs,
        in_specs=in_specs or [whole] * len(inputs),
        out_specs=[whole] * len(outs),
        compiler_params=pltpu.CompilerParams(vmem_limit_bytes=16 << 20),
        cost_estimate=pl.CostEstimate(flops=flops, bytes_accessed=nbytes, transcendentals=0),
    )(*inputs)


def gather_plan(
    attn_queries,
    attn_keys,
    attn_values,
    out_grad,
    fold_maps,
    dec_grad,
    conv_input,
    pre_act,
    proj_weight,
):
    devices, images = lax.axis_size("seq"), lax.axis_size("dp")
    width, channels, latents = pre_act.shape[2], pre_act.shape[3], proj_weight.shape[0]
    span = channels // devices
    split_at = HALF * HEAD_DIM
    heads = (attn_queries, attn_keys, attn_values, out_grad)
    struct = jax.ShapeDtypeStruct
    members = images * devices
    chips = devices // 2
    seq_order = [(devices // 2 + 1 - slot) % devices for slot in range(devices)]
    chip_order = [(members // 2 - 1 - 3 * slot) % (members // 2) for slot in range(members // 2)]
    core_groups = [
        [member // chips * devices + member % chips * 2 + core for member in chip_order]
        for core in range(2)
    ]
    columns = [pl.BlockSpec((1, 1, width, split_at), lambda step: (0, 0, 0, 1))] * 4
    whole = pl.BlockSpec(memory_space=pltpu.VMEM)
    inputs = (*heads, fold_maps, dec_grad, conv_input, pre_act, proj_weight)
    packed, row_share, slopes, fold_own, conv_blocks, proj_rep, pre_near = pl.pallas_call(
        functools.partial(local_kernel, seq_order),
        out_shape=[
            struct((devices, 4, width, HEAD_DIM), HALFWORD),
            struct((width, LANES), FLOAT),
            struct((width, LANES), FLOAT),
            struct((3, LANES, HEAD_DIM), HALFWORD),
            struct((devices, width, LANES), FLOAT),
            struct((LANES, channels), HALFWORD),
            struct(pre_act.shape, HALFWORD),
        ],
        in_specs=[pl.BlockSpec(memory_space=pltpu.HBM)] * len(inputs),
        out_specs=[whole] * 7,
        scratch_shapes=[pltpu.VMEM((4, width, split_at), HALFWORD)]
        + [pltpu.VMEM(one.shape, one.dtype) for one in inputs[4:]]
        + [pltpu.SemaphoreType.DMA] * 3,
        compiler_params=pltpu.CompilerParams(vmem_limit_bytes=16 << 20),
    )(*[pltpu.with_memory_space_constraint(one, pltpu.HBM) for one in inputs])
    column = lax.all_to_all(packed, "seq", split_axis=0, concat_axis=0, axis_index_groups=[seq_order], tiled=True)
    (shared,) = call(
        functools.partial(column_kernel, seq_order, chip_order),
        [struct((members // 2, width, channels + 2 * LANES), HALFWORD)],
        (column, fold_own, row_share, slopes, conv_blocks, pre_near),
    )
    spread = lax.all_to_all(
        shared,
        ("dp", "seq"),
        split_axis=0,
        concat_axis=0,
        axis_index_groups=core_groups,
        tiled=True,
    )
    partner = lax.ppermute(spread, "seq", [(one, one ^ 1) for one in range(devices)])
    outs = [struct((9, span, channels), FLOAT), struct((latents, span), FLOAT)]
    conv_out, proj_out = pl.pallas_call(
        functools.partial(final_kernel, chip_order),
        out_shape=outs,
        in_specs=[whole] * 3,
        out_specs=[pl.BlockSpec(memory_space=pltpu.HBM)] * 2,
        scratch_shapes=[pltpu.VMEM((9 * span, images * devices * width), HALFWORD)]
        + [pltpu.VMEM(one.shape, one.dtype) for one in outs]
        + [pltpu.SemaphoreType.DMA((4,))],
        compiler_params=pltpu.CompilerParams(vmem_limit_bytes=16 << 20),
    )(spread, partner, proj_rep)
    return (jnp.transpose(conv_out, (1, 0, 2)), jnp.transpose(proj_out, (1, 0)))


def on_device(*arrays):
    queries, conv_input, proj_weight = arrays[0], arrays[6], arrays[8]
    devices, images = lax.axis_size("seq"), lax.axis_size("dp")
    rows, width, channels = conv_input.shape[1:]
    latents = proj_weight.shape[0]
    heads = queries.shape[3] // HEAD_DIM - HALF
    positions = images * devices * rows * width
    fits = (
        (conv_input.shape[0], rows, width, heads) == (1, 1, devices, devices)
        and channels // devices % 8 == 0
        and (HALF * 2, width, images * devices % 8) == (queries.shape[3] // HEAD_DIM, 8, 0)
        and devices % 2 == 0
        and math.gcd(3, images * devices // 2) == 1
        and channels // devices + 2 * latents * width == LANES
    )
    if fits and positions * channels * 2 <= 9 * channels * channels * 4:
        return gather_plan(*arrays)
    return reduce_plan(*arrays)


def solution(mesh):
    return jax.shard_map(
        on_device,
        mesh=mesh,
        in_specs=(
            P("dp", "seq", None, None),
            P("dp", "seq", None, None),
            P("dp", "seq", None, None),
            P("dp", "seq", None, None),
            P(),
            P("dp", None, "seq", None),
            P("dp", "seq", None, None),
            P("dp", "seq", None, None),
            P(),
        ),
        out_specs=(P("seq", None, None), P("seq", None)),
        check_vma=False,
    )
```

```python
import functools
import math

import jax
import jax.numpy as jnp
from jax import lax
from jax.experimental import pallas as pl
from jax.experimental.pallas import tpu as pltpu
from jax.sharding import PartitionSpec as P

HEAD_DIM = 128
HALF = 8


fsq_levels = (8.0, 8.0, 8.0, 5.0, 5.0, 5.0)
fsq_bins = (4.0, 4.0, 4.0, 2.0, 2.0, 2.0)


def padded_2(block, sides, width):
    for axis, dim in sides:
        count = lax.axis_size(axis)
        forward = [(i, i + 1) for i in range(count - 1)]
        backward = [(target, source) for source, target in forward]
        low = lax.ppermute(
            lax.slice_in_dim(block, block.shape[dim] - width, None, axis=dim), axis, forward
        )
        high = lax.ppermute(lax.slice_in_dim(block, 0, width, axis=dim), axis, backward)
        block = jnp.concatenate([low, block, high], axis=dim)
    return block


def bound_tables():
    halves = [(levels_one - 1.0) * 1.001 / 2.0 for levels_one in fsq_levels]
    shifts = []
    for levels_one, half_width in zip(fsq_levels, halves):
        offset_one = 0.5 if levels_one % 2.0 == 0.0 else 0.0
        ratio_one = offset_one / half_width
        shifts.append(0.5 * math.log((1.0 + ratio_one) / (1.0 - ratio_one)))
    return (
        jnp.array(halves, jnp.float32),
        jnp.array(shifts, jnp.float32),
        jnp.array(fsq_bins, jnp.float32),
    )


def attend_back(queries, keys_in, values_in, grads_in):
    scaling = 1.0 / math.sqrt(queries.shape[-1])
    length = queries.shape[1]
    scores = (
        jnp.einsum("blhd,bmhd->bhlm", queries, keys_in, preferred_element_type=jnp.float32)
        * scaling
    )
    causal = jnp.arange(length)[:, None] >= jnp.arange(length)[None, :]
    scores = jnp.where(causal, scores, -jnp.inf)
    exp_scores = jnp.exp(scores - jnp.max(scores, axis=-1, keepdims=True))
    attn_probs = exp_scores / jnp.sum(exp_scores, axis=-1, keepdims=True)
    probs_low = attn_probs.astype(jnp.bfloat16)
    dprobs = jnp.einsum("blhd,bmhd->bhlm", grads_in, values_in, preferred_element_type=jnp.float32)
    rowdot = jnp.sum(attn_probs * dprobs, axis=-1, keepdims=True)
    dscore = (attn_probs * (dprobs - rowdot) * scaling).astype(jnp.bfloat16)
    grad_query = jnp.einsum(
        "bhlm,bmhd->blhd", dscore, keys_in, preferred_element_type=jnp.float32
    ).astype(jnp.bfloat16)
    grad_key = jnp.einsum(
        "bhlm,blhd->bmhd", dscore, queries, preferred_element_type=jnp.float32
    ).astype(jnp.bfloat16)
    grad_value = jnp.einsum(
        "bhlm,blhd->bmhd", probs_low, grads_in, preferred_element_type=jnp.float32
    ).astype(jnp.bfloat16)
    return (grad_query, grad_key, grad_value)


def fold_sum(grads, maps):
    total = jnp.einsum("cw,iyxw->icyx", maps[0], grads[0], preferred_element_type=jnp.float32)
    total = total + jnp.einsum(
        "cw,iyxw->icyx", maps[1], grads[1], preferred_element_type=jnp.float32
    )
    return total + jnp.einsum(
        "cw,iyxw->icyx", maps[2], grads[2], preferred_element_type=jnp.float32
    )


def reduce_plan(
    attn_queries,
    attn_keys,
    attn_values,
    out_grad,
    fold_maps,
    dec_grad,
    conv_input,
    pre_act,
    proj_weight,
):
    split_at = HALF * HEAD_DIM
    width_cols = attn_queries.shape[2]
    rim_rows = padded_2(conv_input, (("seq", 1),), 1)
    column_parts = (
        lax.all_to_all(
            attn_queries[..., split_at:], "seq", split_axis=2, concat_axis=1, tiled=True
        ),
        lax.all_to_all(attn_keys[..., split_at:], "seq", split_axis=2, concat_axis=1, tiled=True),
        lax.all_to_all(attn_values[..., split_at:], "seq", split_axis=2, concat_axis=1, tiled=True),
        lax.all_to_all(out_grad[..., split_at:], "seq", split_axis=2, concat_axis=1, tiled=True),
    )

    def row_heads(array_in):
        return array_in[0, :, :, :split_at].reshape(array_in.shape[1], width_cols, HALF, HEAD_DIM)

    row_grads = attend_back(
        row_heads(attn_queries), row_heads(attn_keys), row_heads(attn_values), row_heads(out_grad)
    )
    row_grads = [grad_one.reshape(1, 1, width_cols, split_at) for grad_one in row_grads]
    grid_rows = column_parts[0].shape[1]
    col_count = column_parts[0].shape[2]

    def col_heads(array_in):
        return jnp.transpose(array_in[0], (1, 0, 2)).reshape(col_count, grid_rows, HALF, HEAD_DIM)

    col_grads = attend_back(
        col_heads(column_parts[0]),
        col_heads(column_parts[1]),
        col_heads(column_parts[2]),
        col_heads(column_parts[3]),
    )
    col_grads = [
        jnp.transpose(grad_one.reshape(col_count, grid_rows, split_at), (1, 0, 2))[None]
        for grad_one in col_grads
    ]
    latent_col = fold_sum(col_grads, fold_maps[:, :, split_at:])
    latent_rows = lax.all_to_all(latent_col, "seq", split_axis=2, concat_axis=3, tiled=True)
    latent = fold_sum(row_grads, fold_maps[:, :, :split_at]) + latent_rows
    halves, shifts, bins_arr = bound_tables()
    pre_wide = pre_act.astype(jnp.float32)
    sigmoid_v = jax.nn.sigmoid(pre_wide)
    act_low = (pre_wide * sigmoid_v).astype(jnp.bfloat16)
    latent_pre = jnp.einsum(
        "iyxj,cj->icyx", act_low, proj_weight, preferred_element_type=jnp.float32
    )
    tanh_val = jnp.tanh(latent_pre + shifts[None, :, None, None])
    slope_fsq = (halves / bins_arr)[None, :, None, None] * (1.0 - tanh_val * tanh_val)
    latent_grad = ((latent + dec_grad) * slope_fsq).astype(jnp.bfloat16)
    proj_term = jnp.einsum(
        "icyx,iyxj->jc", latent_grad, act_low, preferred_element_type=jnp.float32
    )
    act_grad = jnp.einsum(
        "icyx,cj->iyxj", latent_grad, proj_weight, preferred_element_type=jnp.float32
    )
    pre_grad = (act_grad * sigmoid_v * (1.0 + pre_wide * (1.0 - sigmoid_v))).astype(jnp.bfloat16)
    padded = jnp.pad(rim_rows, ((0, 0), (0, 0), (1, 1), (0, 0)))
    windows = jnp.stack(
        [
            padded[0, row_off, col_off : col_off + width_cols]
            for row_off in range(3)
            for col_off in range(3)
        ]
    )
    conv_term = jnp.einsum(
        "kpa,pb->akb", windows, pre_grad[0, 0], preferred_element_type=jnp.float32
    )
    shares = (
        lax.psum_scatter(conv_term, "seq", scatter_dimension=0, tiled=True),
        lax.psum_scatter(proj_term, "seq", scatter_dimension=0, tiled=True),
    )
    conv_out, proj_out = lax.psum((shares[0], shares[1]), "dp")
    return (conv_out, proj_out)


LANES = 128
FLOAT = jnp.float32
HALFWORD = jnp.bfloat16


def dot(lhs, rhs, lhs_dim=1, rhs_dim=0, precision=None):
    return lax.dot_general(
        lhs,
        rhs,
        (((lhs_dim,), (rhs_dim,)), ((), ())),
        precision=precision,
        preferred_element_type=FLOAT,
    )


def iota(shape, axis):
    return lax.broadcasted_iota(jnp.int32, shape, axis)


def attend_tile(queries, keys_in, values_in, grads_in, allowed):
    scaling = 1.0 / math.sqrt(queries.shape[-1])
    scores = jnp.where(allowed, dot(queries, keys_in, 1, 1) * scaling, -jnp.inf)
    exp_scores = jnp.exp(scores - jnp.max(scores, axis=-1, keepdims=True))
    attn_probs = exp_scores / jnp.sum(exp_scores, axis=-1, keepdims=True)
    dprobs = dot(grads_in, values_in, 1, 1)
    rowdot = jnp.sum(attn_probs * dprobs, axis=-1, keepdims=True)
    dscore = (attn_probs * (dprobs - rowdot) * scaling).astype(HALFWORD)
    return (
        dot(dscore, keys_in).astype(HALFWORD),
        dot(dscore, queries, 0, 0).astype(HALFWORD),
        dot(attn_probs.astype(HALFWORD), grads_in, 0, 0).astype(HALFWORD),
    )


def div(value, count):
    if count & (count - 1) == 0:
        return lax.shift_right_logical(value, count.bit_length() - 1)
    return lax.div(value, count)


def rem(value, count):
    if count & (count - 1) == 0:
        return value & (count - 1)
    return lax.rem(value, count)


def lane_places(rows, lanes, start, latents, width):
    lane = iota((rows, lanes), 1)
    inside = lane >= start
    offset = rem(jnp.maximum(lane - start, 0), latents * width)
    return inside, div(offset, width), rem(offset, width)


def local_kernel(
    order,
    query_hbm,
    key_hbm,
    value_hbm,
    grad_hbm,
    fold_hbm,
    dec_hbm,
    conv_hbm,
    pre_hbm,
    proj_hbm,
    packed_ref,
    row_ref,
    slope_ref,
    fold_own_ref,
    conv_out_ref,
    proj_rep_ref,
    pre_out_ref,
    rows_ref,
    fold_ref,
    dec_ref,
    conv_ref,
    pre_ref,
    proj_ref,
    sem,
    rest_sem,
    pack_sem,
):
    split_at = HALF * HEAD_DIM
    heads = (query_hbm, key_hbm, value_hbm, grad_hbm)
    copies = [
        pltpu.make_async_copy(ref.at[0, 0, :, pl.ds(0, split_at)], rows_ref.at[part], sem)
        for part, ref in enumerate(heads)
    ]
    copies += [
        pltpu.make_async_copy(source, target, rest_sem)
        for source, target in (
            (fold_hbm, fold_ref),
            (dec_hbm, dec_ref),
            (conv_hbm, conv_ref),
            (pre_hbm, pre_ref),
            (proj_hbm, proj_ref),
        )
    ]
    packs = []
    for slot, device in enumerate(order):
        lanes = pl.ds((HALF + device) * HEAD_DIM, HEAD_DIM)
        for part, ref in enumerate(heads):
            packs.append(
                pltpu.make_async_copy(ref.at[0, 0, :, lanes], packed_ref.at[slot, part], pack_sem)
            )
    for copy in copies + packs:
        copy.start()
    for copy in copies[: len(heads)]:
        copy.wait()
    width = query_hbm.shape[2]
    latents = fold_ref.shape[1]
    devices, _, lanes = conv_out_ref.shape
    span = conv_ref.shape[3] // devices
    mine = lax.axis_index("seq")

    def stacked(part):
        return jnp.concatenate(
            [
                rows_ref[part, :, head * HEAD_DIM : (head + 1) * HEAD_DIM].astype(FLOAT)
                for head in range(HALF)
            ],
            axis=0,
        ).astype(HALFWORD)

    count = HALF * width
    row, col = iota((count, count), 0), iota((count, count), 1)
    allowed = (div(row, width) == div(col, width)) & (col <= row)
    grads = attend_tile(
        stacked(0), stacked(1), stacked(2), stacked(3), allowed
    )
    for copy in copies[len(heads) :]:
        copy.wait()
    inside, channel, place = lane_places(width, lanes, span, latents, width)
    lane = iota((lanes, latents), 0)
    spread_at = rem(jnp.maximum(lane - span, 0), latents * width)
    hit = (lane >= span) & (div(spread_at, width) == iota((lanes, latents), 1))
    spread = jnp.where(hit, 1.0, 0.0).astype(HALFWORD)
    once = jnp.where(hit & (lane < span + latents * width), 1.0, 0.0).astype(HALFWORD)
    compact = jnp.zeros((width, latents), FLOAT)
    for part in range(3):
        wide = grads[part].astype(FLOAT)
        wide = jnp.concatenate(
            [wide[head * width : (head + 1) * width] for head in range(HALF)], axis=1
        ).astype(HALFWORD)
        compact = compact + dot(wide, fold_ref[part, :, :split_at], 1, 1)
        own = fold_ref[part, :, pl.ds(pl.multiple_of(split_at + mine * HEAD_DIM, HEAD_DIM), HEAD_DIM)]
        fold_own_ref[part] = dot(spread, own).astype(HALFWORD)
    diagonal = inside & (iota((width, lanes), 0) == place)

    def spread_out(values):
        result = jnp.zeros((width, lanes), FLOAT)
        for index in range(latents):
            result = jnp.where(diagonal & (channel == index), values[:, index : index + 1], result)
        return result

    total = spread_out(compact)
    decoder = dec_ref[0, :, 0, :]
    column = rem(iota((latents, lanes), 1), width)
    tiled = jnp.zeros((latents, lanes), FLOAT)
    for index in range(width):
        tiled = jnp.where(column == index, decoder[:, index : index + 1], tiled)
    decoder = tiled
    _, owner, _ = lane_places(latents, lanes, span, latents, width)
    keep = (iota((latents, lanes), 1) >= span) & (iota((latents, lanes), 0) == owner)
    vector = jnp.sum(total, axis=0, keepdims=True) + jnp.sum(
        jnp.where(keep, decoder, 0.0), axis=0, keepdims=True
    )
    row_ref[...] = jnp.where(iota((width, lanes), 0) == mine, vector, 0.0)
    proj_rep_ref[...] = dot(once, proj_ref[...]).astype(HALFWORD)
    pre_out_ref[...] = pre_ref[...]
    pre_wide = pre_ref[0, 0].astype(FLOAT)
    act_low = (pre_wide * jax.nn.sigmoid(pre_wide)).astype(HALFWORD)
    latent_pre = spread_out(dot(act_low, proj_ref[...], 1, 1))
    halves = [(levels_one - 1.0) * 1.001 / 2.0 for levels_one in fsq_levels]
    shift = jnp.zeros((width, lanes), FLOAT)
    slope = jnp.zeros((width, lanes), FLOAT)
    for index, (levels_one, bins_one, half_width) in enumerate(zip(fsq_levels, fsq_bins, halves)):
        ratio_one = (0.5 if levels_one % 2.0 == 0.0 else 0.0) / half_width
        shift_one = 0.5 * math.log((1.0 + ratio_one) / (1.0 - ratio_one))
        shift = jnp.where(channel == index, shift_one, shift)
        slope = jnp.where(channel == index, half_width / bins_one, slope)
    tanh_val = jnp.tanh(latent_pre + shift)
    slope = slope * (1.0 - tanh_val * tanh_val)
    slope = jnp.where(diagonal, slope, 0.0)
    vector = jnp.sum(slope, axis=0, keepdims=True)
    slope_ref[...] = jnp.where(iota((width, lanes), 0) == mine, vector, 0.0)
    for device in range(devices):
        first = device * span
        block = conv_ref[0, 0, :, first // lanes * lanes : first // lanes * lanes + lanes].astype(FLOAT)
        if first % lanes:
            block = pltpu.roll(block, lanes - first % lanes, 1)
        conv_out_ref[device] = block
    for copy in packs:
        copy.wait()


def column_kernel(
    seq_order, chip_order, recv_ref, fold_ref, row_ref, slope_ref, conv_ref, pre_ref, out_ref
):
    rows, _, width, _ = recv_ref.shape
    devices, _, lanes = conv_ref.shape
    channels = pre_ref.shape[3]
    span = channels // devices
    half = (lanes - span) // 2
    count = rows * width

    def stacked(part):
        tiles = [recv_ref[seq_order.index(source), part].astype(FLOAT) for source in range(rows)]
        return jnp.concatenate(tiles, axis=0).astype(HALFWORD)

    row, col = iota((count, count), 0), iota((count, count), 1)
    allowed = (rem(row, width) == rem(col, width)) & (col <= row)
    grads = attend_tile(stacked(0), stacked(1), stacked(2), stacked(3), allowed)
    total = dot(grads[0], fold_ref[0], 1, 1)
    total = total + dot(grads[1], fold_ref[1], 1, 1)
    total = total + dot(grads[2], fold_ref[2], 1, 1)
    match = iota((width, lanes), 0) == rem(iota((width, lanes), 1), width)
    total = jnp.where(match[None], total.reshape(rows, width, lanes), 0.0)
    share = jnp.sum(total, axis=1) + row_ref[...]
    lane = iota((rows, lanes), 1)

    def pair(value):
        high = value.astype(HALFWORD).astype(FLOAT)
        return jnp.where(lane < span + half, high, value - high)

    parts = (pair(share), pair(slope_ref[...]))
    pre = pre_ref[0, 0]
    chips = devices // 2
    for chip in range(chips):
        blocks = [
            jnp.where(lane < span, conv_ref[2 * chip + core], parts[core]).astype(HALFWORD)
            for core in range(2)
        ]
        for slot, member in enumerate(chip_order):
            if member % chips == chip:
                out_ref[slot, :, :channels] = pre
                out_ref[slot, :, channels : channels + lanes] = blocks[0]
                out_ref[slot, :, channels + lanes :] = blocks[1]


def final_kernel(
    chip_order, own_ref, other_ref, proj_rep_ref, conv_out_ref, proj_out_ref, stage, held, small, sem
):
    members, width, _ = own_ref.shape
    taps, span, channels = conv_out_ref.shape
    latents = proj_out_ref.shape[0]
    lanes = proj_rep_ref.shape[0]
    devices = channels // span
    chips = devices // 2
    sources = 2 * members
    images = sources // devices
    count = sources * width
    mine = lax.axis_index("seq")
    half = latents * width
    lane = iota((width, lanes), 1)
    match = (lane >= span) & (lane < span + half) & (iota((width, lanes), 0) == rem(lane, width))

    def finish(core):
        def rows(first, size):
            tiles = []
            for source in range(sources):
                image, place = divmod(source, devices)
                ref = own_ref if place % 2 == core else other_ref
                slot = chip_order.index(image * chips + place // 2)
                tiles.append(ref[slot, :, first : first + size].astype(FLOAT))
            return jnp.stack(tiles, axis=0)

        tails = [rows(channels, lanes), rows(channels + lanes, lanes)]
        pick = jnp.where(iota((span, lanes), 0) == iota((span, lanes), 1), 1.0, 0.0)
        inputs = dot(
            pick.astype(HALFWORD), tails[core].reshape(count, lanes).astype(HALFWORD), 1, 1
        )
        position = iota((8, count), 1)
        place_x = rem(position, width)
        place_y = rem(div(position, width), devices)
        for row_off in (-1, 0, 1):
            for col_off in (-1, 0, 1):
                step = row_off * width + col_off
                window = pltpu.roll(inputs, -step % count, 1) if step else inputs
                valid = (
                    (place_x + col_off >= 0)
                    & (place_x + col_off < width)
                    & (place_y + row_off >= 0)
                    & (place_y + row_off < devices)
                )
                window = jnp.where(valid[None], window.reshape(span // 8, 8, count), 0.0)
                tap = 3 * row_off + col_off + 4
                stage[pl.ds(tap * span, span), :] = window.reshape(span, count).astype(HALFWORD)
        proj_rep = proj_rep_ref[...]
        latent, slope = [
            jnp.sum(tail.reshape(images, devices, width, lanes), axis=1).reshape(sources, lanes)
            for tail in tails
        ]
        latent = latent + pltpu.roll(latent, lanes - half, 1)
        slope = slope + pltpu.roll(slope, lanes - half, 1)
        latent_grad = (latent * slope).reshape(sources, 1, lanes)
        wide = jnp.broadcast_to(latent_grad, (sources, width, lanes))
        wide = jnp.where(match[None], wide, 0.0).reshape(count, lanes).astype(HALFWORD)
        act_grad = dot(wide, proj_rep)
        pre_wide = rows(0, channels).reshape(count, channels)
        sigmoid_v = 0.5 + 0.5 * jnp.tanh(0.5 * pre_wide)
        act_wide = pre_wide * sigmoid_v
        act_low = act_wide.astype(HALFWORD)
        silu_grad = sigmoid_v + act_wide * (1.0 - sigmoid_v)
        pre_grad = (act_grad * silu_grad).astype(HALFWORD)
        copies = []
        for part in range(3):
            block = pl.ds(3 * part, 3)
            windows = stage[3 * part * span : 3 * (part + 1) * span, :]
            held[block] = dot(windows, pre_grad).reshape(3, span, channels)
            copies.append(
                pltpu.make_async_copy(held.at[block], conv_out_ref.at[block], sem.at[part])
            )
            copies[-1].start()
        proj_term = dot(wide, act_low, 0, 0)[span : span + half]
        proj_term = jnp.sum(proj_term.reshape(latents, width, channels), axis=1)
        turn = rem(channels - mine * span, channels)
        small[...] = pltpu.roll(proj_term, turn, 1)[:, :span]
        copies.append(pltpu.make_async_copy(small, proj_out_ref, sem.at[3]))
        copies[-1].start()
        for copy in copies:
            copy.wait()

    for core in range(2):
        pl.when(rem(mine, 2) == core)(functools.partial(finish, core))


def call(kernel, outs, inputs, in_specs=None, flops=1 << 22):
    whole = pl.BlockSpec(memory_space=pltpu.VMEM)
    nbytes = sum(math.prod(one.shape) * one.dtype.itemsize for one in (*inputs, *outs))
    return pl.pallas_call(
        kernel,
        grid=(1,),
        out_shape=outs,
        in_specs=in_specs or [whole] * len(inputs),
        out_specs=[whole] * len(outs),
        compiler_params=pltpu.CompilerParams(vmem_limit_bytes=16 << 20),
        cost_estimate=pl.CostEstimate(flops=flops, bytes_accessed=nbytes, transcendentals=0),
    )(*inputs)


def gather_plan(
    attn_queries,
    attn_keys,
    attn_values,
    out_grad,
    fold_maps,
    dec_grad,
    conv_input,
    pre_act,
    proj_weight,
):
    devices, images = lax.axis_size("seq"), lax.axis_size("dp")
    width, channels, latents = pre_act.shape[2], pre_act.shape[3], proj_weight.shape[0]
    span = channels // devices
    split_at = HALF * HEAD_DIM
    heads = (attn_queries, attn_keys, attn_values, out_grad)
    struct = jax.ShapeDtypeStruct
    members = images * devices
    chips = devices // 2
    seq_order = [(devices // 2 + 1 - slot) % devices for slot in range(devices)]
    chip_order = [(members // 2 - 1 - 3 * slot) % (members // 2) for slot in range(members // 2)]
    core_groups = [
        [member // chips * devices + member % chips * 2 + core for member in chip_order]
        for core in range(2)
    ]
    columns = [pl.BlockSpec((1, 1, width, split_at), lambda step: (0, 0, 0, 1))] * 4
    whole = pl.BlockSpec(memory_space=pltpu.VMEM)
    inputs = (*heads, fold_maps, dec_grad, conv_input, pre_act, proj_weight)
    packed, row_share, slopes, fold_own, conv_blocks, proj_rep, pre_near = pl.pallas_call(
        functools.partial(local_kernel, seq_order),
        out_shape=[
            struct((devices, 4, width, HEAD_DIM), HALFWORD),
            struct((width, LANES), FLOAT),
            struct((width, LANES), FLOAT),
            struct((3, LANES, HEAD_DIM), HALFWORD),
            struct((devices, width, LANES), FLOAT),
            struct((LANES, channels), HALFWORD),
            struct(pre_act.shape, HALFWORD),
        ],
        in_specs=[pl.BlockSpec(memory_space=pltpu.HBM)] * len(inputs),
        out_specs=[whole] * 7,
        scratch_shapes=[pltpu.VMEM((4, width, split_at), HALFWORD)]
        + [pltpu.VMEM(one.shape, one.dtype) for one in inputs[4:]]
        + [pltpu.SemaphoreType.DMA] * 3,
        compiler_params=pltpu.CompilerParams(vmem_limit_bytes=16 << 20),
    )(*[pltpu.with_memory_space_constraint(one, pltpu.HBM) for one in inputs])
    column = lax.all_to_all(packed, "seq", split_axis=0, concat_axis=0, axis_index_groups=[seq_order], tiled=True)
    (shared,) = call(
        functools.partial(column_kernel, seq_order, chip_order),
        [struct((members // 2, width, channels + 2 * LANES), HALFWORD)],
        (column, fold_own, row_share, slopes, conv_blocks, pre_near),
    )
    spread = lax.all_to_all(
        shared,
        ("dp", "seq"),
        split_axis=0,
        concat_axis=0,
        axis_index_groups=core_groups,
        tiled=True,
    )
    partner = lax.ppermute(spread, "seq", [(one, one ^ 1) for one in range(devices)])
    outs = [struct((9, span, channels), FLOAT), struct((latents, span), FLOAT)]
    conv_out, proj_out = pl.pallas_call(
        functools.partial(final_kernel, chip_order),
        out_shape=outs,
        in_specs=[whole] * 3,
        out_specs=[pl.BlockSpec(memory_space=pltpu.HBM)] * 2,
        scratch_shapes=[pltpu.VMEM((9 * span, images * devices * width), HALFWORD)]
        + [pltpu.VMEM(one.shape, one.dtype) for one in outs]
        + [pltpu.SemaphoreType.DMA((4,))],
        compiler_params=pltpu.CompilerParams(vmem_limit_bytes=16 << 20),
    )(spread, partner, proj_rep)
    return (jnp.transpose(conv_out, (1, 0, 2)), jnp.transpose(proj_out, (1, 0)))


def on_device(*arrays):
    queries, conv_input, proj_weight = arrays[0], arrays[6], arrays[8]
    devices, images = lax.axis_size("seq"), lax.axis_size("dp")
    rows, width, channels = conv_input.shape[1:]
    latents = proj_weight.shape[0]
    heads = queries.shape[3] // HEAD_DIM - HALF
    positions = images * devices * rows * width
    fits = (
        (conv_input.shape[0], rows, width, heads) == (1, 1, devices, devices)
        and channels // devices % 8 == 0
        and (HALF * 2, width, images * devices % 8) == (queries.shape[3] // HEAD_DIM, 8, 0)
        and devices % 2 == 0
        and math.gcd(3, images * devices // 2) == 1
        and channels // devices + 2 * latents * width == LANES
    )
    if fits and positions * channels * 2 <= 9 * channels * channels * 4:
        return gather_plan(*arrays)
    return reduce_plan(*arrays)


def solution(mesh):
    return jax.shard_map(
        on_device,
        mesh=mesh,
        in_specs=(
            P("dp", "seq", None, None),
            P("dp", "seq", None, None),
            P("dp", "seq", None, None),
            P("dp", "seq", None, None),
            P(),
            P("dp", None, "seq", None),
            P("dp", "seq", None, None),
            P("dp", "seq", None, None),
            P(),
        ),
        out_specs=(P("seq", None, None), P("seq", None)),
        check_vma=False,
    )
```
